32 devices in a mesh: seg: 8 (over z, x), space: 4 (over y, core).
Axes of the slice: x: 2, y: 2, z: 4, core: 2. Of those that a mesh axis runs over, the one named last changes fastest.
Arguments:
- states: float32 [8, 32, 65, 128], P('seg', 'space'), may hold values from -6 to 6
- forcing: float32 [32, 65, 128], P('space'), may hold values from -6 to 6
- wall_viscosity: float32 [65], replicated, may hold values from 0.5 to 4
Outputs:
- new_states: float32 [8, 32, 65, 128], P('seg', 'space')
- mismatch: float32 [8, 32, 65, 128], P('seg', 'space')
The draws below stay inside these ranges and needn't reach their ends.
All inputs are finite; a program needn't handle non-finite values.
Results may differ from the reference program's by a relative error of at most 0.0075.
Values sent between devices are 32-bit elements; how exact they have to be, the bound alone decides.
No kernel may reach another device: no remote copies, remote signals or barrier semaphores. Data moves between devices by JAX's collectives and lax.ppermute only.
A program may use at most 64 MiB of HBM per device.

```python
import math
import jax
import jax.numpy as jnp
from jax import lax

NY = 65
NZ = 128
STEPS = 4
ITERS = 2
NX = 32
NSEG = 8


def draw_states(key, part):
    first, second = jax.random.split(key, 2)
    ramp = (jnp.arange(NSEG, dtype=jnp.float32) / (NSEG - 1)).reshape(NSEG, 1, 1, 1)
    rough = jax.random.truncated_normal(first, -4.0, 4.0, (NSEG, NX, NY, NZ), jnp.float32)
    jitter = jax.random.uniform(second, (NSEG, 1, 1, 1), jnp.float32, 0.9, 1.07)
    scales = jnp.exp(math.log(0.4) + ramp * (math.log(1.4) - math.log(0.4))) * jitter
    return scales * rough


def steps_of(own_key, dims, pieces, low, top_value):
    def one(dim, parts):
        steps = jax.random.uniform(jax.random.fold_in(jax.random.fold_in(own_key, 6), dim), (parts,), jnp.float32, low / len(pieces), top_value / len(pieces))
        return jnp.repeat(jnp.exp(steps), dims[dim] // parts).reshape((-1,) + (1,) * (len(dims) - dim - 1))

    level = one(*pieces[0])
    for cut in pieces[1:]:
        level = level * one(*cut)
    return level


def bell_draw(stream_key, shape, deviation, reach, cuts=(), kind=jnp.bfloat16):
    loudness = steps_of(stream_key, shape, cuts, -0.22, 0.18) if cuts else 1.0
    array = jax.random.normal(stream_key, shape, jnp.float32) * deviation * loudness
    return jnp.minimum(jnp.maximum(array, -reach), reach).astype(kind)


def setup_inputs(seed: int = 0) -> dict:
    streams_of = jax.random.split(jax.random.key(seed), 4)
    states = draw_states(jax.random.fold_in(streams_of[3], 71), 0)
    forcing = bell_draw(streams_of[1], (NX, NY, NZ), 1.0, 6.0, ((0, 4),), jnp.float32)
    wall_viscosity = jnp.clip(jnp.exp(jax.random.uniform(streams_of[2], (NY,), jnp.float32, math.log(0.5), math.log(4.0))), 0.5, 4.0)
    return dict(states=states, forcing=forcing, wall_viscosity=wall_viscosity)


ADVECT = 0.15
SPREAD = 0.2
PUSHED = 0.25
EPSILON = 1e-06

def inverses(viscosity):
    points = viscosity.shape[0]
    zero = jnp.zeros((1,), jnp.float32)
    negative = -viscosity
    centre = 1.0 + 2.0 * viscosity
    lower = jnp.concatenate([zero, negative[1:]])
    upper = jnp.concatenate([negative[:-1], zero])
    identity = jnp.eye(points, dtype=jnp.float32)
    return lax.linalg.tridiagonal_solve(lower[None], centre[None], upper[None], identity[None])[0]

def apply_inverse(inverse, field):
    return jnp.einsum('jk,xkz->xjz', inverse, field, precision=lax.Precision.HIGHEST)

def apply_transposed(inverse, field):
    return jnp.einsum('kj,xkz->xjz', inverse, field, precision=lax.Precision.HIGHEST)

def spanwise(field):
    return jnp.roll(field, 1, 2) + jnp.roll(field, -1, 2) - 2.0 * field

def periodic(field):
    return jnp.concatenate([field[-1:], field, field[:1]], axis=0)

def forward_step(field, forcing, base, inverse):
    padded = periodic(field)
    slope = 0.5 * (padded[2:] - padded[:-2])
    pushed = field - ADVECT * (base + field) * slope + SPREAD * spanwise(field) + PUSHED * forcing
    return (apply_inverse(inverse, pushed), slope)

def adjoint_step(weight, field, slope, base, inverse):
    carried = apply_transposed(inverse, weight)
    flux = (base + field) * carried
    padded = periodic(flux)
    return carried - ADVECT * carried * slope + ADVECT * (0.5 * (padded[2:] - padded[:-2])) + SPREAD * spanwise(carried)

def reference(states, forcing, wall_viscosity):
    base = (2.0 * jnp.arange(NY, dtype=jnp.float32) / (NY - 1) - 1.0)[None, :, None]
    inverse = inverses(wall_viscosity)

    def integrate(field):
        for step in range(STEPS):
            field, slope = forward_step(field, forcing, base, inverse)
        return field

    def gradient_part(pair):
        field, weight = pair
        saved = []
        for step in range(STEPS):
            following, slope = forward_step(field, forcing, base, inverse)
            saved.append((field, slope))
            field = following
        for step in reversed(range(STEPS)):
            weight = adjoint_step(weight, saved[step][0], saved[step][1], base, inverse)
        return weight
    current = states
    mismatch = states
    for iteration in range(ITERS):
        ends = lax.map(integrate, current)
        mismatch = ends - jnp.roll(current, -1, axis=0)
        back = lax.map(gradient_part, (current, mismatch))
        descent = back - jnp.roll(mismatch, 1, axis=0)
        total = 0.5 * jnp.sum(mismatch * mismatch)
        squares = jnp.sum(descent * descent)
        current = current - total / (squares + EPSILON) * descent
    return (current, mismatch)
```

```python
import functools

import jax
import jax.numpy as jnp
from jax import lax
from jax.experimental import pallas as pl
from jax.experimental.pallas import tpu as pltpu
from jax.sharding import PartitionSpec as P

STEPS = 4
ITERS = 2
ADVECT = 0.15
SPREAD = 0.2
PUSHED = 0.25
EPSILON = 1e-06
BOTH = ("seg", "space")
VMEM = pl.BlockSpec(memory_space=pltpu.VMEM)
LANES = 128


def padded(count, step):
    return -(-count // step) * step


def call(kernel, name, outs, operands, scratch=()):
    return pl.pallas_call(
        kernel,
        name=name,
        out_shape=[jax.ShapeDtypeStruct(shape, dtype) for shape, dtype in outs],
        in_specs=[VMEM] * len(operands),
        out_specs=[VMEM] * len(outs),
        scratch_shapes=list(scratch),
        compiler_params=pltpu.CompilerParams(vmem_limit_bytes=48 * 1024 * 1024),
    )(*operands)


def inverse_kernel(points, rows, k_ref, forward_ref, backward_ref, square):
    row = lax.broadcasted_iota(jnp.int32, (LANES, LANES), 0)
    lane = lax.broadcasted_iota(jnp.int32, (LANES, LANES), 1)
    k = k_ref[...]
    zero = jnp.zeros_like(k)
    a = jnp.where((row >= 1) & (row < points), -k, zero)
    c = jnp.where(row < points - 1, -k, zero)
    b = jnp.where(row < points, 1.0 + 2.0 * k, 1.0)
    d = jnp.where((row == lane) & (row < points), 1.0, 0.0)
    step = 1
    while step < points:
        up = lambda v: pltpu.roll(v, step, 0)
        down = lambda v: pltpu.roll(v, LANES - step, 0)
        alpha = -a / up(b)
        gamma = -c / down(b)
        b = b + alpha * up(c) + gamma * down(a)
        d = d + alpha * up(d) + gamma * down(d)
        a, c = alpha * up(a), gamma * down(c)
        step *= 2
    inverse = d / b
    square[...] = inverse
    stride = padded(points, 16)
    for ref, matrix in ((forward_ref, SPREAD * inverse), (backward_ref, square[...].T)):
        head = matrix.astype(jnp.bfloat16).astype(jnp.float32)
        tail = (matrix - head).astype(jnp.bfloat16).astype(jnp.float32)
        tail = pltpu.roll(tail, stride, 1)
        left = jnp.where(lane >= stride, tail, head)
        right = jnp.where(lane < stride + points - LANES, tail, pltpu.roll(head, 2 * stride - LANES, 1))
        ref[:, :LANES] = left[:rows].astype(jnp.bfloat16)
        ref[:, LANES:] = right[: rows, : 3 * stride - LANES].astype(jnp.bfloat16)


def product(matrix, planes):
    columns = []
    for plane in planes:
        rows = plane.shape[0]
        fill = jnp.zeros((padded(rows, 16) - rows, LANES), jnp.float32)
        plane = jnp.concatenate([plane, fill], 0) if fill.shape[0] else plane
        head = plane.astype(jnp.bfloat16)
        tail = (plane - head.astype(jnp.float32)).astype(jnp.bfloat16)
        columns.append(jnp.concatenate([head, head, tail], 0))
    right = jnp.concatenate(columns, 1) if len(columns) > 1 else columns[0]
    out = jnp.dot(matrix, right, preferred_element_type=jnp.float32)
    return [out[:, i * LANES : (i + 1) * LANES] for i in range(len(planes))]


def neighbours(plane):
    return pltpu.roll(plane, 1, 1) + pltpu.roll(plane, LANES - 1, 1)


def step_size(sums):
    total = jnp.sum(sums, axis=0, keepdims=True)
    lane = lax.broadcasted_iota(jnp.int32, total.shape, 1)
    squares = jnp.sum(jnp.where(lane < LANES // 2, 0.0, total), axis=1, keepdims=True)
    residual = jnp.sum(jnp.where(lane < LANES // 2, total, 0.0), axis=1, keepdims=True)
    return 0.5 * residual / (squares + EPSILON)


def forward_kernel(nx, points, rows, updated, *refs):
    refs = list(refs)
    matrix_ref, cur, left, right, after, force, force_left, force_right = refs[:8]
    del refs[:8]
    if updated:
        d_cur, d_left, d_right, d_after, sums = refs[:5]
        del refs[:5]
        tau = step_size(sums[...])
    ending_ref, mismatch_ref, first_ref, second_ref, third_ref, low_ref, high_ref, squares_ref, edges_ref = refs[:9]
    start_ref = refs[9] if updated else None
    u0, q = refs[-2:]
    pad = rows - points
    h = STEPS

    def place(target, index, source, i, moved):
        value = source[i]
        if moved is not None:
            value = value - tau * moved[i][:points]
        target[index, :points] = value
        return value

    tail = jnp.zeros((pad, LANES), jnp.float32)
    for i in range(nx + 2 * h):
        u0[i, points:] = tail
    for i in range(nx + 2 * h - 2):
        q[i, points:] = tail
    d = (d_cur, d_left, d_right, d_after) if updated else (None,) * 4
    for i in range(h):
        place(u0, i, left, i, d[1])
        place(u0, h + nx + i, right, i, d[2])
    for i in range(nx):
        place(u0, h + i, cur, i, d[0])
    scale = PUSHED / SPREAD
    for i in range(h - 1):
        q[i, :points] = scale * force_left[i]
        q[h - 1 + nx + i, :points] = scale * force_right[i]
    for i in range(nx):
        q[h - 1 + i, :points] = scale * force[i]
    row = lax.broadcasted_iota(jnp.int32, (rows, LANES), 0).astype(jnp.float32)
    base = row * (2.0 / (points - 1)) - 1.0
    matrix = matrix_ref[...]
    fields = [u0, first_ref, second_ref, third_ref, None]
    for t in range(h):
        source, target = fields[t], fields[t + 1]
        count = nx + 2 * (h - t - 1)
        window = [source[0], source[1]]
        pending = []
        for i in range(count):
            window = window[-2:] + [source[i + 2]]
            before, here, ahead = window
            pushed = 3.0 * here + neighbours(here) + q[i + t] - (base + here) * (ahead - before) * (0.5 * ADVECT / SPREAD)
            pending.append(pushed)
            if len(pending) == 2 or i == count - 1:
                for j, plane in enumerate(product(matrix, pending)):
                    at = i - len(pending) + 1 + j
                    if target is not None:
                        target[at] = plane
                    else:
                        ending_ref[at] = plane
                pending = []
    total = jnp.zeros((rows, LANES), jnp.float32)
    for i in range(nx):
        value = after[i]
        if updated:
            value = value - tau * d_after[i][:points]
        value = ending_ref[i][:points] - value
        mismatch_ref[i] = value
        value = jnp.concatenate([value, tail], 0)
        if i < h:
            low_ref[i] = value
        if i >= nx - h:
            high_ref[i - (nx - h)] = value
        total = total + value * value
    folded = total[:8]
    for r in range(8, rows, 8):
        folded = folded + total[r : r + 8]
    squares_ref[...] = folded
    for i in range(h - 1):
        low_ref[h + i] = third_ref[1 + 1 + i]
        high_ref[h + i] = third_ref[1 + nx - h + i]
    low_ref[2 * h - 1] = second_ref[2 + 2]
    high_ref[2 * h - 1] = second_ref[2 + nx - 3]
    if updated:
        for i in range(nx):
            start_ref[i] = u0[h + i, :points]
    edges_ref[0] = u0[h - 1]
    edges_ref[1] = u0[h + nx]


def adjoint_kernel(nx, points, rows, matrix_ref, cur, edges, first, second, third, mismatch, from_left, from_right, lam_ref, a, b):
    h = STEPS
    row = lax.broadcasted_iota(jnp.int32, (rows, LANES), 0).astype(jnp.float32)
    base = row * (2.0 / (points - 1)) - 1.0
    matrix = matrix_ref[...]
    tail = jnp.zeros((rows - points, LANES), jnp.float32)

    def field(t, i):
        if t == 0:
            if i == -1:
                return edges[0]
            if i == nx:
                return edges[1]
            return jnp.concatenate([cur[i], tail], 0)
        if t == 1:
            return first[i + 3]
        if t == 2:
            if i == -3:
                return from_left[2 * h - 1]
            if i == nx + 2:
                return from_right[2 * h - 1]
            return second[i + 2]
        if i < -1:
            return from_left[h + i + 4]
        if i > nx:
            return from_right[h + i - nx - 1]
        return third[i + 1]

    def weight(i):
        if i < 0:
            return from_left[h + i]
        if i >= nx:
            return from_right[i - nx]
        return jnp.concatenate([mismatch[i], tail], 0)

    for t in reversed(range(h)):
        source, target = (a, b) if t % 2 == 0 else (b, a)
        window = []
        low, high = -(t + 1), nx + t + 1
        done = []
        for start in range(low, high, 2):
            group = list(range(start, min(start + 2, high)))
            lams = [weight(i) if t == h - 1 else source[i + h] for i in group]
            for i, mu in zip(group, product(matrix, lams)):
                u = field(t, i)
                window.append((u, mu, (base + u) * mu))
                window = window[-3:]
                if len(window) == 3:
                    (u0, _, f0), (_, m1, _), (u2, _, f2) = window
                    value = SPREAD * (3.0 * m1 + neighbours(m1)) + (0.5 * ADVECT) * ((f2 - f0) - m1 * (u2 - u0))
                    if t == 0:
                        lam_ref[i - 1] = value
                    else:
                        target[i - 1 + h] = value


def descent_kernel(nx, points, rows, devices, lam, prior, cur, squares, descent_ref, low_ref, high_ref, sums_ref):
    h = STEPS
    total = jnp.zeros((rows, LANES), jnp.float32)
    tail = jnp.zeros((rows - points, LANES), jnp.float32)
    for i in range(nx):
        value = lam[i][:points] - (prior[i][:points] - cur[i])
        value = jnp.concatenate([value, tail], 0)
        descent_ref[i] = value
        if i < h:
            low_ref[i] = value
        if i >= nx - h:
            high_ref[i - (nx - h)] = value
        total = total + value * value
    folded = total[:8]
    for r in range(8, rows, 8):
        folded = folded + total[r : r + 8]

    def fold(v):
        v = jnp.sum(v, axis=0, keepdims=True)
        return v + pltpu.roll(v, LANES // 2, 1)

    lane = lax.broadcasted_iota(jnp.int32, (1, LANES), 1)
    both = jnp.where(lane < LANES // 2, fold(squares[...]), fold(folded))
    sums_ref[...] = jnp.broadcast_to(both, (devices, LANES))


def final_kernel(nx, points, cur, descent, sums, out_ref):
    tau = step_size(sums[...])
    for i in range(nx):
        out_ref[i] = cur[i] - tau * descent[i][:points]


def shift(block, axis, distance):
    devices = lax.axis_size(axis)
    return lax.ppermute(block, axis, [((i - distance) % devices, i) for i in range(devices)])


def per_device(states, forcing, wall_viscosity):
    cur = states[0]
    nx, points, _ = cur.shape
    rows = padded(points, 8)
    depth = 3 * padded(points, 16)
    devices = lax.axis_size("seg") * lax.axis_size("space")
    h = STEPS
    f32, bf16 = jnp.float32, jnp.bfloat16
    left = shift(cur[nx - h :], "space", 1)
    right = shift(cur[:h], "space", -1)
    force_left = shift(forcing[nx - h + 1 :], "space", 1)
    force_right = shift(forcing[: h - 1], "space", -1)
    after = shift(cur, "seg", -1)
    k = jnp.broadcast_to(jnp.pad(wall_viscosity, (0, LANES - points))[:, None], (LANES, LANES))
    forward, backward = call(
        functools.partial(inverse_kernel, points, rows),
        "inverse",
        [((rows, depth), bf16)] * 2,
        [k],
        [pltpu.VMEM((LANES, LANES), f32)],
    )
    given = [cur, left, right, after, forcing, force_left, force_right]
    moved = []
    start = cur
    mismatch = None
    for iteration in range(ITERS):
        updated = iteration > 0
        outs = [
            ((nx, rows, LANES), f32),
            ((nx, points, LANES), f32),
            ((nx + 6, rows, LANES), f32),
            ((nx + 4, rows, LANES), f32),
            ((nx + 2, rows, LANES), f32),
            ((2 * h, rows, LANES), f32),
            ((2 * h, rows, LANES), f32),
            ((8, LANES), f32),
            ((2, rows, LANES), f32),
        ]
        if updated:
            outs.append(((nx, points, LANES), f32))
        ending, mismatch, first, second, third, low, high, squares, edges, *moved_start = call(
            functools.partial(forward_kernel, nx, points, rows, updated),
            "forward",
            outs,
            [forward] + given + moved,
            [pltpu.VMEM((nx + 2 * h, rows, LANES), f32), pltpu.VMEM((nx + 2 * h - 2, rows, LANES), f32)],
        )
        prior = shift(ending, "seg", 1)
        from_left = shift(high, "space", 1)
        from_right = shift(low, "space", -1)
        start = moved_start[0] if updated else cur
        lam = call(
            functools.partial(adjoint_kernel, nx, points, rows),
            "adjoint",
            [((nx, rows, LANES), f32)],
            [backward, start, edges, first, second, third, mismatch, from_left, from_right],
            [pltpu.VMEM((nx + 2 * h, rows, LANES), f32)] * 2,
        )[0]
        descent, d_low, d_high, sums = call(
            functools.partial(descent_kernel, nx, points, rows, devices),
            "descent",
            [((nx, rows, LANES), f32), ((h, rows, LANES), f32), ((h, rows, LANES), f32), ((devices, LANES), f32)],
            [lam, prior, start, squares],
        )
        if iteration < ITERS - 1:
            moved = [descent, shift(d_high, "space", 1), shift(d_low, "space", -1), shift(descent, "seg", -1)]
        sums = lax.all_to_all(sums, BOTH, 0, 0, tiled=True)
        moved = moved + [sums] if iteration < ITERS - 1 else moved
    new = call(
        functools.partial(final_kernel, nx, points),
        "final",
        [((nx, points, LANES), f32)],
        [start, descent, sums],
    )[0]
    return (new[None], mismatch[None])


def solution(mesh):
    placed = (P("seg", "space", None, None), P("space", None, None), P())
    return jax.shard_map(
        per_device,
        mesh=mesh,
        in_specs=placed,
        out_specs=(P("seg", "space", None, None), P("seg", "space", None, None)),
        check_vma=False,
    )
```

```python
import functools

import jax
import jax.numpy as jnp
from jax import lax
from jax.experimental import pallas as pl
from jax.experimental.pallas import tpu as pltpu
from jax.sharding import PartitionSpec as P

STEPS = 4
ITERS = 2
ADVECT = 0.15
SPREAD = 0.2
PUSHED = 0.25
EPSILON = 1e-06
BOTH = ("seg", "space")
VMEM = pl.BlockSpec(memory_space=pltpu.VMEM)
LANES = 128


def padded(count, step):
    return -(-count // step) * step


def load(ref, i, planes):
    points = ref.shape[0] // planes
    plane = ref[pl.ds(i, points, stride=planes), :]
    return jnp.concatenate([plane, jnp.zeros((padded(points, 8) - points, LANES), jnp.float32)], 0)


def store(ref, i, planes, plane):
    points = ref.shape[0] // planes
    ref[pl.ds(i, points, stride=planes), :] = plane[:points]


def call(kernel, name, outs, operands, scratch=()):
    return pl.pallas_call(
        kernel,
        name=name,
        out_shape=[jax.ShapeDtypeStruct(shape, dtype) for shape, dtype in outs],
        in_specs=[VMEM] * len(operands),
        out_specs=[VMEM] * len(outs),
        scratch_shapes=list(scratch),
        compiler_params=pltpu.CompilerParams(vmem_limit_bytes=32 * 1024 * 1024),
    )(*operands)


def inverse_kernel(points, rows, k_ref, forward_ref, backward_ref, square):
    row = lax.broadcasted_iota(jnp.int32, (LANES, LANES), 0)
    lane = lax.broadcasted_iota(jnp.int32, (LANES, LANES), 1)
    k = k_ref[...]
    zero = jnp.zeros_like(k)
    a = jnp.where((row >= 1) & (row < points), -k, zero)
    c = jnp.where(row < points - 1, -k, zero)
    b = jnp.where(row < points, 1.0 + 2.0 * k, 1.0)
    d = jnp.where((row == lane) & (row < points), 1.0, 0.0)
    step = 1
    while step < points:
        up = lambda v: pltpu.roll(v, step, 0)
        down = lambda v: pltpu.roll(v, LANES - step, 0)
        alpha = -a / up(b)
        gamma = -c / down(b)
        b = b + alpha * up(c) + gamma * down(a)
        d = d + alpha * up(d) + gamma * down(d)
        a, c = alpha * up(a), gamma * down(c)
        step *= 2
    inverse = d / b
    square[...] = inverse
    stride = padded(points, 16)
    for ref, matrix in ((forward_ref, SPREAD * inverse), (backward_ref, square[...].T)):
        head = matrix.astype(jnp.bfloat16).astype(jnp.float32)
        tail = (matrix - head).astype(jnp.bfloat16).astype(jnp.float32)
        tail = pltpu.roll(tail, stride, 1)
        left = jnp.where(lane >= stride, tail, head)
        right = jnp.where(lane < stride + points - LANES, tail, pltpu.roll(head, 2 * stride - LANES, 1))
        ref[:, :LANES] = left[:rows].astype(jnp.bfloat16)
        ref[:, LANES:] = right[: rows, : 3 * stride - LANES].astype(jnp.bfloat16)


def product(matrix, planes):
    columns = []
    for plane in planes:
        rows = plane.shape[0]
        fill = jnp.zeros((padded(rows, 16) - rows, LANES), jnp.float32)
        plane = jnp.concatenate([plane, fill], 0) if fill.shape[0] else plane
        head = plane.astype(jnp.bfloat16)
        tail = (plane - head.astype(jnp.float32)).astype(jnp.bfloat16)
        columns.append(jnp.concatenate([head, head, tail], 0))
    right = jnp.concatenate(columns, 1) if len(columns) > 1 else columns[0]
    out = jnp.dot(matrix, right, preferred_element_type=jnp.float32)
    return [out[:, i * LANES : (i + 1) * LANES] for i in range(len(planes))]


def neighbours(plane):
    return pltpu.roll(plane, 1, 1) + pltpu.roll(plane, LANES - 1, 1)


def step_size(sums):
    total = jnp.sum(sums, axis=0, keepdims=True)
    lane = lax.broadcasted_iota(jnp.int32, total.shape, 1)
    squares = jnp.sum(jnp.where(lane < LANES // 2, 0.0, total), axis=1, keepdims=True)
    residual = jnp.sum(jnp.where(lane < LANES // 2, total, 0.0), axis=1, keepdims=True)
    return 0.5 * residual / (squares + EPSILON)


def pack_kernel(nx, states, forcing, to_left, to_right):
    h = STEPS
    for i in range(h):
        store(to_left, i, 2 * h - 1, load(states, i, nx))
        store(to_right, i, 2 * h - 1, load(states, nx - h + i, nx))
    for i in range(h - 1):
        store(to_left, h + i, 2 * h - 1, load(forcing, i, nx))
        store(to_right, h + i, 2 * h - 1, load(forcing, nx - h + 1 + i, nx))


def wall_profile(points, rows):
    row = lax.broadcasted_iota(jnp.int32, (rows, LANES), 0).astype(jnp.float32)
    return row * (2.0 / (points - 1)) - 1.0


def forward_kernel(nx, updated, *refs):
    h = STEPS
    m = 2 * h - 1
    refs = list(refs)
    matrix_ref, states, forcing, left, right = refs[:5]
    del refs[:5]
    if updated:
        descent, d_left, d_right, sums = refs[:4]
        del refs[:4]
        tau = step_size(sums[...])
    ending_ref, start_ref, first_ref, second_ref, third_ref = refs[:5]
    moved_ref = refs[5] if updated else None
    u0, q = refs[-2:]
    points = states.shape[0] // nx
    rows = padded(points, 8)
    scale = PUSHED / SPREAD
    for i in range(h):
        before, ahead = load(left, i, m), load(right, i, m)
        if updated:
            before = before - tau * load(d_left, i, h)
            ahead = ahead - tau * load(d_right, i, h)
        u0[i] = before
        u0[h + nx + i] = ahead
        if i == h - 1:
            start_ref[0] = before
        if i == 0:
            start_ref[nx + 1] = ahead
    for i in range(nx):
        here = load(states, i, nx)
        if updated:
            here = here - tau * load(descent, i, nx)
            store(moved_ref, i, nx, here)
        u0[h + i] = here
        start_ref[1 + i] = here
    for i in range(h - 1):
        q[i] = scale * load(left, h + i, m)
        q[h - 1 + nx + i] = scale * load(right, h + i, m)
    for i in range(nx):
        q[h - 1 + i] = scale * load(forcing, i, nx)
    base = wall_profile(points, rows)
    matrix = matrix_ref[...]
    fields = [u0, first_ref, second_ref, third_ref, None]
    for t in range(h):
        source, target = fields[t], fields[t + 1]
        count = nx + 2 * (h - t - 1)
        window = [source[0], source[1]]
        pending = []
        for i in range(count):
            window = window[-2:] + [source[i + 2]]
            before, here, ahead = window
            pending.append(
                3.0 * here + neighbours(here) + q[i + t] - (base + here) * (ahead - before) * (0.5 * ADVECT / SPREAD)
            )
            if len(pending) == 2 or i == count - 1:
                for j, plane in enumerate(product(matrix, pending)):
                    at = i - len(pending) + 1 + j
                    if target is not None:
                        target[at] = plane
                    else:
                        store(ending_ref, at, nx, plane)
                pending = []


def halve(total):
    row = jnp.sum(total, axis=0, keepdims=True)
    return row + pltpu.roll(row, LANES // 2, 1)


def mismatch_kernel(nx, updated, *refs):
    h = STEPS
    refs = list(refs)
    ending, after, second, third = refs[:4]
    del refs[:4]
    if updated:
        d_after, sums = refs[:2]
        del refs[:2]
        tau = step_size(sums[...])
    mismatch_ref, low_ref, high_ref, squares_ref = refs
    total = None
    for i in range(nx):
        value = load(after, i, nx)
        if updated:
            value = value - tau * load(d_after, i, nx)
        value = load(ending, i, nx) - value
        store(mismatch_ref, i, nx, value)
        if i < h:
            store(low_ref, i, 2 * h, value)
        if i >= nx - h:
            store(high_ref, i - (nx - h), 2 * h, value)
        total = value * value if total is None else total + value * value
    squares_ref[...] = halve(total)
    for i in range(h - 1):
        store(low_ref, h + i, 2 * h, third[1 + 1 + i])
        store(high_ref, h + i, 2 * h, third[1 + nx - h + i])
    store(low_ref, 2 * h - 1, 2 * h, second[2 + 2])
    store(high_ref, 2 * h - 1, 2 * h, second[2 + nx - 3])


def adjoint_kernel(nx, matrix_ref, start, first, second, third, mismatch, from_left, from_right, lam_ref, a, b):
    h = STEPS
    points = mismatch.shape[0] // nx
    base = wall_profile(points, padded(points, 8))
    matrix = matrix_ref[...]

    def field(t, i):
        if t == 0:
            return start[i + 1]
        if t == 1:
            return first[i + 3]
        if t == 2:
            if i == -3:
                return load(from_left, 2 * h - 1, 2 * h)
            if i == nx + 2:
                return load(from_right, 2 * h - 1, 2 * h)
            return second[i + 2]
        if i < -1:
            return load(from_left, h + i + 4, 2 * h)
        if i > nx:
            return load(from_right, h + i - nx - 1, 2 * h)
        return third[i + 1]

    def weight(i):
        if i < 0:
            return load(from_left, h + i, 2 * h)
        if i >= nx:
            return load(from_right, i - nx, 2 * h)
        return load(mismatch, i, nx)

    for t in reversed(range(h)):
        source, target = (a, b) if t % 2 == 0 else (b, a)
        window = []
        low, high = -(t + 1), nx + t + 1
        for start_at in range(low, high, 2):
            group = list(range(start_at, min(start_at + 2, high)))
            lams = [weight(i) if t == h - 1 else source[i + h] for i in group]
            for i, mu in zip(group, product(matrix, lams)):
                u = field(t, i)
                window.append((u, mu, (base + u) * mu))
                window = window[-3:]
                if len(window) == 3:
                    (u0, _, f0), (_, m1, _), (u2, _, f2) = window
                    value = SPREAD * (3.0 * m1 + neighbours(m1)) + (0.5 * ADVECT) * ((f2 - f0) - m1 * (u2 - u0))
                    if t == 0:
                        lam_ref[i - 1] = value
                    else:
                        target[i - 1 + h] = value


def sums_kernel(nx, devices, lam, prior, states, squares, sums_ref):
    total = None
    for i in range(nx):
        value = lam[i] - (load(prior, i, nx) - load(states, i, nx))
        total = value * value if total is None else total + value * value
    lane = lax.broadcasted_iota(jnp.int32, (1, LANES), 1)
    sums_ref[...] = jnp.broadcast_to(jnp.where(lane < LANES // 2, squares[...], halve(total)), (devices, LANES))


def descent_kernel(nx, lam, prior, states, descent_ref, low_ref, high_ref):
    h = STEPS
    for i in range(nx):
        value = lam[i] - (load(prior, i, nx) - load(states, i, nx))
        store(descent_ref, i, nx, value)
        if i < h:
            store(low_ref, i, h, value)
        if i >= nx - h:
            store(high_ref, i - (nx - h), h, value)


def final_kernel(nx, lam, prior, states, sums, out_ref):
    tau = step_size(sums[...])
    for i in range(nx):
        here = load(states, i, nx)
        store(out_ref, i, nx, here - tau * (lam[i] - (load(prior, i, nx) - here)))


def shift(block, axis, distance):
    devices = lax.axis_size(axis)
    return lax.ppermute(block, axis, [((i - distance) % devices, i) for i in range(devices)])


def per_device(states, forcing, wall_viscosity):
    nx, points, _ = forcing.shape
    rows = padded(points, 8)
    depth = 3 * padded(points, 16)
    devices = lax.axis_size("seg") * lax.axis_size("space")
    h = STEPS
    f32, bf16 = jnp.float32, jnp.bfloat16

    def flat(planes):
        return ((planes * points, LANES), f32)

    def tiles(planes):
        return ((planes, rows, LANES), f32)

    states = jnp.transpose(states[0], (1, 0, 2)).reshape(nx * points, LANES)
    forcing = jnp.transpose(forcing, (1, 0, 2)).reshape(nx * points, LANES)
    to_left, to_right = call(
        functools.partial(pack_kernel, nx), "pack", [flat(2 * h - 1)] * 2, [states, forcing]
    )
    left = shift(to_right, "space", 1)
    right = shift(to_left, "space", -1)
    after = shift(states, "seg", -1)
    k = jnp.broadcast_to(jnp.pad(wall_viscosity, (0, LANES - points))[:, None], (LANES, LANES))
    forward, backward = call(
        functools.partial(inverse_kernel, points, rows),
        "inverse",
        [((rows, depth), bf16)] * 2,
        [k],
        [pltpu.VMEM((LANES, LANES), f32)],
    )
    current = states
    moved = d_after = sums = None
    for iteration in range(ITERS):
        updated = iteration > 0
        ending, start, first, second, third, *now = call(
            functools.partial(forward_kernel, nx, updated),
            "forward",
            [flat(nx), tiles(nx + 2), tiles(nx + 6), tiles(nx + 4), tiles(nx + 2)] + [flat(nx)] * updated,
            [forward, states, forcing, left, right] + (moved + [sums] if updated else []),
            [pltpu.VMEM((nx + 2 * h, rows, LANES), f32), pltpu.VMEM((nx + 2 * h - 2, rows, LANES), f32)],
        )
        current = now[0] if updated else states
        prior = shift(ending, "seg", 1)
        mismatch, low, high, squares = call(
            functools.partial(mismatch_kernel, nx, updated),
            "mismatch",
            [flat(nx), flat(2 * h), flat(2 * h), ((1, LANES), f32)],
            [ending, after, second, third] + ([d_after, sums] if updated else []),
        )
        from_left = shift(high, "space", 1)
        from_right = shift(low, "space", -1)
        lam = call(
            functools.partial(adjoint_kernel, nx),
            "adjoint",
            [tiles(nx)],
            [backward, start, first, second, third, mismatch, from_left, from_right],
            [pltpu.VMEM((nx + 2 * h, rows, LANES), f32)] * 2,
        )[0]
        rows_of_sums = call(
            functools.partial(sums_kernel, nx, devices), "sums", [((devices, LANES), f32)], [lam, prior, current, squares]
        )[0]
        sums = lax.all_to_all(rows_of_sums, BOTH, 0, 0, tiled=True)
        if iteration < ITERS - 1:
            descent, d_low, d_high = call(
                functools.partial(descent_kernel, nx), "descent", [flat(nx), flat(h), flat(h)], [lam, prior, current]
            )
            moved = [descent, shift(d_high, "space", 1), shift(d_low, "space", -1)]
            d_after = shift(descent, "seg", -1)
    new = call(functools.partial(final_kernel, nx), "final", [flat(nx)], [lam, prior, current, sums])[0]

    def placed(block):
        return jnp.transpose(block.reshape(points, nx, LANES), (1, 0, 2))[None]

    return (placed(new), placed(mismatch))


def solution(mesh):
    placed = (P("seg", "space", None, None), P("space", None, None), P())
    return jax.shard_map(
        per_device,
        mesh=mesh,
        in_specs=placed,
        out_specs=(P("seg", "space", None, None), P("seg", "space", None, None)),
        check_vma=False,
    )
```

```python
import functools

import jax
import jax.numpy as jnp
from jax import lax
from jax.experimental import pallas as pl
from jax.experimental.pallas import tpu as pltpu
from jax.sharding import PartitionSpec as P

STEPS = 4
ITERS = 2
ADVECT = 0.15
SPREAD = 0.2
PUSHED = 0.25
EPSILON = 1e-06
BOTH = ("seg", "space")
VMEM = pl.BlockSpec(memory_space=pltpu.VMEM)
LANES = 128


def padded(count, step):
    return -(-count // step) * step


def load(ref, i, planes):
    points = ref.shape[0] // planes
    plane = ref[pl.ds(i, points, stride=planes), :]
    return jnp.concatenate([plane, jnp.zeros((padded(points, 8) - points, LANES), jnp.float32)], 0)


def store(ref, i, planes, plane):
    points = ref.shape[0] // planes
    ref[pl.ds(i, points, stride=planes), :] = plane[:points]


def call(kernel, name, outs, operands, scratch=(), spec=VMEM):
    return pl.pallas_call(
        kernel,
        name=name,
        out_shape=[jax.ShapeDtypeStruct(shape, dtype) for shape, dtype in outs],
        in_specs=[spec] * len(operands),
        out_specs=[VMEM] * len(outs),
        scratch_shapes=list(scratch),
        compiler_params=pltpu.CompilerParams(vmem_limit_bytes=32 * 1024 * 1024),
    )(*operands)


def inverse_kernel(points, rows, k_ref, states, forward_ref, backward_ref, states_ref, square):
    states_ref[...] = states[...]
    row = lax.broadcasted_iota(jnp.int32, (LANES, LANES), 0)
    lane = lax.broadcasted_iota(jnp.int32, (LANES, LANES), 1)
    k = k_ref[...]
    zero = jnp.zeros_like(k)
    a = jnp.where((row >= 1) & (row < points), -k, zero)
    c = jnp.where(row < points - 1, -k, zero)
    b = jnp.where(row < points, 1.0 + 2.0 * k, 1.0)
    d = jnp.where((row == lane) & (row < points), 1.0, 0.0)
    step = 1
    while step < points:
        up = lambda v: pltpu.roll(v, step, 0)
        down = lambda v: pltpu.roll(v, LANES - step, 0)
        alpha = -a / up(b)
        gamma = -c / down(b)
        b = b + alpha * up(c) + gamma * down(a)
        d = d + alpha * up(d) + gamma * down(d)
        a, c = alpha * up(a), gamma * down(c)
        step *= 2
    inverse = d / b
    square[...] = inverse
    stride = padded(points, 16)
    for ref, matrix in ((forward_ref, SPREAD * inverse), (backward_ref, square[...].T)):
        head = matrix.astype(jnp.bfloat16).astype(jnp.float32)
        tail = (matrix - head).astype(jnp.bfloat16).astype(jnp.float32)
        tail = pltpu.roll(tail, stride, 1)
        left = jnp.where(lane >= stride, tail, head)
        right = jnp.where(lane < stride + points - LANES, tail, pltpu.roll(head, 2 * stride - LANES, 1))
        ref[:, :LANES] = left[:rows].astype(jnp.bfloat16)
        ref[:, LANES:] = right[: rows, : 3 * stride - LANES].astype(jnp.bfloat16)


def product(matrix, planes):
    columns = []
    for plane in planes:
        rows = plane.shape[0]
        fill = jnp.zeros((padded(rows, 16) - rows, LANES), jnp.float32)
        plane = jnp.concatenate([plane, fill], 0) if fill.shape[0] else plane
        head = plane.astype(jnp.bfloat16)
        tail = (plane - head.astype(jnp.float32)).astype(jnp.bfloat16)
        columns.append(jnp.concatenate([head, head, tail], 0))
    right = jnp.concatenate(columns, 1) if len(columns) > 1 else columns[0]
    out = jnp.dot(matrix, right, preferred_element_type=jnp.float32)
    return [out[:, i * LANES : (i + 1) * LANES] for i in range(len(planes))]


def neighbours(plane):
    return pltpu.roll(plane, 1, 1) + pltpu.roll(plane, LANES - 1, 1)


def step_size(sums):
    total = jnp.sum(sums, axis=0, keepdims=True)
    lane = lax.broadcasted_iota(jnp.int32, total.shape, 1)
    squares = jnp.sum(jnp.where(lane < LANES // 2, 0.0, total), axis=1, keepdims=True)
    residual = jnp.sum(jnp.where(lane < LANES // 2, total, 0.0), axis=1, keepdims=True)
    return 0.5 * residual / (squares + EPSILON)


def pack_kernel(nx, states_hbm, forcing_hbm, to_left, to_right, states, forcing, sems):
    h = STEPS
    copies = [
        pltpu.make_async_copy(states_hbm, states, sems.at[0]),
        pltpu.make_async_copy(forcing_hbm, forcing, sems.at[1]),
    ]
    for copy in copies:
        copy.start()
    copies[0].wait()
    for i in range(h):
        store(to_left, i, 2 * h - 1, load(states, i, nx))
        store(to_right, i, 2 * h - 1, load(states, nx - h + i, nx))
    copies[1].wait()
    for i in range(h - 1):
        store(to_left, h + i, 2 * h - 1, load(forcing, i, nx))
        store(to_right, h + i, 2 * h - 1, load(forcing, nx - h + 1 + i, nx))


def copy_kernel(given, out):
    out[...] = given[...]


def wall_profile(points, rows):
    row = lax.broadcasted_iota(jnp.int32, (rows, LANES), 0).astype(jnp.float32)
    return row * (2.0 / (points - 1)) - 1.0


def forward_kernel(nx, updated, *refs):
    h = STEPS
    m = 2 * h - 1
    refs = list(refs)
    matrix_ref, states, forcing, left, right = refs[:5]
    del refs[:5]
    if updated:
        descent, d_left, d_right, sums = refs[:4]
        del refs[:4]
        tau = step_size(sums[...])
    ending_ref, start_ref, first_ref, second_ref, third_ref = refs[:5]
    u0, q = refs[-2:]
    points = states.shape[0] // nx
    rows = padded(points, 8)
    scale = PUSHED / SPREAD
    for i in range(h):
        before, ahead = load(left, i, m), load(right, i, m)
        if updated:
            before = before - tau * load(d_left, i, h)
            ahead = ahead - tau * load(d_right, i, h)
        u0[i] = before
        u0[h + nx + i] = ahead
        if i == h - 1:
            start_ref[0] = before
        if i == 0:
            start_ref[nx + 1] = ahead
    for i in range(nx):
        here = load(states, i, nx)
        if updated:
            here = here - tau * load(descent, i, nx)
        u0[h + i] = here
        start_ref[1 + i] = here
    for i in range(h - 1):
        q[i] = scale * load(left, h + i, m)
        q[h - 1 + nx + i] = scale * load(right, h + i, m)
    for i in range(nx):
        q[h - 1 + i] = scale * load(forcing, i, nx)
    base = wall_profile(points, rows)
    matrix = matrix_ref[...]
    fields = [u0, first_ref, second_ref, third_ref, None]
    for t in range(h):
        source, target = fields[t], fields[t + 1]
        count = nx + 2 * (h - t - 1)
        window = [source[0], source[1]]
        pending = []
        for i in range(count):
            window = window[-2:] + [source[i + 2]]
            before, here, ahead = window
            pending.append(
                3.0 * here + neighbours(here) + q[i + t] - (base + here) * (ahead - before) * (0.5 * ADVECT / SPREAD)
            )
            if len(pending) == 2 or i == count - 1:
                for j, plane in enumerate(product(matrix, pending)):
                    at = i - len(pending) + 1 + j
                    if target is not None:
                        target[at] = plane
                    else:
                        store(ending_ref, at, nx, plane)
                pending = []


def halve(total):
    row = jnp.sum(total, axis=0, keepdims=True)
    return row + pltpu.roll(row, LANES // 2, 1)


def mismatch_kernel(nx, updated, *refs):
    h = STEPS
    refs = list(refs)
    ending, after, second, third = refs[:4]
    del refs[:4]
    if updated:
        d_after, sums = refs[:2]
        del refs[:2]
        tau = step_size(sums[...])
    mismatch_ref, low_ref, high_ref, squares_ref = refs
    total = None
    for i in range(nx):
        value = load(after, i, nx)
        if updated:
            value = value - tau * load(d_after, i, nx)
        value = load(ending, i, nx) - value
        store(mismatch_ref, i, nx, value)
        if i < h:
            store(low_ref, i, 2 * h, value)
        if i >= nx - h:
            store(high_ref, i - (nx - h), 2 * h, value)
        total = value * value if total is None else total + value * value
    squares_ref[...] = halve(total)
    for i in range(h - 1):
        store(low_ref, h + i, 2 * h, third[1 + 1 + i])
        store(high_ref, h + i, 2 * h, third[1 + nx - h + i])
    store(low_ref, 2 * h - 1, 2 * h, second[2 + 2])
    store(high_ref, 2 * h - 1, 2 * h, second[2 + nx - 3])


def adjoint_kernel(
    nx, devices, matrix_ref, start, first, second, third, mismatch, from_left, from_right, prior, squares,
    descent_ref, sums_ref, a, b,
):
    h = STEPS
    points = mismatch.shape[0] // nx
    base = wall_profile(points, padded(points, 8))
    matrix = matrix_ref[...]

    def field(t, i):
        if t == 0:
            return start[i + 1]
        if t == 1:
            return first[i + 3]
        if t == 2:
            if i == -3:
                return load(from_left, 2 * h - 1, 2 * h)
            if i == nx + 2:
                return load(from_right, 2 * h - 1, 2 * h)
            return second[i + 2]
        if i < -1:
            return load(from_left, h + i + 4, 2 * h)
        if i > nx:
            return load(from_right, h + i - nx - 1, 2 * h)
        return third[i + 1]

    def weight(i):
        if i < 0:
            return load(from_left, h + i, 2 * h)
        if i >= nx:
            return load(from_right, i - nx, 2 * h)
        return load(mismatch, i, nx)

    total = None
    for t in reversed(range(h)):
        source, target = (a, b) if t % 2 == 0 else (b, a)
        window = []
        low, high = -(t + 1), nx + t + 1
        for start_at in range(low, high, 2):
            group = list(range(start_at, min(start_at + 2, high)))
            lams = [weight(i) if t == h - 1 else source[i + h] for i in group]
            for i, mu in zip(group, product(matrix, lams)):
                u = field(t, i)
                window.append((u, mu, (base + u) * mu))
                window = window[-3:]
                if len(window) == 3:
                    (u0, _, f0), (_, m1, _), (u2, _, f2) = window
                    value = SPREAD * (3.0 * m1 + neighbours(m1)) + (0.5 * ADVECT) * ((f2 - f0) - m1 * (u2 - u0))
                    if t == 0:
                        value = value - (load(prior, i - 1, nx) - start[i])
                        descent_ref[i - 1] = value
                        total = value * value if total is None else total + value * value
                    else:
                        target[i - 1 + h] = value
    lane = lax.broadcasted_iota(jnp.int32, (1, LANES), 1)
    sums_ref[...] = jnp.broadcast_to(jnp.where(lane < LANES // 2, squares[...], halve(total)), (devices, LANES))


def descent_kernel(nx, descent, sums, descent_ref, low_ref, high_ref):
    h = STEPS
    for i in range(nx):
        value = descent[i]
        store(descent_ref, i, nx, value)
        if i < h:
            store(low_ref, i, h, value)
        if i >= nx - h:
            store(high_ref, i - (nx - h), h, value)


def final_kernel(nx, start, descent, sums, out_ref):
    tau = step_size(sums[...])
    for i in range(nx):
        store(out_ref, i, nx, start[i + 1] - tau * descent[i])


def shift(block, axis, distance):
    devices = lax.axis_size(axis)
    return lax.ppermute(block, axis, [((i - distance) % devices, i) for i in range(devices)])


def per_device(states, forcing, wall_viscosity):
    nx, points, _ = forcing.shape
    rows = padded(points, 8)
    depth = 3 * padded(points, 16)
    devices = lax.axis_size("seg") * lax.axis_size("space")
    h = STEPS
    f32, bf16 = jnp.float32, jnp.bfloat16

    def flat(planes):
        return ((planes * points, LANES), f32)

    def tiles(planes):
        return ((planes, rows, LANES), f32)

    states = jnp.transpose(states[0], (1, 0, 2)).reshape(nx * points, LANES)
    forcing = jnp.transpose(forcing, (1, 0, 2)).reshape(nx * points, LANES)
    to_left, to_right, states, forcing = call(
        functools.partial(pack_kernel, nx),
        "pack",
        [flat(2 * h - 1)] * 2 + [flat(nx)] * 2,
        [states, forcing],
        [pltpu.SemaphoreType.DMA((2,))],
        pl.BlockSpec(memory_space=pltpu.HBM),
    )
    left = shift(to_right, "space", 1)
    right = shift(to_left, "space", -1)
    k = jnp.broadcast_to(jnp.pad(wall_viscosity, (0, LANES - points))[:, None], (LANES, LANES))
    forward, backward, states = call(
        functools.partial(inverse_kernel, points, rows),
        "inverse",
        [((rows, depth), bf16)] * 2 + [flat(nx)],
        [k, states],
        [pltpu.VMEM((LANES, LANES), f32)],
    )
    after = shift(states, "seg", -1)
    moved = d_after = sums = None
    for iteration in range(ITERS):
        updated = iteration > 0
        ending, start, first, second, third = call(
            functools.partial(forward_kernel, nx, updated),
            "forward",
            [flat(nx), tiles(nx + 2), tiles(nx + 6), tiles(nx + 4), tiles(nx + 2)],
            [forward, states, forcing, left, right] + (moved + [sums] if updated else []),
            [pltpu.VMEM((nx + 2 * h, rows, LANES), f32), pltpu.VMEM((nx + 2 * h - 2, rows, LANES), f32)],
        )
        prior = shift(ending, "seg", 1)
        mismatch, low, high, squares = call(
            functools.partial(mismatch_kernel, nx, updated),
            "mismatch",
            [flat(nx), flat(2 * h), flat(2 * h), ((1, LANES), f32)],
            [ending, after, second, third] + ([d_after, sums] if updated else []),
        )
        from_left = shift(high, "space", 1)
        from_right = shift(low, "space", -1)
        descent, rows_of_sums = call(
            functools.partial(adjoint_kernel, nx, devices),
            "adjoint",
            [tiles(nx), ((devices, LANES), f32)],
            [backward, start, first, second, third, mismatch, from_left, from_right, prior, squares],
            [pltpu.VMEM((nx + 2 * h, rows, LANES), f32)] * 2,
        )
        sums = lax.all_to_all(rows_of_sums, BOTH, 0, 0, tiled=True)
        if iteration < ITERS - 1:
            descent, d_low, d_high = call(
                functools.partial(descent_kernel, nx),
                "descent",
                [flat(nx), flat(h), flat(h)],
                [descent, rows_of_sums],
            )
            moved = [descent, shift(d_high, "space", 1), shift(d_low, "space", -1)]
            d_after = shift(descent, "seg", -1)
    mismatch = call(copy_kernel, "mismatch_out", [flat(nx)], [mismatch])[0]
    new = call(functools.partial(final_kernel, nx), "final", [flat(nx)], [start, descent, sums])[0]

    def placed(block):
        return jnp.transpose(block.reshape(points, nx, LANES), (1, 0, 2))[None]

    return (placed(new), placed(mismatch))


def solution(mesh):
    placed = (P("seg", "space", None, None), P("space", None, None), P())
    return jax.shard_map(
        per_device,
        mesh=mesh,
        in_specs=placed,
        out_specs=(P("seg", "space", None, None), P("seg", "space", None, None)),
        check_vma=False,
    )
```

```python
import functools

import jax
import jax.numpy as jnp
from jax import lax
from jax.experimental import pallas as pl
from jax.experimental.pallas import tpu as pltpu
from jax.sharding import PartitionSpec as P

STEPS = 4
ITERS = 2
ADVECT = 0.15
SPREAD = 0.2
PUSHED = 0.25
EPSILON = 1e-06
BOTH = ("seg", "space")
VMEM = pl.BlockSpec(memory_space=pltpu.VMEM)
LANES = 128
PARTS = 4


def padded(count, step):
    return -(-count // step) * step


def load(ref, i, planes):
    points = ref.shape[0] // planes
    plane = ref[pl.ds(i, points, stride=planes), :]
    return jnp.concatenate([plane, jnp.zeros((padded(points, 8) - points, LANES), jnp.float32)], 0)


def store(ref, i, planes, plane):
    points = ref.shape[0] // planes
    ref[pl.ds(i, points, stride=planes), :] = plane[:points]


WORK = {"forward": 4e9, "inverse": 1e9}


def call(kernel, name, outs, operands, scratch=(), specs=None, fast=False):
    return pl.pallas_call(
        kernel,
        name=name,
        out_shape=[jax.ShapeDtypeStruct(shape, dtype) for shape, dtype in outs],
        in_specs=specs or [VMEM] * len(operands),
        out_specs=[VMEM] * len(outs),
        scratch_shapes=list(scratch),
        cost_estimate=pl.CostEstimate(flops=int(WORK[name]), transcendentals=0, bytes_accessed=1 << 20) if name in WORK and not fast else None,
        compiler_params=pltpu.CompilerParams(vmem_limit_bytes=32 * 1024 * 1024),
    )(*operands)


def inverse_kernel(points, rows, k_ref, forward_ref, backward_ref, square):
    row = lax.broadcasted_iota(jnp.int32, (LANES, LANES), 0)
    lane = lax.broadcasted_iota(jnp.int32, (LANES, LANES), 1)
    square[0:1, :] = jnp.zeros((1, LANES), jnp.float32)
    square[0:1, :points] = k_ref[...]
    k = jnp.sum(jnp.where(row == lane, square[0:1, :], 0.0), axis=1, keepdims=True)
    k = jnp.broadcast_to(k, (LANES, LANES))
    zero = jnp.zeros_like(k)
    a = jnp.where((row >= 1) & (row < points), -k, zero)
    c = jnp.where(row < points - 1, -k, zero)
    b = jnp.where(row < points, 1.0 + 2.0 * k, 1.0)
    d = jnp.where((row == lane) & (row < points), 1.0, 0.0)
    step = 1
    while step < points:
        up = lambda v: pltpu.roll(v, step, 0)
        down = lambda v: pltpu.roll(v, LANES - step, 0)
        alpha = -a / up(b)
        gamma = -c / down(b)
        b = b + alpha * up(c) + gamma * down(a)
        d = d + alpha * up(d) + gamma * down(d)
        a, c = alpha * up(a), gamma * down(c)
        step *= 2
    inverse = d / b
    square[...] = inverse
    stride = padded(points, 16)
    for ref, matrix in ((forward_ref, SPREAD * inverse), (backward_ref, square[...].T)):
        head = matrix.astype(jnp.bfloat16).astype(jnp.float32)
        tail = (matrix - head).astype(jnp.bfloat16).astype(jnp.float32)
        tail = pltpu.roll(tail, stride, 1)
        left = jnp.where(lane >= stride, tail, head)
        right = jnp.where(lane < stride + points - LANES, tail, pltpu.roll(head, 2 * stride - LANES, 1))
        ref[:, :LANES] = left[:rows].astype(jnp.bfloat16)
        ref[:, LANES:] = right[: rows, : 3 * stride - LANES].astype(jnp.bfloat16)


def product(matrix, planes):
    columns = []
    for plane in planes:
        rows = plane.shape[0]
        fill = jnp.zeros((padded(rows, 16) - rows, LANES), jnp.float32)
        plane = jnp.concatenate([plane, fill], 0) if fill.shape[0] else plane
        head = plane.astype(jnp.bfloat16)
        tail = (plane - head.astype(jnp.float32)).astype(jnp.bfloat16)
        columns.append(jnp.concatenate([head, head, tail], 0))
    right = jnp.concatenate(columns, 1) if len(columns) > 1 else columns[0]
    out = jnp.dot(matrix, right, preferred_element_type=jnp.float32)
    return [out[:, i * LANES : (i + 1) * LANES] for i in range(len(planes))]


def neighbours(plane):
    return pltpu.roll(plane, 1, 1) + pltpu.roll(plane, LANES - 1, 1)


def step_size(sums):
    total = jnp.sum(sums, axis=0, keepdims=True)
    lane = lax.broadcasted_iota(jnp.int32, total.shape, 1)
    squares = jnp.sum(jnp.where(lane < LANES // 2, 0.0, total), axis=1, keepdims=True)
    residual = jnp.sum(jnp.where(lane < LANES // 2, total, 0.0), axis=1, keepdims=True)
    return 0.5 * residual / (squares + EPSILON)


def parts(ref):
    size = padded(-(-ref.shape[0] // PARTS), 8)
    return [pl.ds(at, min(size, ref.shape[0] - at)) for at in range(0, ref.shape[0], size)]


def pack_kernel(nx, states_hbm, forcing_hbm, to_left, to_right, states, forcing, sems):
    h = STEPS
    copies = [
        [pltpu.make_async_copy(source.at[rows], target.at[rows], sems.at[k, j]) for j, rows in enumerate(parts(source))]
        for k, (source, target) in enumerate(((states_hbm, states), (forcing_hbm, forcing)))
    ]
    for copy in copies[0] + copies[1]:
        copy.start()
    for copy in copies[0]:
        copy.wait()
    for i in range(h):
        store(to_left, i, 2 * h - 1, load(states, i, nx))
        store(to_right, i, 2 * h - 1, load(states, nx - h + i, nx))
    for copy in copies[1]:
        copy.wait()
    for i in range(h - 1):
        store(to_left, h + i, 2 * h - 1, load(forcing, i, nx))
        store(to_right, h + i, 2 * h - 1, load(forcing, nx - h + 1 + i, nx))


def copy_kernel(given, out):
    out[...] = given[...]


def wall_profile(points, rows):
    row = lax.broadcasted_iota(jnp.int32, (rows, LANES), 0).astype(jnp.float32)
    return row * (2.0 / (points - 1)) - 1.0


def forward_kernel(nx, updated, *refs):
    h = STEPS
    m = 2 * h - 1
    refs = list(refs)
    matrix_ref, states, forcing, left, right = refs[:5]
    del refs[:5]
    if updated:
        descent, d_left, d_right, sums = refs[:4]
        del refs[:4]
        tau = step_size(sums[...])
    ending_ref, start_ref, first_ref, second_ref, third_ref, low_ref, high_ref = refs[:7]
    u0, q = refs[-2:]
    points = states.shape[0] // nx
    rows = padded(points, 8)
    scale = PUSHED / SPREAD
    for i in range(h):
        before, ahead = load(left, i, m), load(right, i, m)
        if updated:
            before = before - tau * load(d_left, i, h)
            ahead = ahead - tau * load(d_right, i, h)
        u0[i] = before
        u0[h + nx + i] = ahead
        if i == h - 1:
            start_ref[0] = before
        if i == 0:
            start_ref[nx + 1] = ahead
    for i in range(nx):
        here = load(states, i, nx)
        if updated:
            here = here - tau * load(descent, i, nx)
        u0[h + i] = here
        start_ref[1 + i] = here
    for i in range(h - 1):
        q[i] = scale * load(left, h + i, m)
        q[h - 1 + nx + i] = scale * load(right, h + i, m)
    for i in range(nx):
        q[h - 1 + i] = scale * load(forcing, i, nx)
    base = wall_profile(points, rows)
    matrix = matrix_ref[...]
    fields = [u0, first_ref, second_ref, third_ref, None]
    for t in range(h):
        source, target = fields[t], fields[t + 1]
        count = nx + 2 * (h - t - 1)
        window = [source[0], source[1]]
        pending = []
        for i in range(count):
            window = window[-2:] + [source[i + 2]]
            before, here, ahead = window
            pending.append(
                3.0 * here + neighbours(here) + q[i + t] - (base + here) * (ahead - before) * (0.5 * ADVECT / SPREAD)
            )
            if len(pending) == 2 or i == count - 1:
                for j, plane in enumerate(product(matrix, pending)):
                    at = i - len(pending) + 1 + j
                    if target is not None:
                        target[at] = plane
                    else:
                        store(ending_ref, at, nx, plane)
                pending = []
    for i in range(h - 1):
        store(low_ref, i, h, third_ref[1 + 1 + i])
        store(high_ref, i, h, third_ref[1 + nx - h + i])
    store(low_ref, h - 1, h, second_ref[2 + 2])
    store(high_ref, h - 1, h, second_ref[2 + nx - 3])


def halve(total):
    row = jnp.sum(total, axis=0, keepdims=True)
    return row + pltpu.roll(row, LANES // 2, 1)


def mismatch_kernel(nx, updated, *refs):
    h = STEPS
    refs = list(refs)
    ending, after = refs[:2]
    del refs[:2]
    if updated:
        d_after, sums = refs[:2]
        del refs[:2]
        tau = step_size(sums[...])
    mismatch_ref, low_ref, high_ref, squares_ref = refs
    total = None
    for i in range(nx):
        value = load(after, i, nx)
        if updated:
            value = value - tau * load(d_after, i, nx)
        value = load(ending, i, nx) - value
        store(mismatch_ref, i, nx, value)
        if i < h:
            store(low_ref, i, h, value)
        if i >= nx - h:
            store(high_ref, i - (nx - h), h, value)
        total = value * value if total is None else total + value * value
    squares_ref[...] = halve(total)


def adjoint_kernel(nx, matrix_ref, start, first, second, third, mismatch, left_fields, right_fields, left, right, lam_ref, a, b):
    h = STEPS
    points = mismatch.shape[0] // nx
    base = wall_profile(points, padded(points, 8))
    matrix = matrix_ref[...]

    def field(t, i):
        if t == 0:
            return start[i + 1]
        if t == 1:
            return first[i + 3]
        if t == 2:
            if i == -3:
                return load(left_fields, h - 1, h)
            if i == nx + 2:
                return load(right_fields, h - 1, h)
            return second[i + 2]
        if i < -1:
            return load(left_fields, i + h, h)
        if i > nx:
            return load(right_fields, i - nx - 1, h)
        return third[i + 1]

    def weight(i):
        if i < 0:
            return load(left, h + i, h)
        if i >= nx:
            return load(right, i - nx, h)
        return load(mismatch, i, nx)

    for t in reversed(range(h)):
        source, target = (a, b) if t % 2 == 0 else (b, a)
        window = []
        low, high = -(t + 1), nx + t + 1
        for start_at in range(low, high, 2):
            group = list(range(start_at, min(start_at + 2, high)))
            lams = [weight(i) if t == h - 1 else source[i + h] for i in group]
            for i, mu in zip(group, product(matrix, lams)):
                u = field(t, i)
                window.append((u, mu, (base + u) * mu))
                window = window[-3:]
                if len(window) == 3:
                    (u0, _, f0), (_, m1, _), (u2, _, f2) = window
                    value = SPREAD * (3.0 * m1 + neighbours(m1)) + (0.5 * ADVECT) * ((f2 - f0) - m1 * (u2 - u0))
                    if t == 0:
                        lam_ref[i - 1] = value
                    else:
                        target[i - 1 + h] = value

def descent_kernel(nx, devices, sent, lam, prior, start, squares, *refs):
    sums_ref, descent_ref, *edges = refs if sent else refs[1:]
    h = STEPS
    total = None
    for i in range(nx):
        value = lam[i] - (load(prior, i, nx) - start[i + 1])
        if sent:
            store(descent_ref, i, nx, value)
            if i < h:
                store(edges[0], i, h, value)
            if i >= nx - h:
                store(edges[1], i - (nx - h), h, value)
        else:
            descent_ref[i] = value
        total = value * value if total is None else total + value * value
    lane = lax.broadcasted_iota(jnp.int32, (1, LANES), 1)
    sums_ref[...] = jnp.broadcast_to(jnp.where(lane < LANES // 2, squares[...], halve(total)), (devices, LANES))


def final_kernel(nx, start, descent, sums, out_ref):
    tau = step_size(sums[...])
    for i in range(nx):
        store(out_ref, i, nx, start[i + 1] - tau * descent[i])


def shift(block, axis, distance):
    devices = lax.axis_size(axis)
    return lax.ppermute(block, axis, [((i - distance) % devices, i) for i in range(devices)])


def per_device(states, forcing, wall_viscosity):
    nx, points, _ = forcing.shape
    rows = padded(points, 8)
    depth = 3 * padded(points, 16)
    devices = lax.axis_size("seg") * lax.axis_size("space")
    h = STEPS
    f32, bf16 = jnp.float32, jnp.bfloat16

    def flat(planes):
        return ((planes * points, LANES), f32)

    def tiles(planes):
        return ((planes, rows, LANES), f32)

    states = jnp.transpose(states[0], (1, 0, 2)).reshape(nx * points, LANES)
    forcing = jnp.transpose(forcing, (1, 0, 2)).reshape(nx * points, LANES)
    to_left, to_right, states, forcing = call(
        functools.partial(pack_kernel, nx),
        "pack",
        [flat(2 * h - 1)] * 2 + [flat(nx)] * 2,
        [pltpu.with_memory_space_constraint(v, pltpu.HBM) for v in (states, forcing)],
        [pltpu.SemaphoreType.DMA((2, PARTS))],
        [pl.BlockSpec(memory_space=pltpu.HBM)] * 2,
    )
    left = shift(to_right, "space", 1)
    right = shift(to_left, "space", -1)
    after = shift(states, "seg", -1)
    forward, backward = call(
        functools.partial(inverse_kernel, points, rows),
        "inverse",
        [((rows, depth), bf16)] * 2,
        [wall_viscosity.reshape(1, points)],
        [pltpu.VMEM((LANES, LANES), f32)],
    )
    moved = d_after = sums = None
    for iteration in range(ITERS):
        updated = iteration > 0
        ending, start, first, second, third, low, high = call(
            functools.partial(forward_kernel, nx, updated),
            "forward",
            [flat(nx), tiles(nx + 2), tiles(nx + 6), tiles(nx + 4), tiles(nx + 2), flat(h), flat(h)],
            [forward, states, forcing, left, right] + (moved + [sums] if updated else []),
            [pltpu.VMEM((nx + 2 * h, rows, LANES), f32), pltpu.VMEM((nx + 2 * h - 2, rows, LANES), f32)],
            fast=updated,
        )
        prior = shift(ending, "seg", 1)
        sides = [shift(high, "space", 1), shift(low, "space", -1)]
        mismatch, low, high, squares = call(
            functools.partial(mismatch_kernel, nx, updated),
            "mismatch",
            [flat(nx), flat(h), flat(h), ((1, LANES), f32)],
            [ending, after] + ([d_after, sums] if updated else []),
        )
        sides += [shift(high, "space", 1), shift(low, "space", -1)]
        lam = call(
            functools.partial(adjoint_kernel, nx),
            "adjoint",
            [tiles(nx)],
            [backward, start, first, second, third, mismatch] + sides,
            [pltpu.VMEM((nx + 2 * h, rows, LANES), f32)] * 2,
        )[0]
        sent = iteration < ITERS - 1
        if not sent:
            kept = call(copy_kernel, "kept", [flat(nx)], [mismatch])[0]
        sums, descent, *edges = call(
            functools.partial(descent_kernel, nx, devices, sent),
            "descent",
            [((devices, LANES), f32)] + ([flat(nx), flat(h), flat(h)] if sent else [tiles(nx)]),
            [lam, prior, start, squares] + ([] if sent else [kept]),
            specs=[VMEM] * 4 + ([] if sent else [pl.BlockSpec(memory_space=pl.ANY)]),
        )
        sums = lax.all_to_all(sums, BOTH, 0, 0, tiled=True)
        if sent:
            moved = [descent, shift(edges[1], "space", 1), shift(edges[0], "space", -1)]
            d_after = shift(descent, "seg", -1)
    new = call(functools.partial(final_kernel, nx), "final", [flat(nx)], [start, descent, sums])[0]

    def placed(block):
        return jnp.transpose(block.reshape(points, nx, LANES), (1, 0, 2))[None]

    return (placed(new), placed(kept))


def solution(mesh):
    placed = (P("seg", "space", None, None), P("space", None, None), P())
    return jax.shard_map(
        per_device,
        mesh=mesh,
        in_specs=placed,
        out_specs=(P("seg", "space", None, None), P("seg", "space", None, None)),
        check_vma=False,
    )
```

```python
import functools

import jax
import jax.numpy as jnp
from jax import lax
from jax.experimental import pallas as pl
from jax.experimental.pallas import tpu as pltpu
from jax.sharding import PartitionSpec as P

STEPS = 4
ITERS = 2
ADVECT = 0.15
SPREAD = 0.2
PUSHED = 0.25
EPSILON = 1e-06
BOTH = ("seg", "space")
VMEM = pl.BlockSpec(memory_space=pltpu.VMEM)
LANES = 128
PARTS = 4


def padded(count, step):
    return -(-count // step) * step


def load(ref, i, planes):
    points = ref.shape[0] // planes
    plane = ref[pl.ds(i, points, stride=planes), :]
    return jnp.concatenate([plane, jnp.zeros((padded(points, 8) - points, LANES), jnp.float32)], 0)


def store(ref, i, planes, plane):
    points = ref.shape[0] // planes
    ref[pl.ds(i, points, stride=planes), :] = plane[:points]


WORK = {"forward": 4e9, "adjoint": 4e9, "inverse": 1e9}


def call(kernel, name, outs, operands, scratch=(), specs=None, fast=False):
    return pl.pallas_call(
        kernel,
        name=name,
        out_shape=[jax.ShapeDtypeStruct(shape, dtype) for shape, dtype in outs],
        in_specs=specs or [VMEM] * len(operands),
        out_specs=[VMEM] * len(outs),
        scratch_shapes=list(scratch),
        cost_estimate=pl.CostEstimate(flops=int(WORK[name]), transcendentals=0, bytes_accessed=1 << 20) if name in WORK and not fast else None,
        compiler_params=pltpu.CompilerParams(vmem_limit_bytes=32 * 1024 * 1024),
    )(*operands)


def inverse_kernel(points, rows, k_ref, forward_ref, backward_ref, square):
    row = lax.broadcasted_iota(jnp.int32, (LANES, LANES), 0)
    lane = lax.broadcasted_iota(jnp.int32, (LANES, LANES), 1)
    square[0:1, :] = jnp.zeros((1, LANES), jnp.float32)
    square[0:1, :points] = k_ref[...]
    k = jnp.sum(jnp.where(row == lane, square[0:1, :], 0.0), axis=1, keepdims=True)
    k = jnp.broadcast_to(k, (LANES, LANES))
    zero = jnp.zeros_like(k)
    a = jnp.where((row >= 1) & (row < points), -k, zero)
    c = jnp.where(row < points - 1, -k, zero)
    b = jnp.where(row < points, 1.0 + 2.0 * k, 1.0)
    d = jnp.where((row == lane) & (row < points), 1.0, 0.0)
    step = 1
    while step < points:
        up = lambda v: pltpu.roll(v, step, 0)
        down = lambda v: pltpu.roll(v, LANES - step, 0)
        alpha = -a / up(b)
        gamma = -c / down(b)
        b = b + alpha * up(c) + gamma * down(a)
        d = d + alpha * up(d) + gamma * down(d)
        a, c = alpha * up(a), gamma * down(c)
        step *= 2
    inverse = d / b
    square[...] = inverse
    stride = padded(points, 16)
    for ref, matrix in ((forward_ref, SPREAD * inverse), (backward_ref, square[...].T)):
        head = matrix.astype(jnp.bfloat16).astype(jnp.float32)
        tail = (matrix - head).astype(jnp.bfloat16).astype(jnp.float32)
        tail = pltpu.roll(tail, stride, 1)
        left = jnp.where(lane >= stride, tail, head)
        right = jnp.where(lane < stride + points - LANES, tail, pltpu.roll(head, 2 * stride - LANES, 1))
        ref[:, :LANES] = left[:rows].astype(jnp.bfloat16)
        ref[:, LANES:] = right[: rows, : 3 * stride - LANES].astype(jnp.bfloat16)


def product(matrix, planes):
    columns = []
    for plane in planes:
        rows = plane.shape[0]
        fill = jnp.zeros((padded(rows, 16) - rows, LANES), jnp.float32)
        plane = jnp.concatenate([plane, fill], 0) if fill.shape[0] else plane
        head = plane.astype(jnp.bfloat16)
        tail = (plane - head.astype(jnp.float32)).astype(jnp.bfloat16)
        columns.append(jnp.concatenate([head, head, tail], 0))
    right = jnp.concatenate(columns, 1) if len(columns) > 1 else columns[0]
    out = jnp.dot(matrix, right, preferred_element_type=jnp.float32)
    return [out[:, i * LANES : (i + 1) * LANES] for i in range(len(planes))]


def neighbours(plane):
    return pltpu.roll(plane, 1, 1) + pltpu.roll(plane, LANES - 1, 1)


def step_size(sums):
    total = jnp.sum(sums, axis=0, keepdims=True)
    lane = lax.broadcasted_iota(jnp.int32, total.shape, 1)
    squares = jnp.sum(jnp.where(lane < LANES // 2, 0.0, total), axis=1, keepdims=True)
    residual = jnp.sum(jnp.where(lane < LANES // 2, total, 0.0), axis=1, keepdims=True)
    return 0.5 * residual / (squares + EPSILON)


def parts(ref):
    size = padded(-(-ref.shape[0] // PARTS), 8)
    return [pl.ds(at, min(size, ref.shape[0] - at)) for at in range(0, ref.shape[0], size)]


def pack_kernel(nx, states_hbm, forcing_hbm, to_left, to_right, states, forcing, sems):
    h = STEPS
    copies = [
        [pltpu.make_async_copy(source.at[rows], target.at[rows], sems.at[k, j]) for j, rows in enumerate(parts(source))]
        for k, (source, target) in enumerate(((states_hbm, states), (forcing_hbm, forcing)))
    ]
    for copy in copies[0] + copies[1]:
        copy.start()
    for copy in copies[0]:
        copy.wait()
    for i in range(h):
        store(to_left, i, 2 * h - 1, load(states, i, nx))
        store(to_right, i, 2 * h - 1, load(states, nx - h + i, nx))
    for copy in copies[1]:
        copy.wait()
    for i in range(h - 1):
        store(to_left, h + i, 2 * h - 1, load(forcing, i, nx))
        store(to_right, h + i, 2 * h - 1, load(forcing, nx - h + 1 + i, nx))


def copy_kernel(given, order, out):
    out[...] = given[...]


def wall_profile(points, rows):
    row = lax.broadcasted_iota(jnp.int32, (rows, LANES), 0).astype(jnp.float32)
    return row * (2.0 / (points - 1)) - 1.0


def halve(total):
    row = jnp.sum(total, axis=0, keepdims=True)
    return row + pltpu.roll(row, LANES // 2, 1)


def forward_kernel(nx, updated, *refs):
    h = STEPS
    m = 2 * h - 1
    refs = list(refs)
    matrix_ref, states, forcing, left, right = refs[:5]
    del refs[:5]
    if updated:
        descent, d_left, d_right, sums, after, d_after = refs[:6]
        del refs[:6]
        tau = step_size(sums[...])
    ending_ref, start_ref, first_ref, second_ref, third_ref, low_ref, high_ref = refs[:7]
    u0, q = refs[-2:]
    points = states.shape[0] // nx
    rows = padded(points, 8)
    scale = PUSHED / SPREAD
    for i in range(h):
        before, ahead = load(left, i, m), load(right, i, m)
        if updated:
            before = before - tau * load(d_left, i, h)
            ahead = ahead - tau * load(d_right, i, h)
        u0[i] = before
        u0[h + nx + i] = ahead
        if i == h - 1:
            start_ref[0] = before
        if i == 0:
            start_ref[nx + 1] = ahead
    for i in range(nx):
        here = load(states, i, nx)
        if updated:
            here = here - tau * load(descent, i, nx)
        u0[h + i] = here
        start_ref[1 + i] = here
    for i in range(h - 1):
        q[i] = scale * load(left, h + i, m)
        q[h - 1 + nx + i] = scale * load(right, h + i, m)
    for i in range(nx):
        q[h - 1 + i] = scale * load(forcing, i, nx)
    base = wall_profile(points, rows)
    matrix = matrix_ref[...]
    fields = [u0, first_ref, second_ref, third_ref, None]
    for t in range(h):
        source, target = fields[t], fields[t + 1]
        count = nx + 2 * (h - t - 1)
        window = [source[0], source[1]]
        pending = []
        for i in range(count):
            window = window[-2:] + [source[i + 2]]
            before, here, ahead = window
            pending.append(
                3.0 * here + neighbours(here) + q[i + t] - (base + here) * (ahead - before) * (0.5 * ADVECT / SPREAD)
            )
            if len(pending) == 2 or i == count - 1:
                for j, plane in enumerate(product(matrix, pending)):
                    at = i - len(pending) + 1 + j
                    if target is not None:
                        target[at] = plane
                    else:
                        store(ending_ref, at, nx, plane)
                pending = []
    sent = 2 * h if updated else h
    for i in range(h - 1):
        store(low_ref, i, sent, third_ref[1 + 1 + i])
        store(high_ref, i, sent, third_ref[1 + nx - h + i])
    store(low_ref, h - 1, sent, second_ref[2 + 2])
    store(high_ref, h - 1, sent, second_ref[2 + nx - 3])
    if updated:
        mismatch_ref, squares_ref = refs[7:9]
        total = None
        for i in range(nx):
            value = load(ending_ref, i, nx) - (load(after, i, nx) - tau * load(d_after, i, nx))
            store(mismatch_ref, i, nx, value)
            if i < h:
                store(low_ref, h + i, sent, value)
            if i >= nx - h:
                store(high_ref, h + i - (nx - h), sent, value)
            total = value * value if total is None else total + value * value
        squares_ref[...] = halve(total)


def mismatch_kernel(nx, ending, after, mismatch_ref, low_ref, high_ref, squares_ref):
    h = STEPS
    total = None
    for i in range(nx):
        value = load(ending, i, nx) - load(after, i, nx)
        store(mismatch_ref, i, nx, value)
        if i < h:
            store(low_ref, i, h, value)
        if i >= nx - h:
            store(high_ref, i - (nx - h), h, value)
        total = value * value if total is None else total + value * value
    squares_ref[...] = halve(total)


def adjoint_kernel(nx, matrix_ref, start, first, second, third, mismatch, *refs):
    h = STEPS
    *sides, lam_ref, a, b = refs
    points = mismatch.shape[0] // nx
    sent = sides[0].shape[0] // points
    left_fields, right_fields = sides[:2]
    left, right = sides[-2:]
    base = wall_profile(points, padded(points, 8))
    matrix = matrix_ref[...]

    def field(t, i):
        if t == 0:
            return start[i + 1]
        if t == 1:
            return first[i + 3]
        if t == 2:
            if i == -3:
                return load(left_fields, h - 1, sent)
            if i == nx + 2:
                return load(right_fields, h - 1, sent)
            return second[i + 2]
        if i < -1:
            return load(left_fields, i + h, sent)
        if i > nx:
            return load(right_fields, i - nx - 1, sent)
        return third[i + 1]

    def weight(i):
        if i < 0:
            return load(left, sent + i, sent)
        if i >= nx:
            return load(right, sent - h + i - nx, sent)
        return load(mismatch, i, nx)

    for t in reversed(range(h)):
        source, target = (a, b) if t % 2 == 0 else (b, a)
        window = []
        low, high = -(t + 1), nx + t + 1
        for start_at in range(low, high, 2):
            group = list(range(start_at, min(start_at + 2, high)))
            lams = [weight(i) if t == h - 1 else source[i + h] for i in group]
            for i, mu in zip(group, product(matrix, lams)):
                u = field(t, i)
                window.append((u, mu, (base + u) * mu))
                window = window[-3:]
                if len(window) == 3:
                    (u0, _, f0), (_, m1, _), (u2, _, f2) = window
                    value = SPREAD * (3.0 * m1 + neighbours(m1)) + (0.5 * ADVECT) * ((f2 - f0) - m1 * (u2 - u0))
                    if t == 0:
                        lam_ref[i - 1] = value
                    else:
                        target[i - 1 + h] = value

def descent_kernel(nx, devices, sent, lam, prior, start, squares, *refs):
    sums_ref, descent_ref, *edges = refs if sent else refs[1:]
    h = STEPS
    total = None
    for i in range(nx):
        value = lam[i] - (load(prior, i, nx) - start[i + 1])
        if sent:
            store(descent_ref, i, nx, value)
            if i < h:
                store(edges[0], i, h, value)
            if i >= nx - h:
                store(edges[1], i - (nx - h), h, value)
        else:
            descent_ref[i] = value
        total = value * value if total is None else total + value * value
    lane = lax.broadcasted_iota(jnp.int32, (1, LANES), 1)
    sums_ref[...] = jnp.broadcast_to(jnp.where(lane < LANES // 2, squares[...], halve(total)), (devices, LANES))


def final_kernel(nx, start, descent, sums, out_ref):
    tau = step_size(sums[...])
    for i in range(nx):
        store(out_ref, i, nx, start[i + 1] - tau * descent[i])


def shift(block, axis, distance):
    devices = lax.axis_size(axis)
    return lax.ppermute(block, axis, [((i - distance) % devices, i) for i in range(devices)])


def per_device(states, forcing, wall_viscosity):
    nx, points, _ = forcing.shape
    rows = padded(points, 8)
    depth = 3 * padded(points, 16)
    devices = lax.axis_size("seg") * lax.axis_size("space")
    h = STEPS
    f32, bf16 = jnp.float32, jnp.bfloat16

    def flat(planes):
        return ((planes * points, LANES), f32)

    def tiles(planes):
        return ((planes, rows, LANES), f32)

    states = jnp.transpose(states[0], (1, 0, 2)).reshape(nx * points, LANES)
    forcing = jnp.transpose(forcing, (1, 0, 2)).reshape(nx * points, LANES)
    to_left, to_right, states, forcing = call(
        functools.partial(pack_kernel, nx),
        "pack",
        [flat(2 * h - 1)] * 2 + [flat(nx)] * 2,
        [pltpu.with_memory_space_constraint(v, pltpu.HBM) for v in (states, forcing)],
        [pltpu.SemaphoreType.DMA((2, PARTS))],
        [pl.BlockSpec(memory_space=pltpu.HBM)] * 2,
    )
    left = shift(to_right, "space", 1)
    right = shift(to_left, "space", -1)
    after = shift(states, "seg", -1)
    forward, backward = call(
        functools.partial(inverse_kernel, points, rows),
        "inverse",
        [((rows, depth), bf16)] * 2,
        [wall_viscosity.reshape(1, points)],
        [pltpu.VMEM((LANES, LANES), f32)],
    )
    moved = d_after = sums = None
    for iteration in range(ITERS):
        updated = iteration > 0
        sent = 2 * h if updated else h
        ending, start, first, second, third, low, high, *rest = call(
            functools.partial(forward_kernel, nx, updated),
            "forward",
            [flat(nx), tiles(nx + 2), tiles(nx + 6), tiles(nx + 4), tiles(nx + 2), flat(sent), flat(sent)]
            + ([flat(nx), ((1, LANES), f32)] if updated else []),
            [forward, states, forcing, left, right] + (moved + [sums, after, d_after] if updated else []),
            [pltpu.VMEM((nx + 2 * h, rows, LANES), f32), pltpu.VMEM((nx + 2 * h - 2, rows, LANES), f32)],
            fast=updated,
        )
        prior = shift(ending, "seg", 1)
        sides = [shift(high, "space", 1), shift(low, "space", -1)]
        if updated:
            mismatch, squares = rest
        else:
            mismatch, low, high, squares = call(
                functools.partial(mismatch_kernel, nx),
                "mismatch",
                [flat(nx), flat(h), flat(h), ((1, LANES), f32)],
                [ending, after],
            )
            sides += [shift(high, "space", 1), shift(low, "space", -1)]
        lam = call(
            functools.partial(adjoint_kernel, nx),
            "adjoint",
            [tiles(nx)],
            [backward, start, first, second, third, mismatch] + sides,
            [pltpu.VMEM((nx + 2 * h, rows, LANES), f32)] * 2,
            fast=not updated,
        )[0]
        sent = iteration < ITERS - 1
        if not sent:
            kept = call(copy_kernel, "kept", [flat(nx)], [mismatch, lam], specs=[VMEM, pl.BlockSpec(memory_space=pl.ANY)])[0]
        sums, descent, *edges = call(
            functools.partial(descent_kernel, nx, devices, sent),
            "descent",
            [((devices, LANES), f32)] + ([flat(nx), flat(h), flat(h)] if sent else [tiles(nx)]),
            [lam, prior, start, squares] + ([] if sent else [pltpu.with_memory_space_constraint(kept, pltpu.HBM)]),
            specs=[VMEM] * 4 + ([] if sent else [pl.BlockSpec(memory_space=pltpu.HBM)]),
        )
        sums = lax.all_to_all(sums, BOTH, 0, 0, tiled=True)
        if sent:
            moved = [descent, shift(edges[1], "space", 1), shift(edges[0], "space", -1)]
            d_after = shift(descent, "seg", -1)
    new = call(functools.partial(final_kernel, nx), "final", [flat(nx)], [start, descent, sums])[0]

    def placed(block):
        return jnp.transpose(block.reshape(points, nx, LANES), (1, 0, 2))[None]

    return (placed(new), placed(kept))


def solution(mesh):
    placed = (P("seg", "space", None, None), P("space", None, None), P())
    return jax.shard_map(
        per_device,
        mesh=mesh,
        in_specs=placed,
        out_specs=(P("seg", "space", None, None), P("seg", "space", None, None)),
        check_vma=False,
    )
```

```python
import functools

import jax
import jax.numpy as jnp
from jax import lax
from jax.experimental import pallas as pl
from jax.experimental.pallas import tpu as pltpu
from jax.sharding import PartitionSpec as P

STEPS = 4
ITERS = 2
ADVECT = 0.15
SPREAD = 0.2
PUSHED = 0.25
EPSILON = 1e-06
BOTH = ("seg", "space")
VMEM = pl.BlockSpec(memory_space=pltpu.VMEM)
LANES = 128
PARTS = 4


def padded(count, step):
    return -(-count // step) * step


def load(ref, i, planes):
    points = ref.shape[0] // planes
    plane = ref[pl.ds(i, points, stride=planes), :]
    return jnp.concatenate([plane, jnp.zeros((padded(points, 8) - points, LANES), jnp.float32)], 0)


def store(ref, i, planes, plane):
    points = ref.shape[0] // planes
    ref[pl.ds(i, points, stride=planes), :] = plane[:points]


WORK = {"forward": 4e9, "inverse": 1e9}


def call(kernel, name, outs, operands, scratch=(), specs=None, fast=False):
    return pl.pallas_call(
        kernel,
        name=name,
        out_shape=[jax.ShapeDtypeStruct(shape, dtype) for shape, dtype in outs],
        in_specs=specs or [VMEM] * len(operands),
        out_specs=[VMEM] * len(outs),
        scratch_shapes=list(scratch),
        cost_estimate=pl.CostEstimate(flops=int(WORK[name]), transcendentals=0, bytes_accessed=1 << 20) if name in WORK and not fast else None,
        compiler_params=pltpu.CompilerParams(vmem_limit_bytes=32 * 1024 * 1024),
    )(*operands)


def inverse_kernel(points, rows, k_ref, forward_ref, backward_ref, square):
    row = lax.broadcasted_iota(jnp.int32, (LANES, LANES), 0)
    lane = lax.broadcasted_iota(jnp.int32, (LANES, LANES), 1)
    square[0:1, :] = jnp.zeros((1, LANES), jnp.float32)
    square[0:1, :points] = k_ref[...]
    k = jnp.sum(jnp.where(row == lane, square[0:1, :], 0.0), axis=1, keepdims=True)
    k = jnp.broadcast_to(k, (LANES, LANES))
    zero = jnp.zeros_like(k)
    a = jnp.where((row >= 1) & (row < points), -k, zero)
    c = jnp.where(row < points - 1, -k, zero)
    b = jnp.where(row < points, 1.0 + 2.0 * k, 1.0)
    d = jnp.where((row == lane) & (row < points), 1.0, 0.0)
    step = 1
    while step < points:
        up = lambda v: pltpu.roll(v, step, 0)
        down = lambda v: pltpu.roll(v, LANES - step, 0)
        alpha = -a / up(b)
        gamma = -c / down(b)
        b = b + alpha * up(c) + gamma * down(a)
        d = d + alpha * up(d) + gamma * down(d)
        a, c = alpha * up(a), gamma * down(c)
        step *= 2
    inverse = d / b
    square[...] = inverse
    stride = padded(points, 16)
    for ref, matrix in ((forward_ref, SPREAD * inverse), (backward_ref, square[...].T)):
        head = matrix.astype(jnp.bfloat16).astype(jnp.float32)
        tail = (matrix - head).astype(jnp.bfloat16).astype(jnp.float32)
        tail = pltpu.roll(tail, stride, 1)
        left = jnp.where(lane >= stride, tail, head)
        right = jnp.where(lane < stride + points - LANES, tail, pltpu.roll(head, 2 * stride - LANES, 1))
        ref[:, :LANES] = left[:rows].astype(jnp.bfloat16)
        ref[:, LANES:] = right[: rows, : 3 * stride - LANES].astype(jnp.bfloat16)


def product(matrix, planes):
    columns = []
    for plane in planes:
        rows = plane.shape[0]
        fill = jnp.zeros((padded(rows, 16) - rows, LANES), jnp.float32)
        plane = jnp.concatenate([plane, fill], 0) if fill.shape[0] else plane
        head = plane.astype(jnp.bfloat16)
        tail = (plane - head.astype(jnp.float32)).astype(jnp.bfloat16)
        columns.append(jnp.concatenate([head, head, tail], 0))
    right = jnp.concatenate(columns, 1) if len(columns) > 1 else columns[0]
    out = jnp.dot(matrix, right, preferred_element_type=jnp.float32)
    return [out[:, i * LANES : (i + 1) * LANES] for i in range(len(planes))]


def neighbours(plane):
    return pltpu.roll(plane, 1, 1) + pltpu.roll(plane, LANES - 1, 1)


def step_size(sums):
    total = jnp.sum(sums, axis=0, keepdims=True)
    lane = lax.broadcasted_iota(jnp.int32, total.shape, 1)
    squares = jnp.sum(jnp.where(lane < LANES // 2, 0.0, total), axis=1, keepdims=True)
    residual = jnp.sum(jnp.where(lane < LANES // 2, total, 0.0), axis=1, keepdims=True)
    return 0.5 * residual / (squares + EPSILON)


def parts(ref):
    size = padded(-(-ref.shape[0] // PARTS), 8)
    return [pl.ds(at, min(size, ref.shape[0] - at)) for at in range(0, ref.shape[0], size)]


def pack_kernel(nx, states_hbm, forcing_hbm, to_left, to_right, states, forcing, sems):
    h = STEPS
    copies = [
        [pltpu.make_async_copy(source.at[rows], target.at[rows], sems.at[k, j]) for j, rows in enumerate(parts(source))]
        for k, (source, target) in enumerate(((states_hbm, states), (forcing_hbm, forcing)))
    ]
    for copy in copies[0] + copies[1]:
        copy.start()
    for copy in copies[0]:
        copy.wait()
    for i in range(h):
        store(to_left, i, 2 * h - 1, load(states, i, nx))
        store(to_right, i, 2 * h - 1, load(states, nx - h + i, nx))
    for copy in copies[1]:
        copy.wait()
    for i in range(h - 1):
        store(to_left, h + i, 2 * h - 1, load(forcing, i, nx))
        store(to_right, h + i, 2 * h - 1, load(forcing, nx - h + 1 + i, nx))


def copy_kernel(given, order, out):
    out[...] = given[...]


def wall_profile(points, rows):
    row = lax.broadcasted_iota(jnp.int32, (rows, LANES), 0).astype(jnp.float32)
    return row * (2.0 / (points - 1)) - 1.0


def halve(total):
    row = jnp.sum(total, axis=0, keepdims=True)
    return row + pltpu.roll(row, LANES // 2, 1)


def forward_kernel(nx, updated, *refs):
    h = STEPS
    m = 2 * h - 1
    refs = list(refs)
    matrix_ref, states, forcing, left, right = refs[:5]
    del refs[:5]
    if updated:
        descent, d_left, d_right, sums, after, d_after = refs[:6]
        del refs[:6]
        tau = step_size(sums[...])
    ending_ref, start_ref, first_ref, second_ref, third_ref, low_ref, high_ref = refs[:7]
    u0, q = refs[-2:]
    points = states.shape[0] // nx
    rows = padded(points, 8)
    scale = PUSHED / SPREAD
    for i in range(h):
        before, ahead = load(left, i, m), load(right, i, m)
        if updated:
            before = before - tau * load(d_left, i, h)
            ahead = ahead - tau * load(d_right, i, h)
        u0[i] = before
        u0[h + nx + i] = ahead
        if i == h - 1:
            start_ref[0] = before
        if i == 0:
            start_ref[nx + 1] = ahead
    for i in range(nx):
        here = load(states, i, nx)
        if updated:
            here = here - tau * load(descent, i, nx)
        u0[h + i] = here
        start_ref[1 + i] = here
    for i in range(h - 1):
        q[i] = scale * load(left, h + i, m)
        q[h - 1 + nx + i] = scale * load(right, h + i, m)
    for i in range(nx):
        q[h - 1 + i] = scale * load(forcing, i, nx)
    base = wall_profile(points, rows)
    matrix = matrix_ref[...]
    fields = [u0, first_ref, second_ref, third_ref, None]
    for t in range(h):
        source, target = fields[t], fields[t + 1]
        count = nx + 2 * (h - t - 1)
        window = [source[0], source[1]]
        pending = []
        for i in range(count):
            window = window[-2:] + [source[i + 2]]
            before, here, ahead = window
            pending.append(
                3.0 * here + neighbours(here) + q[i + t] - (base + here) * (ahead - before) * (0.5 * ADVECT / SPREAD)
            )
            if len(pending) == 2 or i == count - 1:
                for j, plane in enumerate(product(matrix, pending)):
                    at = i - len(pending) + 1 + j
                    if target is not None:
                        target[at] = plane
                    else:
                        store(ending_ref, at, nx, plane)
                pending = []
    sent = 2 * h if updated else h
    for i in range(h - 1):
        store(low_ref, i, sent, third_ref[1 + 1 + i])
        store(high_ref, i, sent, third_ref[1 + nx - h + i])
    store(low_ref, h - 1, sent, second_ref[2 + 2])
    store(high_ref, h - 1, sent, second_ref[2 + nx - 3])
    if updated:
        mismatch_ref, squares_ref = refs[7:9]
        total = None
        for i in range(nx):
            value = load(ending_ref, i, nx) - (load(after, i, nx) - tau * load(d_after, i, nx))
            store(mismatch_ref, i, nx, value)
            if i < h:
                store(low_ref, h + i, sent, value)
            if i >= nx - h:
                store(high_ref, h + i - (nx - h), sent, value)
            total = value * value if total is None else total + value * value
        squares_ref[...] = halve(total)


def mismatch_kernel(nx, ending, after, mismatch_ref, low_ref, high_ref, squares_ref):
    h = STEPS
    total = None
    for i in range(nx):
        value = load(ending, i, nx) - load(after, i, nx)
        store(mismatch_ref, i, nx, value)
        if i < h:
            store(low_ref, i, h, value)
        if i >= nx - h:
            store(high_ref, i - (nx - h), h, value)
        total = value * value if total is None else total + value * value
    squares_ref[...] = halve(total)


def adjoint_value(before, here, ahead):
    (u0, _, f0), (_, m1, _), (u2, _, f2) = before, here, ahead
    return SPREAD * (3.0 * m1 + neighbours(m1)) + (0.5 * ADVECT) * ((f2 - f0) - m1 * (u2 - u0))


def own_field(start, first, second, third, t, i):
    return ((start, 1), (first, 3), (second, 2), (third, 1))[t][0][i + (1, 3, 2, 1)[t]]


def inner_range(nx, t):
    low = STEPS - 1 - t
    return low, nx - low, sum(nx - 2 * j for j in range(low))


def adjoint_inner_kernel(nx, matrix_ref, start, first, second, third, mismatch, mu_ref, flux_ref, a, b):
    h = STEPS
    points = mismatch.shape[0] // nx
    base = wall_profile(points, padded(points, 8))
    matrix = matrix_ref[...]
    for t in reversed(range(h)):
        source, target = (a, b) if t % 2 == 0 else (b, a)
        low, high, at = inner_range(nx, t)
        window = []
        for begin in range(low, high, 2):
            group = list(range(begin, min(begin + 2, high)))
            lams = [load(mismatch, i, nx) if t == h - 1 else source[i] for i in group]
            for i, mu in zip(group, product(matrix, lams)):
                u = own_field(start, first, second, third, t, i)
                flux = (base + u) * mu
                mu_ref[at + i - low] = mu
                flux_ref[at + i - low] = flux
                window = window[-2:] + [(u, mu, flux)]
                if len(window) == 3 and t > 0:
                    target[i - 1] = adjoint_value(*window)


def adjoint_outer_kernel(nx, matrix_ref, start, first, second, third, mu_ref, flux_ref, *refs):
    h = STEPS
    *sides, lam_ref, lams, mus, fluxes = refs
    points = sides[0].shape[0] // (2 * h) if len(sides) == 2 else sides[0].shape[0] // h
    sent = sides[0].shape[0] // points
    left_fields, right_fields = sides[:2]
    left, right = sides[-2:]
    base = wall_profile(points, padded(points, 8))
    matrix = matrix_ref[...]

    def field(t, i):
        if t == 2 and i == -3:
            return load(left_fields, h - 1, sent)
        if t == 2 and i == nx + 2:
            return load(right_fields, h - 1, sent)
        if t == 3 and i < -1:
            return load(left_fields, i + h, sent)
        if t == 3 and i > nx:
            return load(right_fields, i - nx - 1, sent)
        return own_field(start, first, second, third, t, i)

    for t in reversed(range(h)):
        low, high, at = inner_range(nx, t)
        planes = list(range(low - h, low)) + list(range(high, high + h))
        for begin in range(0, 2 * h, 2):
            group = planes[begin : begin + 2]
            if t < h - 1:
                given = [lams[begin + j] for j in range(2)]
            elif begin < h:
                given = [load(left, sent + i, sent) for i in group]
            else:
                given = [load(right, sent - h + i - nx, sent) for i in group]
            for j, mu in enumerate(product(matrix, given)):
                mus[begin + j] = mu
                fluxes[begin + j] = (base + field(t, group[j])) * mu

        def known(i, t=t, planes=planes, low=low, at=at):
            if i in planes:
                j = planes.index(i)
                return field(t, i), mus[j], fluxes[j]
            return field(t, i), mu_ref[at + i - low], flux_ref[at + i - low]

        for j, i in enumerate(list(range(low - h + 1, low + 1)) + list(range(high - 1, high + h - 1))):
            value = adjoint_value(known(i - 1), known(i), known(i + 1))
            if t == 0:
                lam_ref[i] = value
            else:
                lams[j] = value


def descent_kernel(nx, devices, sent, lam, prior, start, squares, *refs):
    sums_ref, descent_ref, *edges = refs if sent else refs[1:]
    h = STEPS
    total = None
    for i in range(nx):
        value = lam[i] - (load(prior, i, nx) - start[i + 1])
        if sent:
            store(descent_ref, i, nx, value)
            if i < h:
                store(edges[0], i, h, value)
            if i >= nx - h:
                store(edges[1], i - (nx - h), h, value)
        else:
            descent_ref[i] = value
        total = value * value if total is None else total + value * value
    lane = lax.broadcasted_iota(jnp.int32, (1, LANES), 1)
    sums_ref[...] = jnp.broadcast_to(jnp.where(lane < LANES // 2, squares[...], halve(total)), (devices, LANES))


def final_kernel(nx, start, descent, sums, out_ref):
    tau = step_size(sums[...])
    for i in range(nx):
        store(out_ref, i, nx, start[i + 1] - tau * descent[i])


def shift(block, axis, distance):
    devices = lax.axis_size(axis)
    return lax.ppermute(block, axis, [((i - distance) % devices, i) for i in range(devices)])


def per_device(states, forcing, wall_viscosity):
    nx, points, _ = forcing.shape
    rows = padded(points, 8)
    depth = 3 * padded(points, 16)
    devices = lax.axis_size("seg") * lax.axis_size("space")
    h = STEPS
    f32, bf16 = jnp.float32, jnp.bfloat16

    def flat(planes):
        return ((planes * points, LANES), f32)

    def tiles(planes):
        return ((planes, rows, LANES), f32)

    states = jnp.transpose(states[0], (1, 0, 2)).reshape(nx * points, LANES)
    forcing = jnp.transpose(forcing, (1, 0, 2)).reshape(nx * points, LANES)
    to_left, to_right, states, forcing = call(
        functools.partial(pack_kernel, nx),
        "pack",
        [flat(2 * h - 1)] * 2 + [flat(nx)] * 2,
        [pltpu.with_memory_space_constraint(v, pltpu.HBM) for v in (states, forcing)],
        [pltpu.SemaphoreType.DMA((2, PARTS))],
        [pl.BlockSpec(memory_space=pltpu.HBM)] * 2,
    )
    left = shift(to_right, "space", 1)
    right = shift(to_left, "space", -1)
    after = shift(states, "seg", -1)
    forward, backward = call(
        functools.partial(inverse_kernel, points, rows),
        "inverse",
        [((rows, depth), bf16)] * 2,
        [wall_viscosity.reshape(1, points)],
        [pltpu.VMEM((LANES, LANES), f32)],
    )
    moved = d_after = sums = None
    for iteration in range(ITERS):
        updated = iteration > 0
        sent = 2 * h if updated else h
        ending, start, first, second, third, low, high, *rest = call(
            functools.partial(forward_kernel, nx, updated),
            "forward",
            [flat(nx), tiles(nx + 2), tiles(nx + 6), tiles(nx + 4), tiles(nx + 2), flat(sent), flat(sent)]
            + ([flat(nx), ((1, LANES), f32)] if updated else []),
            [forward, states, forcing, left, right] + (moved + [sums, after, d_after] if updated else []),
            [pltpu.VMEM((nx + 2 * h, rows, LANES), f32), pltpu.VMEM((nx + 2 * h - 2, rows, LANES), f32)],
            fast=updated,
        )
        prior = shift(ending, "seg", 1)
        sides = [shift(high, "space", 1), shift(low, "space", -1)]
        if updated:
            mismatch, squares = rest
        else:
            mismatch, low, high, squares = call(
                functools.partial(mismatch_kernel, nx),
                "mismatch",
                [flat(nx), flat(h), flat(h), ((1, LANES), f32)],
                [ending, after],
            )
            sides += [shift(high, "space", 1), shift(low, "space", -1)]
        fields = [start, first, second, third]
        planes = sum(nx - 2 * j for j in range(h))
        inner = call(
            functools.partial(adjoint_inner_kernel, nx),
            "adjoint_inner",
            [tiles(planes)] * 2,
            [backward, *fields, mismatch],
            [pltpu.VMEM((nx, rows, LANES), f32)] * 2,
        )
        lam = call(
            functools.partial(adjoint_outer_kernel, nx),
            "adjoint_outer",
            [tiles(nx)],
            [backward, *fields, *inner, *sides],
            [pltpu.VMEM((2 * h, rows, LANES), f32)] * 3,
        )[0]
        sent = iteration < ITERS - 1
        if not sent:
            kept = call(copy_kernel, "kept", [flat(nx)], [mismatch, inner[0]], specs=[VMEM, pl.BlockSpec(memory_space=pl.ANY)])[0]
        sums, descent, *edges = call(
            functools.partial(descent_kernel, nx, devices, sent),
            "descent",
            [((devices, LANES), f32)] + ([flat(nx), flat(h), flat(h)] if sent else [tiles(nx)]),
            [lam, prior, start, squares] + ([] if sent else [pltpu.with_memory_space_constraint(kept, pltpu.HBM)]),
            specs=[VMEM] * 4 + ([] if sent else [pl.BlockSpec(memory_space=pltpu.HBM)]),
        )
        sums = lax.all_to_all(sums, BOTH, 0, 0, tiled=True)
        if sent:
            moved = [descent, shift(edges[1], "space", 1), shift(edges[0], "space", -1)]
            d_after = shift(descent, "seg", -1)
    new = call(functools.partial(final_kernel, nx), "final", [flat(nx)], [start, descent, sums])[0]

    def placed(block):
        return jnp.transpose(block.reshape(points, nx, LANES), (1, 0, 2))[None]

    return (placed(new), placed(kept))


def solution(mesh):
    placed = (P("seg", "space", None, None), P("space", None, None), P())
    return jax.shard_map(
        per_device,
        mesh=mesh,
        in_specs=placed,
        out_specs=(P("seg", "space", None, None), P("seg", "space", None, None)),
        check_vma=False,
    )
```

```python
import functools

import jax
import jax.numpy as jnp
from jax import lax
from jax.experimental import pallas as pl
from jax.experimental.pallas import tpu as pltpu
from jax.sharding import PartitionSpec as P

STEPS = 4
ITERS = 2
ADVECT = 0.15
SPREAD = 0.2
PUSHED = 0.25
EPSILON = 1e-06
BOTH = ("seg", "space")
VMEM = pl.BlockSpec(memory_space=pltpu.VMEM)
LANES = 128
PARTS = 4


def padded(count, step):
    return -(-count // step) * step


def load(ref, i, planes):
    points = ref.shape[0] // planes
    plane = ref[pl.ds(i, points, stride=planes), :]
    return jnp.concatenate([plane, jnp.zeros((padded(points, 8) - points, LANES), jnp.float32)], 0)


def store(ref, i, planes, plane):
    points = ref.shape[0] // planes
    ref[pl.ds(i, points, stride=planes), :] = plane[:points]


WORK = {"forward": 4e9, "inverse": 1e9}


def call(kernel, name, outs, operands, scratch=(), specs=None, fast=False):
    return pl.pallas_call(
        kernel,
        name=name,
        out_shape=[jax.ShapeDtypeStruct(shape, dtype) for shape, dtype in outs],
        in_specs=specs or [VMEM] * len(operands),
        out_specs=[VMEM] * len(outs),
        scratch_shapes=list(scratch),
        cost_estimate=pl.CostEstimate(flops=int(WORK[name]), transcendentals=0, bytes_accessed=1 << 20) if name in WORK and not fast else None,
        compiler_params=pltpu.CompilerParams(vmem_limit_bytes=32 * 1024 * 1024),
    )(*operands)


def inverse_kernel(points, rows, k_ref, forward_ref, backward_ref, square):
    row = lax.broadcasted_iota(jnp.int32, (LANES, LANES), 0)
    lane = lax.broadcasted_iota(jnp.int32, (LANES, LANES), 1)
    square[0:1, :] = jnp.zeros((1, LANES), jnp.float32)
    square[0:1, :points] = k_ref[...]
    k = jnp.sum(jnp.where(row == lane, square[0:1, :], 0.0), axis=1, keepdims=True)
    k = jnp.broadcast_to(k, (LANES, LANES))
    zero = jnp.zeros_like(k)
    a = jnp.where((row >= 1) & (row < points), -k, zero)
    c = jnp.where(row < points - 1, -k, zero)
    b = jnp.where(row < points, 1.0 + 2.0 * k, 1.0)
    d = jnp.where((row == lane) & (row < points), 1.0, 0.0)
    step = 1
    while step < points:
        up = lambda v: pltpu.roll(v, step, 0)
        down = lambda v: pltpu.roll(v, LANES - step, 0)
        alpha = -a / up(b)
        gamma = -c / down(b)
        b = b + alpha * up(c) + gamma * down(a)
        d = d + alpha * up(d) + gamma * down(d)
        a, c = alpha * up(a), gamma * down(c)
        step *= 2
    inverse = d / b
    square[...] = inverse
    stride = padded(points, 16)
    for ref, matrix in ((forward_ref, SPREAD * inverse), (backward_ref, square[...].T)):
        head = matrix.astype(jnp.bfloat16).astype(jnp.float32)
        tail = (matrix - head).astype(jnp.bfloat16).astype(jnp.float32)
        tail = pltpu.roll(tail, stride, 1)
        left = jnp.where(lane >= stride, tail, head)
        right = jnp.where(lane < stride + points - LANES, tail, pltpu.roll(head, 2 * stride - LANES, 1))
        ref[:, :LANES] = left[:rows].astype(jnp.bfloat16)
        ref[:, LANES:] = right[: rows, : 3 * stride - LANES].astype(jnp.bfloat16)


def product(matrix, planes):
    columns = []
    for plane in planes:
        rows = plane.shape[0]
        fill = jnp.zeros((padded(rows, 16) - rows, LANES), jnp.float32)
        plane = jnp.concatenate([plane, fill], 0) if fill.shape[0] else plane
        head = plane.astype(jnp.bfloat16)
        tail = (plane - head.astype(jnp.float32)).astype(jnp.bfloat16)
        columns.append(jnp.concatenate([head, head, tail], 0))
    right = jnp.concatenate(columns, 1) if len(columns) > 1 else columns[0]
    out = jnp.dot(matrix, right, preferred_element_type=jnp.float32)
    return [out[:, i * LANES : (i + 1) * LANES] for i in range(len(planes))]


def neighbours(plane):
    return pltpu.roll(plane, 1, 1) + pltpu.roll(plane, LANES - 1, 1)


def step_size(sums):
    total = jnp.sum(sums, axis=0, keepdims=True)
    lane = lax.broadcasted_iota(jnp.int32, total.shape, 1)
    squares = jnp.sum(jnp.where(lane < LANES // 2, 0.0, total), axis=1, keepdims=True)
    residual = jnp.sum(jnp.where(lane < LANES // 2, total, 0.0), axis=1, keepdims=True)
    return 0.5 * residual / (squares + EPSILON)


def parts(ref):
    size = padded(-(-ref.shape[0] // PARTS), 8)
    return [pl.ds(at, min(size, ref.shape[0] - at)) for at in range(0, ref.shape[0], size)]


def pack_kernel(nx, states_hbm, forcing_hbm, to_left, to_right, states, forcing, sems):
    h = STEPS
    copies = [
        [pltpu.make_async_copy(source.at[rows], target.at[rows], sems.at[k, j]) for j, rows in enumerate(parts(source))]
        for k, (source, target) in enumerate(((states_hbm, states), (forcing_hbm, forcing)))
    ]
    for copy in copies[0] + copies[1]:
        copy.start()
    for copy in copies[0]:
        copy.wait()
    for i in range(h):
        store(to_left, i, 2 * h - 1, load(states, i, nx))
        store(to_right, i, 2 * h - 1, load(states, nx - h + i, nx))
    for copy in copies[1]:
        copy.wait()
    for i in range(h - 1):
        store(to_left, h + i, 2 * h - 1, load(forcing, i, nx))
        store(to_right, h + i, 2 * h - 1, load(forcing, nx - h + 1 + i, nx))


def copy_kernel(given, order, out):
    out[...] = given[...]


def wall_profile(points, rows):
    row = lax.broadcasted_iota(jnp.int32, (rows, LANES), 0).astype(jnp.float32)
    return row * (2.0 / (points - 1)) - 1.0


def halve(total):
    row = jnp.sum(total, axis=0, keepdims=True)
    return row + pltpu.roll(row, LANES // 2, 1)


def halo_widths(updated):
    return (7, 6, 5, 4, 0) if updated else (4, 3, 2, 1, 0)


def forward_kernel(nx, updated, *refs):
    h = STEPS
    m = 2 * h - 1
    refs = list(refs)
    matrix_ref, states, forcing, left, right = refs[:5]
    del refs[:5]
    widths = halo_widths(updated)
    wide, reach = widths[0], widths[1]
    if updated:
        descent, d_left, d_right, sums, after, d_after = refs[:6]
        del refs[:6]
        tau = step_size(sums[...])
    ending_ref, start_ref, first_ref, second_ref, third_ref, low_ref, high_ref = refs[:7]
    u0, q = refs[-2:]
    points = states.shape[0] // nx
    rows = padded(points, 8)
    scale = PUSHED / SPREAD
    more = wide - h
    parts = wide + 2 * more
    for j in range(wide):
        if j < h:
            before, ahead = load(left, h - 1 - j, m), load(right, j, m)
        else:
            before, ahead = load(d_left, wide + wide - 1 - j, parts), load(d_right, wide + j - h, parts)
        if updated:
            before = before - tau * load(d_left, wide - 1 - j, parts)
            ahead = ahead - tau * load(d_right, j, parts)
        u0[wide - 1 - j] = before
        u0[wide + nx + j] = ahead
        if j == 0:
            start_ref[0] = before
            start_ref[nx + 1] = ahead
    for i in range(nx):
        here = load(states, i, nx)
        if updated:
            here = here - tau * load(descent, i, nx)
        u0[wide + i] = here
        start_ref[1 + i] = here
    for j in range(reach):
        if j < h - 1:
            before, ahead = load(left, m - 1 - j, m), load(right, h + j, m)
        else:
            before = load(d_left, parts - 1 - (j - h + 1), parts)
            ahead = load(d_right, wide + more + j - h + 1, parts)
        q[reach - 1 - j] = scale * before
        q[reach + nx + j] = scale * ahead
    for i in range(nx):
        q[reach + i] = scale * load(forcing, i, nx)
    base = wall_profile(points, rows)
    matrix = matrix_ref[...]
    fields = [u0, first_ref, second_ref, third_ref, None]
    for t in range(h):
        source, target = fields[t], fields[t + 1]
        count = nx + 2 * widths[t + 1]
        inset = widths[t] - widths[t + 1]
        window = [source[inset - 1], source[inset]]
        pending = []
        for i in range(count):
            window = window[-2:] + [source[inset + i + 1]]
            before, here, ahead = window
            force = q[i + reach - widths[t + 1]]
            pending.append(
                3.0 * here + neighbours(here) + force - (base + here) * (ahead - before) * (0.5 * ADVECT / SPREAD)
            )
            if len(pending) == 2 or i == count - 1:
                for j, plane in enumerate(product(matrix, pending)):
                    at = i - len(pending) + 1 + j
                    if target is not None:
                        target[at] = plane
                    else:
                        store(ending_ref, at, nx, plane)
                pending = []
    if updated:
        mismatch_ref, squares_ref = refs[7:9]
        total = None
        for i in range(nx):
            value = load(ending_ref, i, nx) - (load(after, i, nx) - tau * load(d_after, i, nx))
            store(mismatch_ref, i, nx, value)
            if i < h:
                store(low_ref, i, h, value)
            if i >= nx - h:
                store(high_ref, i - (nx - h), h, value)
            total = value * value if total is None else total + value * value
        squares_ref[...] = halve(total)
    else:
        for i in range(h - 1):
            store(low_ref, i, h, third_ref[1 + 1 + i])
            store(high_ref, i, h, third_ref[1 + nx - h + i])
        store(low_ref, h - 1, h, second_ref[2 + 2])
        store(high_ref, h - 1, h, second_ref[2 + nx - 3])


def mismatch_kernel(nx, ending, after, mismatch_ref, low_ref, high_ref, squares_ref):
    h = STEPS
    total = None
    for i in range(nx):
        value = load(ending, i, nx) - load(after, i, nx)
        store(mismatch_ref, i, nx, value)
        if i < h:
            store(low_ref, i, h, value)
        if i >= nx - h:
            store(high_ref, i - (nx - h), h, value)
        total = value * value if total is None else total + value * value
    squares_ref[...] = halve(total)


def adjoint_value(before, here, ahead):
    (u0, _, f0), (_, m1, _), (u2, _, f2) = before, here, ahead
    return SPREAD * (3.0 * m1 + neighbours(m1)) + (0.5 * ADVECT) * ((f2 - f0) - m1 * (u2 - u0))


def own_field(fields, widths, t, i):
    return fields[t][i + (widths[t] if t else 1)]


def inner_range(nx, t):
    low = STEPS - 1 - t
    return low, nx - low, sum(nx - 2 * j for j in range(low))


def adjoint_inner_kernel(nx, widths, matrix_ref, start, first, second, third, mismatch, mu_ref, flux_ref, a, b):
    h = STEPS
    points = mismatch.shape[0] // nx
    base = wall_profile(points, padded(points, 8))
    matrix = matrix_ref[...]
    for t in reversed(range(h)):
        source, target = (a, b) if t % 2 == 0 else (b, a)
        low, high, at = inner_range(nx, t)
        window = []
        for begin in range(low, high, 2):
            group = list(range(begin, min(begin + 2, high)))
            lams = [load(mismatch, i, nx) if t == h - 1 else source[i] for i in group]
            for i, mu in zip(group, product(matrix, lams)):
                u = own_field((start, first, second, third), widths, t, i)
                flux = (base + u) * mu
                mu_ref[at + i - low] = mu
                flux_ref[at + i - low] = flux
                window = window[-2:] + [(u, mu, flux)]
                if len(window) == 3 and t > 0:
                    target[i - 1] = adjoint_value(*window)


def adjoint_outer_kernel(nx, widths, matrix_ref, start, first, second, third, mu_ref, flux_ref, *refs):
    h = STEPS
    *sides, lam_ref, lams, mus, fluxes = refs
    points = sides[0].shape[0] // h
    left, right = sides[-2:]
    base = wall_profile(points, padded(points, 8))
    matrix = matrix_ref[...]

    def field(t, i):
        if len(sides) > 2:
            left_fields, right_fields = sides[:2]
            if t == 2 and i == -3:
                return load(left_fields, h - 1, h)
            if t == 2 and i == nx + 2:
                return load(right_fields, h - 1, h)
            if t == 3 and i < -1:
                return load(left_fields, i + h, h)
            if t == 3 and i > nx:
                return load(right_fields, i - nx - 1, h)
        return own_field((start, first, second, third), widths, t, i)

    for t in reversed(range(h)):
        low, high, at = inner_range(nx, t)
        planes = list(range(low - h, low)) + list(range(high, high + h))
        for begin in range(0, 2 * h, 2):
            group = planes[begin : begin + 2]
            if t < h - 1:
                given = [lams[begin + j] for j in range(2)]
            elif begin < h:
                given = [load(left, h + i, h) for i in group]
            else:
                given = [load(right, i - nx, h) for i in group]
            for j, mu in enumerate(product(matrix, given)):
                mus[begin + j] = mu
                fluxes[begin + j] = (base + field(t, group[j])) * mu

        def known(i, t=t, planes=planes, low=low, at=at):
            if i in planes:
                j = planes.index(i)
                return field(t, i), mus[j], fluxes[j]
            return field(t, i), mu_ref[at + i - low], flux_ref[at + i - low]

        for j, i in enumerate(list(range(low - h + 1, low + 1)) + list(range(high - 1, high + h - 1))):
            value = adjoint_value(known(i - 1), known(i), known(i + 1))
            if t == 0:
                lam_ref[i] = value
            else:
                lams[j] = value


def descent_kernel(nx, devices, sent, lam, prior, start, squares, *refs):
    h = STEPS
    states, forcing = refs[:2] if sent else (None, None)
    sums_ref, descent_ref, *edges = refs[2:] if sent else refs[1:]
    wide = halo_widths(True)[0]
    more = wide - h
    parts = wide + 2 * more
    total = None
    for i in range(nx):
        value = lam[i] - (load(prior, i, nx) - start[i + 1])
        if sent:
            store(descent_ref, i, nx, value)
            if i < wide:
                store(edges[0], i, parts, value)
            if i >= nx - wide:
                store(edges[1], i - (nx - wide), parts, value)
        else:
            descent_ref[i] = value
        total = value * value if total is None else total + value * value
    for j in range(more if sent else 0):
        store(edges[0], wide + j, parts, load(states, h + j, nx))
        store(edges[1], wide + j, parts, load(states, nx - wide + j, nx))
        store(edges[0], wide + more + j, parts, load(forcing, h - 1 + j, nx))
        store(edges[1], wide + more + j, parts, load(forcing, nx - wide + 1 + j, nx))
    lane = lax.broadcasted_iota(jnp.int32, (1, LANES), 1)
    sums_ref[...] = jnp.broadcast_to(jnp.where(lane < LANES // 2, squares[...], halve(total)), (devices, LANES))


def final_kernel(nx, start, descent, sums, out_ref):
    tau = step_size(sums[...])
    for i in range(nx):
        store(out_ref, i, nx, start[i + 1] - tau * descent[i])


def shift(block, axis, distance):
    devices = lax.axis_size(axis)
    return lax.ppermute(block, axis, [((i - distance) % devices, i) for i in range(devices)])


def per_device(states, forcing, wall_viscosity):
    nx, points, _ = forcing.shape
    rows = padded(points, 8)
    depth = 3 * padded(points, 16)
    devices = lax.axis_size("seg") * lax.axis_size("space")
    h = STEPS
    f32, bf16 = jnp.float32, jnp.bfloat16

    def flat(planes):
        return ((planes * points, LANES), f32)

    def tiles(planes):
        return ((planes, rows, LANES), f32)

    states = jnp.transpose(states[0], (1, 0, 2)).reshape(nx * points, LANES)
    forcing = jnp.transpose(forcing, (1, 0, 2)).reshape(nx * points, LANES)
    to_left, to_right, states, forcing = call(
        functools.partial(pack_kernel, nx),
        "pack",
        [flat(2 * h - 1)] * 2 + [flat(nx)] * 2,
        [pltpu.with_memory_space_constraint(v, pltpu.HBM) for v in (states, forcing)],
        [pltpu.SemaphoreType.DMA((2, PARTS))],
        [pl.BlockSpec(memory_space=pltpu.HBM)] * 2,
    )
    left = shift(to_right, "space", 1)
    right = shift(to_left, "space", -1)
    after = shift(states, "seg", -1)
    forward, backward = call(
        functools.partial(inverse_kernel, points, rows),
        "inverse",
        [((rows, depth), bf16)] * 2,
        [wall_viscosity.reshape(1, points)],
        [pltpu.VMEM((LANES, LANES), f32)],
    )
    moved = d_after = sums = None
    for iteration in range(ITERS):
        updated = iteration > 0
        widths = halo_widths(updated)
        ending, start, first, second, third, low, high, *rest = call(
            functools.partial(forward_kernel, nx, updated),
            "forward",
            [flat(nx), tiles(nx + 2)] + [tiles(nx + 2 * width) for width in widths[1:-1]] + [flat(h)] * 2
            + ([flat(nx), ((1, LANES), f32)] if updated else []),
            [forward, states, forcing, left, right] + (moved + [sums, after, d_after] if updated else []),
            [pltpu.VMEM((nx + 2 * width, rows, LANES), f32) for width in widths[:2]],
            fast=updated,
        )
        prior = shift(ending, "seg", 1)
        sides = [] if updated else [shift(high, "space", 1), shift(low, "space", -1)]
        if updated:
            mismatch, squares = rest
        else:
            mismatch, low, high, squares = call(
                functools.partial(mismatch_kernel, nx),
                "mismatch",
                [flat(nx), flat(h), flat(h), ((1, LANES), f32)],
                [ending, after],
            )
        sides += [shift(high, "space", 1), shift(low, "space", -1)]
        fields = [start, first, second, third]
        planes = sum(nx - 2 * j for j in range(h))
        inner = call(
            functools.partial(adjoint_inner_kernel, nx, widths),
            "adjoint_inner",
            [tiles(planes)] * 2,
            [backward, *fields, mismatch],
            [pltpu.VMEM((nx, rows, LANES), f32)] * 2,
        )
        lam = call(
            functools.partial(adjoint_outer_kernel, nx, widths),
            "adjoint_outer",
            [tiles(nx)],
            [backward, *fields, *inner, *sides],
            [pltpu.VMEM((2 * h, rows, LANES), f32)] * 3,
        )[0]
        sent = iteration < ITERS - 1
        if not sent:
            kept = call(copy_kernel, "kept", [flat(nx)], [mismatch, inner[0]], specs=[VMEM, pl.BlockSpec(memory_space=pl.ANY)])[0]
        wide = halo_widths(True)[0]
        side = flat(wide + 2 * (wide - h))
        sums, descent, *edges = call(
            functools.partial(descent_kernel, nx, devices, sent),
            "descent",
            [((devices, LANES), f32)] + ([flat(nx), side, side] if sent else [tiles(nx)]),
            [lam, prior, start, squares]
            + ([states, forcing] if sent else [pltpu.with_memory_space_constraint(kept, pltpu.HBM)]),
            specs=[VMEM] * 4 + ([VMEM] * 2 if sent else [pl.BlockSpec(memory_space=pltpu.HBM)]),
        )
        sums = lax.all_to_all(sums, BOTH, 0, 0, tiled=True)
        if sent:
            moved = [descent, shift(edges[1], "space", 1), shift(edges[0], "space", -1)]
            d_after = shift(descent, "seg", -1)
    new = call(functools.partial(final_kernel, nx), "final", [flat(nx)], [start, descent, sums])[0]

    def placed(block):
        return jnp.transpose(block.reshape(points, nx, LANES), (1, 0, 2))[None]

    return (placed(new), placed(kept))


def solution(mesh):
    placed = (P("seg", "space", None, None), P("space", None, None), P())
    return jax.shard_map(
        per_device,
        mesh=mesh,
        in_specs=placed,
        out_specs=(P("seg", "space", None, None), P("seg", "space", None, None)),
        check_vma=False,
    )
```

```python
import functools

import jax
import jax.numpy as jnp
from jax import lax
from jax.experimental import pallas as pl
from jax.experimental.pallas import tpu as pltpu
from jax.sharding import PartitionSpec as P

STEPS = 4
ITERS = 2
ADVECT = 0.15
SPREAD = 0.2
PUSHED = 0.25
EPSILON = 1e-06
BOTH = ("seg", "space")
VMEM = pl.BlockSpec(memory_space=pltpu.VMEM)
LANES = 128
PARTS = 4


def padded(count, step):
    return -(-count // step) * step


def load(ref, i, planes):
    points = ref.shape[0] // planes
    plane = ref[pl.ds(i, points, stride=planes), :]
    return jnp.concatenate([plane, jnp.zeros((padded(points, 8) - points, LANES), jnp.float32)], 0)


def store(ref, i, planes, plane):
    points = ref.shape[0] // planes
    ref[pl.ds(i, points, stride=planes), :] = plane[:points]


WORK = {"forward": 4e9, "inverse": 1e9}


def call(kernel, name, outs, operands, scratch=(), specs=None, fast=False):
    return pl.pallas_call(
        kernel,
        name=name,
        out_shape=[jax.ShapeDtypeStruct(shape, dtype) for shape, dtype in outs],
        in_specs=specs or [VMEM] * len(operands),
        out_specs=[VMEM] * len(outs),
        scratch_shapes=list(scratch),
        cost_estimate=pl.CostEstimate(flops=int(WORK[name]), transcendentals=0, bytes_accessed=1 << 20) if name in WORK and not fast else None,
        compiler_params=pltpu.CompilerParams(vmem_limit_bytes=32 * 1024 * 1024),
    )(*operands)


def inverse_kernel(points, rows, k_ref, forward_ref, backward_ref, square):
    row = lax.broadcasted_iota(jnp.int32, (LANES, LANES), 0)
    lane = lax.broadcasted_iota(jnp.int32, (LANES, LANES), 1)
    square[0:1, :] = jnp.zeros((1, LANES), jnp.float32)
    square[0:1, :points] = k_ref[...]
    k = jnp.sum(jnp.where(row == lane, square[0:1, :], 0.0), axis=1, keepdims=True)
    k = jnp.broadcast_to(k, (LANES, LANES))
    zero = jnp.zeros_like(k)
    a = jnp.where((row >= 1) & (row < points), -k, zero)
    c = jnp.where(row < points - 1, -k, zero)
    b = jnp.where(row < points, 1.0 + 2.0 * k, 1.0)
    d = jnp.where((row == lane) & (row < points), 1.0, 0.0)
    step = 1
    while step < points:
        up = lambda v: pltpu.roll(v, step, 0)
        down = lambda v: pltpu.roll(v, LANES - step, 0)
        alpha = -a / up(b)
        gamma = -c / down(b)
        b = b + alpha * up(c) + gamma * down(a)
        d = d + alpha * up(d) + gamma * down(d)
        a, c = alpha * up(a), gamma * down(c)
        step *= 2
    inverse = d / b
    square[...] = inverse
    stride = padded(points, 16)
    for ref, matrix in ((forward_ref, SPREAD * inverse), (backward_ref, square[...].T)):
        head = matrix.astype(jnp.bfloat16).astype(jnp.float32)
        tail = (matrix - head).astype(jnp.bfloat16).astype(jnp.float32)
        tail = pltpu.roll(tail, stride, 1)
        left = jnp.where(lane >= stride, tail, head)
        right = jnp.where(lane < stride + points - LANES, tail, pltpu.roll(head, 2 * stride - LANES, 1))
        ref[:, :LANES] = left[:rows].astype(jnp.bfloat16)
        ref[:, LANES:] = right[: rows, : 3 * stride - LANES].astype(jnp.bfloat16)


def product(matrix, planes):
    columns = []
    for plane in planes:
        rows = plane.shape[0]
        fill = jnp.zeros((padded(rows, 16) - rows, LANES), jnp.float32)
        plane = jnp.concatenate([plane, fill], 0) if fill.shape[0] else plane
        head = plane.astype(jnp.bfloat16)
        tail = (plane - head.astype(jnp.float32)).astype(jnp.bfloat16)
        columns.append(jnp.concatenate([head, head, tail], 0))
    right = jnp.concatenate(columns, 1) if len(columns) > 1 else columns[0]
    out = jnp.dot(matrix, right, preferred_element_type=jnp.float32)
    return [out[:, i * LANES : (i + 1) * LANES] for i in range(len(planes))]


def neighbours(plane):
    return pltpu.roll(plane, 1, 1) + pltpu.roll(plane, LANES - 1, 1)


def step_size(sums):
    total = jnp.sum(sums, axis=0, keepdims=True)
    lane = lax.broadcasted_iota(jnp.int32, total.shape, 1)
    squares = jnp.sum(jnp.where(lane < LANES // 2, 0.0, total), axis=1, keepdims=True)
    residual = jnp.sum(jnp.where(lane < LANES // 2, total, 0.0), axis=1, keepdims=True)
    return 0.5 * residual / (squares + EPSILON)


def parts(ref):
    size = padded(-(-ref.shape[0] // PARTS), 8)
    return [pl.ds(at, min(size, ref.shape[0] - at)) for at in range(0, ref.shape[0], size)]


def pack_kernel(nx, states_hbm, forcing_hbm, to_left, to_right, states, forcing, sems):
    h = STEPS
    copies = [
        [pltpu.make_async_copy(source.at[rows], target.at[rows], sems.at[k, j]) for j, rows in enumerate(parts(source))]
        for k, (source, target) in enumerate(((states_hbm, states), (forcing_hbm, forcing)))
    ]
    for copy in copies[0] + copies[1]:
        copy.start()
    for copy in copies[0]:
        copy.wait()
    for i in range(h):
        store(to_left, i, 2 * h - 1, load(states, i, nx))
        store(to_right, i, 2 * h - 1, load(states, nx - h + i, nx))
    for copy in copies[1]:
        copy.wait()
    for i in range(h - 1):
        store(to_left, h + i, 2 * h - 1, load(forcing, i, nx))
        store(to_right, h + i, 2 * h - 1, load(forcing, nx - h + 1 + i, nx))


def copy_kernel(given, order, out):
    out[...] = given[...]


def wall_profile(points, rows):
    row = lax.broadcasted_iota(jnp.int32, (rows, LANES), 0).astype(jnp.float32)
    return row * (2.0 / (points - 1)) - 1.0


def halve(total):
    row = jnp.sum(total, axis=0, keepdims=True)
    return row + pltpu.roll(row, LANES // 2, 1)


WIDTHS = (4, 3, 2, 1, 0)
WIDE = 7


def forward_kernel(nx, updated, *refs):
    h = STEPS
    m = 2 * h - 1
    refs = list(refs)
    matrix_ref, states, forcing, left, right = refs[:5]
    del refs[:5]
    reach = WIDTHS[1]
    if updated:
        descent, d_left, d_right, sums = refs[:4]
        del refs[:4]
        tau = step_size(sums[...])
    ending_ref, start_ref, first_ref, second_ref, third_ref = refs[:5]
    u0, q = refs[-2:]
    points = states.shape[0] // nx
    rows = padded(points, 8)
    scale = PUSHED / SPREAD
    parts = WIDE + 2 * (WIDE - h)
    for j in range(h):
        before, ahead = load(left, h - 1 - j, m), load(right, j, m)
        if updated:
            before = before - tau * load(d_left, WIDE - 1 - j, parts)
            ahead = ahead - tau * load(d_right, j, parts)
        u0[h - 1 - j] = before
        u0[h + nx + j] = ahead
        if j == 0:
            start_ref[0] = before
            start_ref[nx + 1] = ahead
    for i in range(nx):
        here = load(states, i, nx)
        if updated:
            here = here - tau * load(descent, i, nx)
        u0[h + i] = here
        start_ref[1 + i] = here
    for j in range(reach):
        q[reach - 1 - j] = scale * load(left, m - 1 - j, m)
        q[reach + nx + j] = scale * load(right, h + j, m)
    for i in range(nx):
        q[reach + i] = scale * load(forcing, i, nx)
    base = wall_profile(points, rows)
    matrix = matrix_ref[...]
    fields = [u0, first_ref, second_ref, third_ref, None]
    for t in range(h):
        source, target = fields[t], fields[t + 1]
        count = nx + 2 * WIDTHS[t + 1]
        inset = WIDTHS[t] - WIDTHS[t + 1]
        window = [source[inset - 1], source[inset]]
        pending = []
        for i in range(count):
            window = window[-2:] + [source[inset + i + 1]]
            before, here, ahead = window
            force = q[i + reach - WIDTHS[t + 1]]
            pending.append(
                3.0 * here + neighbours(here) + force - (base + here) * (ahead - before) * (0.5 * ADVECT / SPREAD)
            )
            if len(pending) == 2 or i == count - 1:
                for j, plane in enumerate(product(matrix, pending)):
                    at = i - len(pending) + 1 + j
                    if target is not None:
                        target[at] = plane
                    else:
                        store(ending_ref, at, nx, plane)
                pending = []
    if not updated:
        low_ref, high_ref = refs[5:7]
        for i in range(h - 1):
            store(low_ref, i, h, third_ref[1 + 1 + i])
            store(high_ref, i, h, third_ref[1 + nx - h + i])
        store(low_ref, h - 1, h, second_ref[2 + 2])
        store(high_ref, h - 1, h, second_ref[2 + nx - 3])


def wide_kernel(nx, matrix_ref, left, right, d_left, d_right, sums, first, second, left_fields, right_fields):
    h = STEPS
    m = 2 * h - 1
    more = WIDE - h
    parts = WIDE + 2 * more
    points = left.shape[0] // m
    base = wall_profile(points, padded(points, 8))
    matrix = matrix_ref[...]
    tau = step_size(sums[...])
    scale = PUSHED / SPREAD

    def state(side, d):
        if side == 0:
            value = load(left, h - d, m) if d <= h else load(d_left, WIDE + WIDE - d, parts)
            return value - tau * load(d_left, WIDE - d, parts)
        value = load(right, d - 1, m) if d <= h else load(d_right, WIDE + d - 1 - h, parts)
        return value - tau * load(d_right, d - 1, parts)

    def push(side, d):
        if side == 0:
            return scale * (load(left, m - d, m) if d < h else load(d_left, parts - 1 - (d - h), parts))
        return scale * (load(right, h + d - 1, m) if d < h else load(d_right, WIDE + more + d - h, parts))

    u = [{d: state(side, d) for d in range(h - 1, WIDE + 1)} for side in range(2)]
    for t in range(3):
        reach = WIDE - t
        pushed, places = [], []
        for side in range(2):
            sign = 1.0 if side else -1.0
            for d in range(reach - 3, reach):
                here = u[side][d]
                slope = sign * (u[side][d + 1] - u[side][d - 1])
                pushed.append(
                    3.0 * here + neighbours(here) + push(side, d) - (base + here) * slope * (0.5 * ADVECT / SPREAD)
                )
                places.append((side, d))
        out = [{}, {}]
        for k in range(0, len(places), 2):
            for (side, d), plane in zip(places[k : k + 2], product(matrix, pushed[k : k + 2])):
                out[side][d] = plane
        for d in range(reach - 5, reach - 3):
            if t == 0:
                out[0][d], out[1][d] = first[WIDTHS[1] - d], first[WIDTHS[1] + nx - 1 + d]
            elif t == 1:
                out[0][d], out[1][d] = second[WIDTHS[2] - d], second[WIDTHS[2] + nx - 1 + d]
        u = out
        if t == 1:
            store(left_fields, h - 1, h, u[0][3])
            store(right_fields, h - 1, h, u[1][3])
    for d in range(2, h + 1):
        store(left_fields, h - d, h, u[0][d])
        store(right_fields, d - 2, h, u[1][d])


def mismatch_kernel(nx, updated, *refs):
    h = STEPS
    ending, after, *given = refs[:-4]
    mismatch_ref, low_ref, high_ref, squares_ref = refs[-4:]
    if updated:
        tau = step_size(given[1][...])
    total = None
    for i in range(nx):
        value = load(after, i, nx)
        if updated:
            value = value - tau * load(given[0], i, nx)
        value = load(ending, i, nx) - value
        store(mismatch_ref, i, nx, value)
        if i < h:
            store(low_ref, i, h, value)
        if i >= nx - h:
            store(high_ref, i - (nx - h), h, value)
        total = value * value if total is None else total + value * value
    squares_ref[...] = halve(total)


def adjoint_value(before, here, ahead):
    (u0, _, f0), (_, m1, _), (u2, _, f2) = before, here, ahead
    return SPREAD * (3.0 * m1 + neighbours(m1)) + (0.5 * ADVECT) * ((f2 - f0) - m1 * (u2 - u0))


def own_field(fields, t, i):
    return fields[t][i + (WIDTHS[t] if t else 1)]


def inner_range(nx, t):
    low = STEPS - 1 - t
    return low, nx - low, sum(nx - 2 * j for j in range(low))


def adjoint_inner_kernel(nx, matrix_ref, start, first, second, third, mismatch, mu_ref, flux_ref, a, b):
    h = STEPS
    points = mismatch.shape[0] // nx
    base = wall_profile(points, padded(points, 8))
    matrix = matrix_ref[...]
    for t in reversed(range(h)):
        source, target = (a, b) if t % 2 == 0 else (b, a)
        low, high, at = inner_range(nx, t)
        window = []
        for begin in range(low, high, 2):
            group = list(range(begin, min(begin + 2, high)))
            lams = [load(mismatch, i, nx) if t == h - 1 else source[i] for i in group]
            for i, mu in zip(group, product(matrix, lams)):
                u = own_field((start, first, second, third), t, i)
                flux = (base + u) * mu
                mu_ref[at + i - low] = mu
                flux_ref[at + i - low] = flux
                window = window[-2:] + [(u, mu, flux)]
                if len(window) == 3 and t > 0:
                    target[i - 1] = adjoint_value(*window)


def adjoint_outer_kernel(nx, matrix_ref, start, first, second, third, mu_ref, flux_ref, *refs):
    h = STEPS
    *sides, lam_ref, lams, mus, fluxes = refs
    points = sides[0].shape[0] // h
    left_fields, right_fields, left, right = sides
    base = wall_profile(points, padded(points, 8))
    matrix = matrix_ref[...]

    def field(t, i):
        if t == 2 and i == -3:
            return load(left_fields, h - 1, h)
        if t == 2 and i == nx + 2:
            return load(right_fields, h - 1, h)
        if t == 3 and i < -1:
            return load(left_fields, i + h, h)
        if t == 3 and i > nx:
            return load(right_fields, i - nx - 1, h)
        return own_field((start, first, second, third), t, i)

    for t in reversed(range(h)):
        low, high, at = inner_range(nx, t)
        planes = list(range(low - h, low)) + list(range(high, high + h))
        for begin in range(0, 2 * h, 2):
            group = planes[begin : begin + 2]
            if t < h - 1:
                given = [lams[begin + j] for j in range(2)]
            elif begin < h:
                given = [load(left, h + i, h) for i in group]
            else:
                given = [load(right, i - nx, h) for i in group]
            for j, mu in enumerate(product(matrix, given)):
                mus[begin + j] = mu
                fluxes[begin + j] = (base + field(t, group[j])) * mu

        def known(i, t=t, planes=planes, low=low, at=at):
            if i in planes:
                j = planes.index(i)
                return field(t, i), mus[j], fluxes[j]
            return field(t, i), mu_ref[at + i - low], flux_ref[at + i - low]

        for j, i in enumerate(list(range(low - h + 1, low + 1)) + list(range(high - 1, high + h - 1))):
            value = adjoint_value(known(i - 1), known(i), known(i + 1))
            if t == 0:
                lam_ref[i] = value
            else:
                lams[j] = value


def descent_kernel(nx, devices, sent, lam, prior, start, squares, *refs):
    h = STEPS
    states, forcing = refs[:2] if sent else (None, None)
    sums_ref, descent_ref, *edges = refs[2:] if sent else refs[1:]
    wide = WIDE
    more = wide - h
    parts = wide + 2 * more
    total = None
    for i in range(nx):
        value = lam[i] - (load(prior, i, nx) - start[i + 1])
        if sent:
            store(descent_ref, i, nx, value)
            if i < wide:
                store(edges[0], i, parts, value)
            if i >= nx - wide:
                store(edges[1], i - (nx - wide), parts, value)
        else:
            descent_ref[i] = value
        total = value * value if total is None else total + value * value
    for j in range(more if sent else 0):
        store(edges[0], wide + j, parts, load(states, h + j, nx))
        store(edges[1], wide + j, parts, load(states, nx - wide + j, nx))
        store(edges[0], wide + more + j, parts, load(forcing, h - 1 + j, nx))
        store(edges[1], wide + more + j, parts, load(forcing, nx - wide + 1 + j, nx))
    lane = lax.broadcasted_iota(jnp.int32, (1, LANES), 1)
    sums_ref[...] = jnp.broadcast_to(jnp.where(lane < LANES // 2, squares[...], halve(total)), (devices, LANES))


def final_kernel(nx, start, descent, sums, out_ref):
    tau = step_size(sums[...])
    for i in range(nx):
        store(out_ref, i, nx, start[i + 1] - tau * descent[i])


def shift(block, axis, distance):
    devices = lax.axis_size(axis)
    return lax.ppermute(block, axis, [((i - distance) % devices, i) for i in range(devices)])


def per_device(states, forcing, wall_viscosity):
    nx, points, _ = forcing.shape
    rows = padded(points, 8)
    depth = 3 * padded(points, 16)
    devices = lax.axis_size("seg") * lax.axis_size("space")
    h = STEPS
    f32, bf16 = jnp.float32, jnp.bfloat16

    def flat(planes):
        return ((planes * points, LANES), f32)

    def tiles(planes):
        return ((planes, rows, LANES), f32)

    states = jnp.transpose(states[0], (1, 0, 2)).reshape(nx * points, LANES)
    forcing = jnp.transpose(forcing, (1, 0, 2)).reshape(nx * points, LANES)
    to_left, to_right, states, forcing = call(
        functools.partial(pack_kernel, nx),
        "pack",
        [flat(2 * h - 1)] * 2 + [flat(nx)] * 2,
        [pltpu.with_memory_space_constraint(v, pltpu.HBM) for v in (states, forcing)],
        [pltpu.SemaphoreType.DMA((2, PARTS))],
        [pl.BlockSpec(memory_space=pltpu.HBM)] * 2,
    )
    left = shift(to_right, "space", 1)
    right = shift(to_left, "space", -1)
    after = shift(states, "seg", -1)
    forward, backward = call(
        functools.partial(inverse_kernel, points, rows),
        "inverse",
        [((rows, depth), bf16)] * 2,
        [wall_viscosity.reshape(1, points)],
        [pltpu.VMEM((LANES, LANES), f32)],
    )
    moved = d_after = sums = None
    for iteration in range(ITERS):
        updated = iteration > 0
        ending, start, first, second, third, *sides = call(
            functools.partial(forward_kernel, nx, updated),
            "forward",
            [flat(nx), tiles(nx + 2)]
            + [tiles(nx + 2 * width) for width in WIDTHS[1:-1]]
            + ([] if updated else [flat(h)] * 2),
            [forward, states, forcing, left, right] + (moved + [sums] if updated else []),
            [pltpu.VMEM((nx + 2 * width, rows, LANES), f32) for width in WIDTHS[:2]],
            fast=updated,
        )
        prior = shift(ending, "seg", 1)
        if updated:
            sides = call(
                functools.partial(wide_kernel, nx),
                "wide",
                [flat(h)] * 2,
                [forward, left, right, *moved[1:], sums, first, second],
            )
        else:
            sides = [shift(sides[1], "space", 1), shift(sides[0], "space", -1)]
        mismatch, low, high, squares = call(
            functools.partial(mismatch_kernel, nx, updated),
            "mismatch",
            [flat(nx), flat(h), flat(h), ((1, LANES), f32)],
            [ending, after] + ([d_after, sums] if updated else []),
        )
        sides = [*sides, shift(high, "space", 1), shift(low, "space", -1)]
        fields = [start, first, second, third]
        planes = sum(nx - 2 * j for j in range(h))
        inner = call(
            functools.partial(adjoint_inner_kernel, nx),
            "adjoint_inner",
            [tiles(planes)] * 2,
            [backward, *fields, mismatch],
            [pltpu.VMEM((nx, rows, LANES), f32)] * 2,
        )
        lam = call(
            functools.partial(adjoint_outer_kernel, nx),
            "adjoint_outer",
            [tiles(nx)],
            [backward, *fields, *inner, *sides],
            [pltpu.VMEM((2 * h, rows, LANES), f32)] * 3,
        )[0]
        sent = iteration < ITERS - 1
        if not sent:
            kept = call(copy_kernel, "kept", [flat(nx)], [mismatch, inner[0]], specs=[VMEM, pl.BlockSpec(memory_space=pl.ANY)])[0]
        side = flat(WIDE + 2 * (WIDE - h))
        sums, descent, *edges = call(
            functools.partial(descent_kernel, nx, devices, sent),
            "descent",
            [((devices, LANES), f32)] + ([flat(nx), side, side] if sent else [tiles(nx)]),
            [lam, prior, start, squares]
            + ([states, forcing] if sent else [pltpu.with_memory_space_constraint(kept, pltpu.HBM)]),
            specs=[VMEM] * 4 + ([VMEM] * 2 if sent else [pl.BlockSpec(memory_space=pltpu.HBM)]),
        )
        sums = lax.all_to_all(sums, BOTH, 0, 0, tiled=True)
        if sent:
            moved = [descent, shift(edges[1], "space", 1), shift(edges[0], "space", -1)]
            d_after = shift(descent, "seg", -1)
    new = call(functools.partial(final_kernel, nx), "final", [flat(nx)], [start, descent, sums])[0]

    def placed(block):
        return jnp.transpose(block.reshape(points, nx, LANES), (1, 0, 2))[None]

    return (placed(new), placed(kept))


def solution(mesh):
    placed = (P("seg", "space", None, None), P("space", None, None), P())
    return jax.shard_map(
        per_device,
        mesh=mesh,
        in_specs=placed,
        out_specs=(P("seg", "space", None, None), P("seg", "space", None, None)),
        check_vma=False,
    )
```

```python
import functools

import jax
import jax.numpy as jnp
from jax import lax
from jax.experimental import pallas as pl
from jax.experimental.pallas import tpu as pltpu
from jax.sharding import PartitionSpec as P

STEPS = 4
ITERS = 2
ADVECT = 0.15
SPREAD = 0.2
PUSHED = 0.25
EPSILON = 1e-06
BOTH = ("seg", "space")
VMEM = pl.BlockSpec(memory_space=pltpu.VMEM)
LANES = 128
PARTS = 4


def padded(count, step):
    return -(-count // step) * step


def load(ref, i, planes):
    points = ref.shape[0] // planes
    plane = ref[pl.ds(i, points, stride=planes), :]
    return jnp.concatenate([plane, jnp.zeros((padded(points, 8) - points, LANES), jnp.float32)], 0)


def store(ref, i, planes, plane):
    points = ref.shape[0] // planes
    ref[pl.ds(i, points, stride=planes), :] = plane[:points]


WORK = {"forward_outer": 4e9, "inverse": 1e9}


def call(kernel, name, outs, operands, scratch=(), specs=None, fast=False, aliases=None):
    return pl.pallas_call(
        kernel,
        name=name,
        out_shape=[jax.ShapeDtypeStruct(shape, dtype) for shape, dtype in outs],
        in_specs=specs or [VMEM] * len(operands),
        out_specs=[VMEM] * len(outs),
        scratch_shapes=list(scratch),
        input_output_aliases=aliases or {},
        cost_estimate=pl.CostEstimate(flops=int(WORK[name]), transcendentals=0, bytes_accessed=1 << 20) if name in WORK and not fast else None,
        compiler_params=pltpu.CompilerParams(vmem_limit_bytes=32 * 1024 * 1024),
    )(*operands)


def inverse_kernel(points, rows, k_ref, forward_ref, backward_ref, square):
    row = lax.broadcasted_iota(jnp.int32, (LANES, LANES), 0)
    lane = lax.broadcasted_iota(jnp.int32, (LANES, LANES), 1)
    square[0:1, :] = jnp.zeros((1, LANES), jnp.float32)
    square[0:1, :points] = k_ref[...]
    k = jnp.sum(jnp.where(row == lane, square[0:1, :], 0.0), axis=1, keepdims=True)
    k = jnp.broadcast_to(k, (LANES, LANES))
    zero = jnp.zeros_like(k)
    a = jnp.where((row >= 1) & (row < points), -k, zero)
    c = jnp.where(row < points - 1, -k, zero)
    b = jnp.where(row < points, 1.0 + 2.0 * k, 1.0)
    d = jnp.where((row == lane) & (row < points), 1.0, 0.0)
    step = 1
    while step < points:
        up = lambda v: pltpu.roll(v, step, 0)
        down = lambda v: pltpu.roll(v, LANES - step, 0)
        alpha = -a / up(b)
        gamma = -c / down(b)
        b = b + alpha * up(c) + gamma * down(a)
        d = d + alpha * up(d) + gamma * down(d)
        a, c = alpha * up(a), gamma * down(c)
        step *= 2
    inverse = d / b
    square[...] = inverse
    stride = padded(points, 16)
    for ref, matrix in ((forward_ref, SPREAD * inverse), (backward_ref, square[...].T)):
        head = matrix.astype(jnp.bfloat16).astype(jnp.float32)
        tail = (matrix - head).astype(jnp.bfloat16).astype(jnp.float32)
        tail = pltpu.roll(tail, stride, 1)
        left = jnp.where(lane >= stride, tail, head)
        right = jnp.where(lane < stride + points - LANES, tail, pltpu.roll(head, 2 * stride - LANES, 1))
        ref[:, :LANES] = left[:rows].astype(jnp.bfloat16)
        ref[:, LANES:] = right[: rows, : 3 * stride - LANES].astype(jnp.bfloat16)


def product(matrix, planes):
    columns = []
    for plane in planes:
        rows = plane.shape[0]
        fill = jnp.zeros((padded(rows, 16) - rows, LANES), jnp.float32)
        plane = jnp.concatenate([plane, fill], 0) if fill.shape[0] else plane
        head = plane.astype(jnp.bfloat16)
        tail = (plane - head.astype(jnp.float32)).astype(jnp.bfloat16)
        columns.append(jnp.concatenate([head, head, tail], 0))
    right = jnp.concatenate(columns, 1) if len(columns) > 1 else columns[0]
    out = jnp.dot(matrix, right, preferred_element_type=jnp.float32)
    return [out[:, i * LANES : (i + 1) * LANES] for i in range(len(planes))]


def neighbours(plane):
    return pltpu.roll(plane, 1, 1) + pltpu.roll(plane, LANES - 1, 1)


def step_size(sums):
    total = jnp.sum(sums, axis=0, keepdims=True)
    lane = lax.broadcasted_iota(jnp.int32, total.shape, 1)
    squares = jnp.sum(jnp.where(lane < LANES // 2, 0.0, total), axis=1, keepdims=True)
    residual = jnp.sum(jnp.where(lane < LANES // 2, total, 0.0), axis=1, keepdims=True)
    return 0.5 * residual / (squares + EPSILON)


def parts(ref):
    size = padded(-(-ref.shape[0] // PARTS), 8)
    return [pl.ds(at, min(size, ref.shape[0] - at)) for at in range(0, ref.shape[0], size)]


def pack_kernel(nx, states_hbm, forcing_hbm, to_left, to_right, states, forcing, sems):
    h = STEPS
    copies = [
        [pltpu.make_async_copy(source.at[rows], target.at[rows], sems.at[k, j]) for j, rows in enumerate(parts(source))]
        for k, (source, target) in enumerate(((states_hbm, states), (forcing_hbm, forcing)))
    ]
    for copy in copies[0] + copies[1]:
        copy.start()
    for copy in copies[0]:
        copy.wait()
    for i in range(h):
        store(to_left, i, 2 * h - 1, load(states, i, nx))
        store(to_right, i, 2 * h - 1, load(states, nx - h + i, nx))
    for copy in copies[1]:
        copy.wait()
    for i in range(h - 1):
        store(to_left, h + i, 2 * h - 1, load(forcing, i, nx))
        store(to_right, h + i, 2 * h - 1, load(forcing, nx - h + 1 + i, nx))


def copy_kernel(given, order, out):
    out[...] = given[...]


def wall_profile(points, rows):
    row = lax.broadcasted_iota(jnp.int32, (rows, LANES), 0).astype(jnp.float32)
    return row * (2.0 / (points - 1)) - 1.0


def halve(total):
    row = jnp.sum(total, axis=0, keepdims=True)
    return row + pltpu.roll(row, LANES // 2, 1)


WIDTHS = (4, 3, 2, 1, 0)
WIDE = 7


def pushed_plane(base, before, here, ahead, force):
    return 3.0 * here + neighbours(here) + force - (base + here) * (ahead - before) * (0.5 * ADVECT / SPREAD)


def field_plane(nx, u0, start, fields, t, i):
    if t == 0:
        return u0[STEPS + i] if i < 0 else u0[STEPS + i - nx] if i >= nx else start[1 + i]
    return fields[t - 1][WIDTHS[t] + i]


def force_plane(nx, left, right, q_own, i):
    m = 2 * STEPS - 1
    if i < 0:
        return (PUSHED / SPREAD) * load(left, m + i, m)
    if i >= nx:
        return (PUSHED / SPREAD) * load(right, STEPS + i - nx, m)
    return q_own[i]


def forward_kernel(nx, matrix_ref, left, right, q_own, old, descent, d_left, d_right, sums, ending_ref, start, first, second, third, u0):
    h = STEPS
    m = 2 * h - 1
    parts = WIDE + 2 * (WIDE - h)
    points = left.shape[0] // m
    base = wall_profile(points, padded(points, 8))
    matrix = matrix_ref[...]
    tau = step_size(sums[...])
    for j in range(h):
        before = load(left, h - 1 - j, m) - tau * load(d_left, WIDE - 1 - j, parts)
        ahead = load(right, j, m) - tau * load(d_right, j, parts)
        if j == 0:
            start[0] = before
            start[nx + 1] = ahead
        u0[h - 1 - j] = before
        u0[h + j] = ahead
    for i in range(nx):
        start[1 + i] = old[1 + i] - tau * load(descent, i, nx)
    value = functools.partial(field_plane, nx, u0, start, (first, second, third))
    for t in range(h):
        planes = list(range(-WIDTHS[t + 1], nx + WIDTHS[t + 1]))
        for begin in range(0, len(planes), 2):
            group = planes[begin : begin + 2]
            pushed = [
                pushed_plane(base, value(t, i - 1), value(t, i), value(t, i + 1), force_plane(nx, left, right, q_own, i))
                for i in group
            ]
            for i, plane in zip(group, product(matrix, pushed)):
                if t == h - 1:
                    store(ending_ref, i, nx, plane)
                else:
                    (first, second, third)[t][WIDTHS[t + 1] + i] = plane


def forward_inner_kernel(nx, matrix_ref, states, forcing, start_ref, q_ref, first_ref, second_ref, third_ref):
    h = STEPS
    points = states.shape[0] // nx
    base = wall_profile(points, padded(points, 8))
    matrix = matrix_ref[...]
    for i in range(nx):
        start_ref[1 + i] = load(states, i, nx)
        q_ref[i] = (PUSHED / SPREAD) * load(forcing, i, nx)
    fields = ((start_ref, 1), (first_ref, WIDTHS[1]), (second_ref, WIDTHS[2]), (third_ref, WIDTHS[3]))
    for t in range(h - 1):
        (source, a), (target, b) = fields[t], fields[t + 1]
        planes = list(range(t + 1, nx - t - 1))
        for begin in range(0, len(planes), 2):
            group = planes[begin : begin + 2]
            pushed = [
                pushed_plane(base, source[a + i - 1], source[a + i], source[a + i + 1], q_ref[i]) for i in group
            ]
            for i, plane in zip(group, product(matrix, pushed)):
                target[b + i] = plane


def forward_outer_kernel(nx, matrix_ref, left, right, q_own, start_in, first_in, second_in, third_in, ending_ref, start, first, second, third, low_ref, high_ref, u0):
    h = STEPS
    m = 2 * h - 1
    points = left.shape[0] // m
    base = wall_profile(points, padded(points, 8))
    matrix = matrix_ref[...]
    for j in range(h):
        before, ahead = load(left, h - 1 - j, m), load(right, j, m)
        if j == 0:
            start[0] = before
            start[nx + 1] = ahead
        u0[h - 1 - j] = before
        u0[h + j] = ahead

    value = functools.partial(field_plane, nx, u0, start, (first, second, third))
    for t in range(h):
        planes = list(range(t + 1 - h, t + 1)) + list(range(nx - 1 - t, nx - 1 - t + h))
        for begin in range(0, 2 * h, 2):
            group = planes[begin : begin + 2]
            pushed = [
                pushed_plane(base, value(t, i - 1), value(t, i), value(t, i + 1), force_plane(nx, left, right, q_own, i))
                for i in group
            ]
            for i, plane in zip(group, product(matrix, pushed)):
                if t == h - 1:
                    store(ending_ref, i, nx, plane)
                else:
                    (first, second, third)[t][WIDTHS[t + 1] + i] = plane
    for i in range(h - 1):
        store(low_ref, i, h, third[WIDTHS[3] + 1 + i])
        store(high_ref, i, h, third[WIDTHS[3] + nx - h + i])
    store(low_ref, h - 1, h, second[WIDTHS[2] + 2])
    store(high_ref, h - 1, h, second[WIDTHS[2] + nx - 3])


def wide_kernel(nx, matrix_ref, left, right, d_left, d_right, sums, first, second, left_fields, right_fields):
    h = STEPS
    m = 2 * h - 1
    more = WIDE - h
    parts = WIDE + 2 * more
    points = left.shape[0] // m
    base = wall_profile(points, padded(points, 8))
    matrix = matrix_ref[...]
    tau = step_size(sums[...])
    scale = PUSHED / SPREAD

    def state(side, d):
        if side == 0:
            value = load(left, h - d, m) if d <= h else load(d_left, WIDE + WIDE - d, parts)
            return value - tau * load(d_left, WIDE - d, parts)
        value = load(right, d - 1, m) if d <= h else load(d_right, WIDE + d - 1 - h, parts)
        return value - tau * load(d_right, d - 1, parts)

    def push(side, d):
        if side == 0:
            return scale * (load(left, m - d, m) if d < h else load(d_left, parts - 1 - (d - h), parts))
        return scale * (load(right, h + d - 1, m) if d < h else load(d_right, WIDE + more + d - h, parts))

    u = [{d: state(side, d) for d in range(h - 1, WIDE + 1)} for side in range(2)]
    for t in range(3):
        reach = WIDE - t
        pushed, places = [], []
        for side in range(2):
            sign = 1.0 if side else -1.0
            for d in range(reach - 3, reach):
                here = u[side][d]
                slope = sign * (u[side][d + 1] - u[side][d - 1])
                pushed.append(
                    3.0 * here + neighbours(here) + push(side, d) - (base + here) * slope * (0.5 * ADVECT / SPREAD)
                )
                places.append((side, d))
        out = [{}, {}]
        for k in range(0, len(places), 2):
            for (side, d), plane in zip(places[k : k + 2], product(matrix, pushed[k : k + 2])):
                out[side][d] = plane
        for d in range(reach - 5, reach - 3):
            if t == 0:
                out[0][d], out[1][d] = first[WIDTHS[1] - d], first[WIDTHS[1] + nx - 1 + d]
            elif t == 1:
                out[0][d], out[1][d] = second[WIDTHS[2] - d], second[WIDTHS[2] + nx - 1 + d]
        u = out
        if t == 1:
            store(left_fields, h - 1, h, u[0][3])
            store(right_fields, h - 1, h, u[1][3])
    for d in range(2, h + 1):
        store(left_fields, h - d, h, u[0][d])
        store(right_fields, d - 2, h, u[1][d])


def mismatch_kernel(nx, updated, *refs):
    h = STEPS
    ending, after, *given = refs[:-4]
    mismatch_ref, low_ref, high_ref, squares_ref = refs[-4:]
    if updated:
        tau = step_size(given[1][...])
    total = None
    for i in range(nx):
        value = load(after, i, nx)
        if updated:
            value = value - tau * load(given[0], i, nx)
        value = load(ending, i, nx) - value
        store(mismatch_ref, i, nx, value)
        if i < h:
            store(low_ref, i, h, value)
        if i >= nx - h:
            store(high_ref, i - (nx - h), h, value)
        total = value * value if total is None else total + value * value
    squares_ref[...] = halve(total)


def adjoint_value(before, here, ahead):
    (u0, _, f0), (_, m1, _), (u2, _, f2) = before, here, ahead
    return SPREAD * (3.0 * m1 + neighbours(m1)) + (0.5 * ADVECT) * ((f2 - f0) - m1 * (u2 - u0))


def own_field(fields, t, i):
    return fields[t][i + (WIDTHS[t] if t else 1)]


def inner_range(nx, t):
    low = STEPS - 1 - t
    return low, nx - low, sum(nx - 2 * j for j in range(low))


def adjoint_inner_kernel(nx, matrix_ref, start, first, second, third, mismatch, mu_ref, flux_ref, a, b):
    h = STEPS
    points = mismatch.shape[0] // nx
    base = wall_profile(points, padded(points, 8))
    matrix = matrix_ref[...]
    for t in reversed(range(h)):
        source, target = (a, b) if t % 2 == 0 else (b, a)
        low, high, at = inner_range(nx, t)
        window = []
        for begin in range(low, high, 2):
            group = list(range(begin, min(begin + 2, high)))
            lams = [load(mismatch, i, nx) if t == h - 1 else source[i] for i in group]
            for i, mu in zip(group, product(matrix, lams)):
                u = own_field((start, first, second, third), t, i)
                flux = (base + u) * mu
                mu_ref[at + i - low] = mu
                flux_ref[at + i - low] = flux
                window = window[-2:] + [(u, mu, flux)]
                if len(window) == 3 and t > 0:
                    target[i - 1] = adjoint_value(*window)


def adjoint_outer_kernel(nx, matrix_ref, start, first, second, third, mu_ref, flux_ref, *refs):
    h = STEPS
    *sides, lam_ref, lams, mus, fluxes = refs
    points = sides[0].shape[0] // h
    left_fields, right_fields, left, right = sides
    base = wall_profile(points, padded(points, 8))
    matrix = matrix_ref[...]

    def field(t, i):
        if t == 2 and i == -3:
            return load(left_fields, h - 1, h)
        if t == 2 and i == nx + 2:
            return load(right_fields, h - 1, h)
        if t == 3 and i < -1:
            return load(left_fields, i + h, h)
        if t == 3 and i > nx:
            return load(right_fields, i - nx - 1, h)
        return own_field((start, first, second, third), t, i)

    for t in reversed(range(h)):
        low, high, at = inner_range(nx, t)
        planes = list(range(low - h, low)) + list(range(high, high + h))
        for begin in range(0, 2 * h, 2):
            group = planes[begin : begin + 2]
            if t < h - 1:
                given = [lams[begin + j] for j in range(2)]
            elif begin < h:
                given = [load(left, h + i, h) for i in group]
            else:
                given = [load(right, i - nx, h) for i in group]
            for j, mu in enumerate(product(matrix, given)):
                mus[begin + j] = mu
                fluxes[begin + j] = (base + field(t, group[j])) * mu

        def known(i, t=t, planes=planes, low=low, at=at):
            if i in planes:
                j = planes.index(i)
                return field(t, i), mus[j], fluxes[j]
            return field(t, i), mu_ref[at + i - low], flux_ref[at + i - low]

        for j, i in enumerate(list(range(low - h + 1, low + 1)) + list(range(high - 1, high + h - 1))):
            value = adjoint_value(known(i - 1), known(i), known(i + 1))
            if t == 0:
                lam_ref[i] = value
            else:
                lams[j] = value


def descent_kernel(nx, devices, sent, lam, prior, start, squares, *refs):
    h = STEPS
    states, forcing = refs[:2] if sent else (None, None)
    sums_ref, descent_ref, *edges = refs[2:] if sent else refs[1:]
    wide = WIDE
    more = wide - h
    parts = wide + 2 * more
    total = None
    for i in range(nx):
        value = lam[i] - (load(prior, i, nx) - start[i + 1])
        if sent:
            store(descent_ref, i, nx, value)
            if i < wide:
                store(edges[0], i, parts, value)
            if i >= nx - wide:
                store(edges[1], i - (nx - wide), parts, value)
        else:
            descent_ref[i] = value
        total = value * value if total is None else total + value * value
    for j in range(more if sent else 0):
        store(edges[0], wide + j, parts, load(states, h + j, nx))
        store(edges[1], wide + j, parts, load(states, nx - wide + j, nx))
        store(edges[0], wide + more + j, parts, load(forcing, h - 1 + j, nx))
        store(edges[1], wide + more + j, parts, load(forcing, nx - wide + 1 + j, nx))
    lane = lax.broadcasted_iota(jnp.int32, (1, LANES), 1)
    sums_ref[...] = jnp.broadcast_to(jnp.where(lane < LANES // 2, squares[...], halve(total)), (devices, LANES))


def final_kernel(nx, start, descent, sums, out_ref):
    tau = step_size(sums[...])
    for i in range(nx):
        store(out_ref, i, nx, start[i + 1] - tau * descent[i])


def shift(block, axis, distance):
    devices = lax.axis_size(axis)
    return lax.ppermute(block, axis, [((i - distance) % devices, i) for i in range(devices)])


def per_device(states, forcing, wall_viscosity):
    nx, points, _ = forcing.shape
    rows = padded(points, 8)
    depth = 3 * padded(points, 16)
    devices = lax.axis_size("seg") * lax.axis_size("space")
    h = STEPS
    f32, bf16 = jnp.float32, jnp.bfloat16

    def flat(planes):
        return ((planes * points, LANES), f32)

    def tiles(planes):
        return ((planes, rows, LANES), f32)

    states = jnp.transpose(states[0], (1, 0, 2)).reshape(nx * points, LANES)
    forcing = jnp.transpose(forcing, (1, 0, 2)).reshape(nx * points, LANES)
    to_left, to_right, states, forcing = call(
        functools.partial(pack_kernel, nx),
        "pack",
        [flat(2 * h - 1)] * 2 + [flat(nx)] * 2,
        [pltpu.with_memory_space_constraint(v, pltpu.HBM) for v in (states, forcing)],
        [pltpu.SemaphoreType.DMA((2, PARTS))],
        [pl.BlockSpec(memory_space=pltpu.HBM)] * 2,
    )
    left = shift(to_right, "space", 1)
    right = shift(to_left, "space", -1)
    after = shift(states, "seg", -1)
    forward, backward = call(
        functools.partial(inverse_kernel, points, rows),
        "inverse",
        [((rows, depth), bf16)] * 2,
        [wall_viscosity.reshape(1, points)],
        [pltpu.VMEM((LANES, LANES), f32)],
    )
    moved = d_after = sums = None
    for iteration in range(ITERS):
        updated = iteration > 0
        kept_fields = [tiles(nx + 2)] + [tiles(nx + 2 * width) for width in WIDTHS[1:-1]]
        if updated:
            ending, start, first, second, third = call(
                functools.partial(forward_kernel, nx),
                "forward",
                [flat(nx)] + kept_fields,
                [forward, left, right, q, start, *moved, sums],
                [pltpu.VMEM((2 * h, rows, LANES), f32)],
                fast=True,
            )
        else:
            start, q, first, second, third = call(
                functools.partial(forward_inner_kernel, nx),
                "forward_inner",
                [kept_fields[0], tiles(nx)] + kept_fields[1:],
                [forward, states, forcing],
            )
            ending, start, first, second, third, *sides = call(
                functools.partial(forward_outer_kernel, nx),
                "forward_outer",
                [flat(nx)] + kept_fields + [flat(h)] * 2,
                [forward, left, right, q, start, first, second, third],
                [pltpu.VMEM((2 * h, rows, LANES), f32)],
                aliases={4: 1, 5: 2, 6: 3, 7: 4},
            )
        prior = shift(ending, "seg", 1)
        if updated:
            sides = call(
                functools.partial(wide_kernel, nx),
                "wide",
                [flat(h)] * 2,
                [forward, left, right, *moved[1:], sums, first, second],
            )
        else:
            sides = [shift(sides[1], "space", 1), shift(sides[0], "space", -1)]
        mismatch, low, high, squares = call(
            functools.partial(mismatch_kernel, nx, updated),
            "mismatch",
            [flat(nx), flat(h), flat(h), ((1, LANES), f32)],
            [ending, after] + ([d_after, sums] if updated else []),
        )
        sides = [*sides, shift(high, "space", 1), shift(low, "space", -1)]
        fields = [start, first, second, third]
        planes = sum(nx - 2 * j for j in range(h))
        inner = call(
            functools.partial(adjoint_inner_kernel, nx),
            "adjoint_inner",
            [tiles(planes)] * 2,
            [backward, *fields, mismatch],
            [pltpu.VMEM((nx, rows, LANES), f32)] * 2,
        )
        lam = call(
            functools.partial(adjoint_outer_kernel, nx),
            "adjoint_outer",
            [tiles(nx)],
            [backward, *fields, *inner, *sides],
            [pltpu.VMEM((2 * h, rows, LANES), f32)] * 3,
        )[0]
        sent = iteration < ITERS - 1
        if not sent:
            kept = call(copy_kernel, "kept", [flat(nx)], [mismatch, inner[0]], specs=[VMEM, pl.BlockSpec(memory_space=pl.ANY)])[0]
        side = flat(WIDE + 2 * (WIDE - h))
        sums, descent, *edges = call(
            functools.partial(descent_kernel, nx, devices, sent),
            "descent",
            [((devices, LANES), f32)] + ([flat(nx), side, side] if sent else [tiles(nx)]),
            [lam, prior, start, squares]
            + ([states, forcing] if sent else [pltpu.with_memory_space_constraint(kept, pltpu.HBM)]),
            specs=[VMEM] * 4 + ([VMEM] * 2 if sent else [pl.BlockSpec(memory_space=pltpu.HBM)]),
        )
        sums = lax.all_to_all(sums, BOTH, 0, 0, tiled=True)
        if sent:
            moved = [descent, shift(edges[1], "space", 1), shift(edges[0], "space", -1)]
            d_after = shift(descent, "seg", -1)
    new = call(functools.partial(final_kernel, nx), "final", [flat(nx)], [start, descent, sums])[0]

    def placed(block):
        return jnp.transpose(block.reshape(points, nx, LANES), (1, 0, 2))[None]

    return (placed(new), placed(kept))


def solution(mesh):
    placed = (P("seg", "space", None, None), P("space", None, None), P())
    return jax.shard_map(
        per_device,
        mesh=mesh,
        in_specs=placed,
        out_specs=(P("seg", "space", None, None), P("seg", "space", None, None)),
        check_vma=False,
    )
```

```python
import functools

import jax
import jax.numpy as jnp
from jax import lax
from jax.experimental import pallas as pl
from jax.experimental.pallas import tpu as pltpu
from jax.sharding import PartitionSpec as P

STEPS = 4
ITERS = 2
ADVECT = 0.15
SPREAD = 0.2
PUSHED = 0.25
EPSILON = 1e-06
BOTH = ("seg", "space")
VMEM = pl.BlockSpec(memory_space=pltpu.VMEM)
LANES = 128
PARTS = 1


def padded(count, step):
    return -(-count // step) * step


def load(ref, i, planes):
    points = ref.shape[0] // planes
    plane = ref[pl.ds(i, points, stride=planes), :]
    return jnp.concatenate([plane, jnp.zeros((padded(points, 8) - points, LANES), jnp.float32)], 0)


def store(ref, i, planes, plane):
    points = ref.shape[0] // planes
    ref[pl.ds(i, points, stride=planes), :] = plane[:points]


WORK = {"forward_outer": 4e9, "inverse": 1e9}


def call(kernel, name, outs, operands, scratch=(), specs=None, fast=False, aliases=None):
    return pl.pallas_call(
        kernel,
        name=name,
        out_shape=[jax.ShapeDtypeStruct(shape, dtype) for shape, dtype in outs],
        in_specs=specs or [VMEM] * len(operands),
        out_specs=[VMEM] * len(outs),
        scratch_shapes=list(scratch),
        input_output_aliases=aliases or {},
        cost_estimate=pl.CostEstimate(flops=int(WORK[name]), transcendentals=0, bytes_accessed=1 << 20) if name in WORK and not fast else None,
        compiler_params=pltpu.CompilerParams(vmem_limit_bytes=32 * 1024 * 1024),
    )(*operands)


def inverse_kernel(points, rows, k_ref, forward_ref, backward_ref, square):
    row = lax.broadcasted_iota(jnp.int32, (LANES, LANES), 0)
    lane = lax.broadcasted_iota(jnp.int32, (LANES, LANES), 1)
    square[0:1, :] = jnp.zeros((1, LANES), jnp.float32)
    square[0:1, :points] = k_ref[...]
    k = jnp.sum(jnp.where(row == lane, square[0:1, :], 0.0), axis=1, keepdims=True)
    k = jnp.broadcast_to(k, (LANES, LANES))
    zero = jnp.zeros_like(k)
    a = jnp.where((row >= 1) & (row < points), -k, zero)
    c = jnp.where(row < points - 1, -k, zero)
    b = jnp.where(row < points, 1.0 + 2.0 * k, 1.0)
    d = jnp.where((row == lane) & (row < points), 1.0, 0.0)
    step = 1
    while step < points:
        up = lambda v: pltpu.roll(v, step, 0)
        down = lambda v: pltpu.roll(v, LANES - step, 0)
        alpha = -a / up(b)
        gamma = -c / down(b)
        b = b + alpha * up(c) + gamma * down(a)
        d = d + alpha * up(d) + gamma * down(d)
        a, c = alpha * up(a), gamma * down(c)
        step *= 2
    inverse = d / b
    square[...] = inverse
    stride = padded(points, 16)
    for ref, matrix in ((forward_ref, SPREAD * inverse), (backward_ref, square[...].T)):
        head = matrix.astype(jnp.bfloat16).astype(jnp.float32)
        tail = (matrix - head).astype(jnp.bfloat16).astype(jnp.float32)
        tail = pltpu.roll(tail, stride, 1)
        left = jnp.where(lane >= stride, tail, head)
        right = jnp.where(lane < stride + points - LANES, tail, pltpu.roll(head, 2 * stride - LANES, 1))
        ref[:, :LANES] = left[:rows].astype(jnp.bfloat16)
        ref[:, LANES:] = right[: rows, : 3 * stride - LANES].astype(jnp.bfloat16)


def product(matrix, planes):
    columns = []
    for plane in planes:
        rows = plane.shape[0]
        fill = jnp.zeros((padded(rows, 16) - rows, LANES), jnp.float32)
        plane = jnp.concatenate([plane, fill], 0) if fill.shape[0] else plane
        head = plane.astype(jnp.bfloat16)
        tail = (plane - head.astype(jnp.float32)).astype(jnp.bfloat16)
        columns.append(jnp.concatenate([head, head, tail], 0))
    right = jnp.concatenate(columns, 1) if len(columns) > 1 else columns[0]
    out = jnp.dot(matrix, right, preferred_element_type=jnp.float32)
    return [out[:, i * LANES : (i + 1) * LANES] for i in range(len(planes))]


def neighbours(plane):
    return pltpu.roll(plane, 1, 1) + pltpu.roll(plane, LANES - 1, 1)


def step_size(sums):
    total = jnp.sum(sums, axis=0, keepdims=True)
    lane = lax.broadcasted_iota(jnp.int32, total.shape, 1)
    squares = jnp.sum(jnp.where(lane < LANES // 2, 0.0, total), axis=1, keepdims=True)
    residual = jnp.sum(jnp.where(lane < LANES // 2, total, 0.0), axis=1, keepdims=True)
    return 0.5 * residual / (squares + EPSILON)


def parts(ref):
    size = padded(-(-ref.shape[0] // PARTS), 8)
    return [pl.ds(at, min(size, ref.shape[0] - at)) for at in range(0, ref.shape[0], size)]


def pack_kernel(nx, states_hbm, forcing_hbm, to_left, to_right, states, forcing, sems):
    h = STEPS
    copies = [
        [pltpu.make_async_copy(source.at[rows], target.at[rows], sems.at[k, j]) for j, rows in enumerate(parts(source))]
        for k, (source, target) in enumerate(((states_hbm, states), (forcing_hbm, forcing)))
    ]
    for copy in copies[0] + copies[1]:
        copy.start()
    for copy in copies[0]:
        copy.wait()
    for i in range(h):
        store(to_left, i, 2 * h - 1, load(states, i, nx))
        store(to_right, i, 2 * h - 1, load(states, nx - h + i, nx))
    for copy in copies[1]:
        copy.wait()
    for i in range(h - 1):
        store(to_left, h + i, 2 * h - 1, load(forcing, i, nx))
        store(to_right, h + i, 2 * h - 1, load(forcing, nx - h + 1 + i, nx))


def copy_kernel(given, order, out):
    out[...] = given[...]


def wall_profile(points, rows):
    row = lax.broadcasted_iota(jnp.int32, (rows, LANES), 0).astype(jnp.float32)
    return row * (2.0 / (points - 1)) - 1.0


def halve(total):
    row = jnp.sum(total, axis=0, keepdims=True)
    return row + pltpu.roll(row, LANES // 2, 1)


WIDTHS = (4, 3, 2, 1, 0)
WIDE = 7


def pushed_plane(base, before, here, ahead, force):
    return 3.0 * here + neighbours(here) + force - (base + here) * (ahead - before) * (0.5 * ADVECT / SPREAD)


def field_plane(nx, u0, start, fields, t, i):
    if t == 0:
        return u0[STEPS + i] if i < 0 else u0[STEPS + i - nx] if i >= nx else start[1 + i]
    return fields[t - 1][WIDTHS[t] + i]


def force_plane(nx, left, right, q_own, i):
    m = 2 * STEPS - 1
    if i < 0:
        return (PUSHED / SPREAD) * load(left, m + i, m)
    if i >= nx:
        return (PUSHED / SPREAD) * load(right, STEPS + i - nx, m)
    return q_own[i]


def forward_kernel(nx, matrix_ref, left, right, q_own, old, descent, d_left, d_right, sums, ending_ref, start, first, second, third, u0):
    h = STEPS
    m = 2 * h - 1
    parts = WIDE + 2 * (WIDE - h)
    points = left.shape[0] // m
    base = wall_profile(points, padded(points, 8))
    matrix = matrix_ref[...]
    tau = step_size(sums[...])
    for j in range(h):
        before = load(left, h - 1 - j, m) - tau * load(d_left, WIDE - 1 - j, parts)
        ahead = load(right, j, m) - tau * load(d_right, j, parts)
        if j == 0:
            start[0] = before
            start[nx + 1] = ahead
        u0[h - 1 - j] = before
        u0[h + j] = ahead
    for i in range(nx):
        start[1 + i] = old[1 + i] - tau * load(descent, i, nx)
    value = functools.partial(field_plane, nx, u0, start, (first, second, third))
    for t in range(h):
        planes = list(range(-WIDTHS[t + 1], nx + WIDTHS[t + 1]))
        for begin in range(0, len(planes), 2):
            group = planes[begin : begin + 2]
            pushed = [
                pushed_plane(base, value(t, i - 1), value(t, i), value(t, i + 1), force_plane(nx, left, right, q_own, i))
                for i in group
            ]
            for i, plane in zip(group, product(matrix, pushed)):
                if t == h - 1:
                    store(ending_ref, i, nx, plane)
                else:
                    (first, second, third)[t][WIDTHS[t + 1] + i] = plane


def forward_inner_kernel(nx, matrix_ref, states, forcing, start_ref, q_ref, first_ref, second_ref, third_ref):
    h = STEPS
    points = states.shape[0] // nx
    base = wall_profile(points, padded(points, 8))
    matrix = matrix_ref[...]
    for i in range(nx):
        start_ref[1 + i] = load(states, i, nx)
        q_ref[i] = (PUSHED / SPREAD) * load(forcing, i, nx)
    fields = ((start_ref, 1), (first_ref, WIDTHS[1]), (second_ref, WIDTHS[2]), (third_ref, WIDTHS[3]))
    for t in range(h - 1):
        (source, a), (target, b) = fields[t], fields[t + 1]
        planes = list(range(t + 1, nx - t - 1))
        for begin in range(0, len(planes), 2):
            group = planes[begin : begin + 2]
            pushed = [
                pushed_plane(base, source[a + i - 1], source[a + i], source[a + i + 1], q_ref[i]) for i in group
            ]
            for i, plane in zip(group, product(matrix, pushed)):
                target[b + i] = plane


def forward_outer_kernel(nx, matrix_ref, left, right, q_own, start_in, first_in, second_in, third_in, ending_ref, start, first, second, third, low_ref, high_ref, u0):
    h = STEPS
    m = 2 * h - 1
    points = left.shape[0] // m
    base = wall_profile(points, padded(points, 8))
    matrix = matrix_ref[...]
    for j in range(h):
        before, ahead = load(left, h - 1 - j, m), load(right, j, m)
        if j == 0:
            start[0] = before
            start[nx + 1] = ahead
        u0[h - 1 - j] = before
        u0[h + j] = ahead

    value = functools.partial(field_plane, nx, u0, start, (first, second, third))
    for t in range(h):
        planes = list(range(t + 1 - h, t + 1)) + list(range(nx - 1 - t, nx - 1 - t + h))
        for begin in range(0, 2 * h, 2):
            group = planes[begin : begin + 2]
            pushed = [
                pushed_plane(base, value(t, i - 1), value(t, i), value(t, i + 1), force_plane(nx, left, right, q_own, i))
                for i in group
            ]
            for i, plane in zip(group, product(matrix, pushed)):
                if t == h - 1:
                    store(ending_ref, i, nx, plane)
                else:
                    (first, second, third)[t][WIDTHS[t + 1] + i] = plane
    for i in range(h - 1):
        store(low_ref, i, h, third[WIDTHS[3] + 1 + i])
        store(high_ref, i, h, third[WIDTHS[3] + nx - h + i])
    store(low_ref, h - 1, h, second[WIDTHS[2] + 2])
    store(high_ref, h - 1, h, second[WIDTHS[2] + nx - 3])


def wide_kernel(nx, matrix_ref, left, right, d_left, d_right, sums, first, second, left_fields, right_fields):
    h = STEPS
    m = 2 * h - 1
    more = WIDE - h
    parts = WIDE + 2 * more
    points = left.shape[0] // m
    base = wall_profile(points, padded(points, 8))
    matrix = matrix_ref[...]
    tau = step_size(sums[...])
    scale = PUSHED / SPREAD

    def state(side, d):
        if side == 0:
            value = load(left, h - d, m) if d <= h else load(d_left, WIDE + WIDE - d, parts)
            return value - tau * load(d_left, WIDE - d, parts)
        value = load(right, d - 1, m) if d <= h else load(d_right, WIDE + d - 1 - h, parts)
        return value - tau * load(d_right, d - 1, parts)

    def push(side, d):
        if side == 0:
            return scale * (load(left, m - d, m) if d < h else load(d_left, parts - 1 - (d - h), parts))
        return scale * (load(right, h + d - 1, m) if d < h else load(d_right, WIDE + more + d - h, parts))

    u = [{d: state(side, d) for d in range(h - 1, WIDE + 1)} for side in range(2)]
    for t in range(3):
        reach = WIDE - t
        pushed, places = [], []
        for side in range(2):
            sign = 1.0 if side else -1.0
            for d in range(reach - 3, reach):
                here = u[side][d]
                slope = sign * (u[side][d + 1] - u[side][d - 1])
                pushed.append(
                    3.0 * here + neighbours(here) + push(side, d) - (base + here) * slope * (0.5 * ADVECT / SPREAD)
                )
                places.append((side, d))
        out = [{}, {}]
        for k in range(0, len(places), 2):
            for (side, d), plane in zip(places[k : k + 2], product(matrix, pushed[k : k + 2])):
                out[side][d] = plane
        for d in range(reach - 5, reach - 3):
            if t == 0:
                out[0][d], out[1][d] = first[WIDTHS[1] - d], first[WIDTHS[1] + nx - 1 + d]
            elif t == 1:
                out[0][d], out[1][d] = second[WIDTHS[2] - d], second[WIDTHS[2] + nx - 1 + d]
        u = out
        if t == 1:
            store(left_fields, h - 1, h, u[0][3])
            store(right_fields, h - 1, h, u[1][3])
    for d in range(2, h + 1):
        store(left_fields, h - d, h, u[0][d])
        store(right_fields, d - 2, h, u[1][d])


def mismatch_kernel(nx, updated, *refs):
    h = STEPS
    ending, after, *given = refs[:-4]
    mismatch_ref, low_ref, high_ref, squares_ref = refs[-4:]
    if updated:
        tau = step_size(given[1][...])
    total = None
    for i in range(nx):
        value = load(after, i, nx)
        if updated:
            value = value - tau * load(given[0], i, nx)
        value = load(ending, i, nx) - value
        store(mismatch_ref, i, nx, value)
        if i < h:
            store(low_ref, i, h, value)
        if i >= nx - h:
            store(high_ref, i - (nx - h), h, value)
        total = value * value if total is None else total + value * value
    squares_ref[...] = halve(total)


def adjoint_value(before, here, ahead):
    (u0, _, f0), (_, m1, _), (u2, _, f2) = before, here, ahead
    return SPREAD * (3.0 * m1 + neighbours(m1)) + (0.5 * ADVECT) * ((f2 - f0) - m1 * (u2 - u0))


def own_field(fields, t, i):
    return fields[t][i + (WIDTHS[t] if t else 1)]


def inner_range(nx, t):
    low = STEPS - 1 - t
    return low, nx - low, sum(nx - 2 * j for j in range(low))


def adjoint_inner_kernel(nx, matrix_ref, start, first, second, third, mismatch, mu_ref, flux_ref, a, b):
    h = STEPS
    points = mismatch.shape[0] // nx
    base = wall_profile(points, padded(points, 8))
    matrix = matrix_ref[...]
    for t in reversed(range(h)):
        source, target = (a, b) if t % 2 == 0 else (b, a)
        low, high, at = inner_range(nx, t)
        window = []
        for begin in range(low, high, 2):
            group = list(range(begin, min(begin + 2, high)))
            lams = [load(mismatch, i, nx) if t == h - 1 else source[i] for i in group]
            for i, mu in zip(group, product(matrix, lams)):
                u = own_field((start, first, second, third), t, i)
                flux = (base + u) * mu
                mu_ref[at + i - low] = mu
                flux_ref[at + i - low] = flux
                window = window[-2:] + [(u, mu, flux)]
                if len(window) == 3 and t > 0:
                    target[i - 1] = adjoint_value(*window)


def adjoint_outer_kernel(nx, matrix_ref, start, first, second, third, mu_ref, flux_ref, *refs):
    h = STEPS
    *sides, lam_ref, lams, mus, fluxes = refs
    points = sides[0].shape[0] // h
    left_fields, right_fields, left, right = sides
    base = wall_profile(points, padded(points, 8))
    matrix = matrix_ref[...]

    def field(t, i):
        if t == 2 and i == -3:
            return load(left_fields, h - 1, h)
        if t == 2 and i == nx + 2:
            return load(right_fields, h - 1, h)
        if t == 3 and i < -1:
            return load(left_fields, i + h, h)
        if t == 3 and i > nx:
            return load(right_fields, i - nx - 1, h)
        return own_field((start, first, second, third), t, i)

    for t in reversed(range(h)):
        low, high, at = inner_range(nx, t)
        planes = list(range(low - h, low)) + list(range(high, high + h))
        for begin in range(0, 2 * h, 2):
            group = planes[begin : begin + 2]
            if t < h - 1:
                given = [lams[begin + j] for j in range(2)]
            elif begin < h:
                given = [load(left, h + i, h) for i in group]
            else:
                given = [load(right, i - nx, h) for i in group]
            for j, mu in enumerate(product(matrix, given)):
                mus[begin + j] = mu
                fluxes[begin + j] = (base + field(t, group[j])) * mu

        def known(i, t=t, planes=planes, low=low, at=at):
            if i in planes:
                j = planes.index(i)
                return field(t, i), mus[j], fluxes[j]
            return field(t, i), mu_ref[at + i - low], flux_ref[at + i - low]

        for j, i in enumerate(list(range(low - h + 1, low + 1)) + list(range(high - 1, high + h - 1))):
            value = adjoint_value(known(i - 1), known(i), known(i + 1))
            if t == 0:
                lam_ref[i] = value
            else:
                lams[j] = value


def descent_kernel(nx, devices, sent, lam, prior, start, squares, *refs):
    h = STEPS
    states, forcing = refs[:2] if sent else (None, None)
    sums_ref, descent_ref, *edges = refs[2:] if sent else refs[1:]
    wide = WIDE
    more = wide - h
    parts = wide + 2 * more
    total = None
    for i in range(nx):
        value = lam[i] - (load(prior, i, nx) - start[i + 1])
        if sent:
            store(descent_ref, i, nx, value)
            if i < wide:
                store(edges[0], i, parts, value)
            if i >= nx - wide:
                store(edges[1], i - (nx - wide), parts, value)
        else:
            descent_ref[i] = value
        total = value * value if total is None else total + value * value
    for j in range(more if sent else 0):
        store(edges[0], wide + j, parts, load(states, h + j, nx))
        store(edges[1], wide + j, parts, load(states, nx - wide + j, nx))
        store(edges[0], wide + more + j, parts, load(forcing, h - 1 + j, nx))
        store(edges[1], wide + more + j, parts, load(forcing, nx - wide + 1 + j, nx))
    lane = lax.broadcasted_iota(jnp.int32, (1, LANES), 1)
    sums_ref[...] = jnp.broadcast_to(jnp.where(lane < LANES // 2, squares[...], halve(total)), (devices, LANES))


def final_kernel(nx, start, descent, sums, out_ref):
    tau = step_size(sums[...])
    for i in range(nx):
        store(out_ref, i, nx, start[i + 1] - tau * descent[i])


def shift(block, axis, distance):
    devices = lax.axis_size(axis)
    return lax.ppermute(block, axis, [((i - distance) % devices, i) for i in range(devices)])


def per_device(states, forcing, wall_viscosity):
    nx, points, _ = forcing.shape
    rows = padded(points, 8)
    depth = 3 * padded(points, 16)
    devices = lax.axis_size("seg") * lax.axis_size("space")
    h = STEPS
    f32, bf16 = jnp.float32, jnp.bfloat16

    def flat(planes):
        return ((planes * points, LANES), f32)

    def tiles(planes):
        return ((planes, rows, LANES), f32)

    states = jnp.transpose(states[0], (1, 0, 2)).reshape(nx * points, LANES)
    forcing = jnp.transpose(forcing, (1, 0, 2)).reshape(nx * points, LANES)
    to_left, to_right, states, forcing = call(
        functools.partial(pack_kernel, nx),
        "pack",
        [flat(2 * h - 1)] * 2 + [flat(nx)] * 2,
        [pltpu.with_memory_space_constraint(v, pltpu.HBM) for v in (states, forcing)],
        [pltpu.SemaphoreType.DMA((2, PARTS))],
        [pl.BlockSpec(memory_space=pltpu.HBM)] * 2,
    )
    left = shift(to_right, "space", 1)
    right = shift(to_left, "space", -1)
    after = shift(states, "seg", -1)
    forward, backward = call(
        functools.partial(inverse_kernel, points, rows),
        "inverse",
        [((rows, depth), bf16)] * 2,
        [wall_viscosity.reshape(1, points)],
        [pltpu.VMEM((LANES, LANES), f32)],
    )
    moved = d_after = sums = None
    for iteration in range(ITERS):
        updated = iteration > 0
        kept_fields = [tiles(nx + 2)] + [tiles(nx + 2 * width) for width in WIDTHS[1:-1]]
        if updated:
            ending, start, first, second, third = call(
                functools.partial(forward_kernel, nx),
                "forward",
                [flat(nx)] + kept_fields,
                [forward, left, right, q, start, *moved, sums],
                [pltpu.VMEM((2 * h, rows, LANES), f32)],
                fast=True,
            )
        else:
            start, q, first, second, third = call(
                functools.partial(forward_inner_kernel, nx),
                "forward_inner",
                [kept_fields[0], tiles(nx)] + kept_fields[1:],
                [forward, states, forcing],
            )
            ending, start, first, second, third, *sides = call(
                functools.partial(forward_outer_kernel, nx),
                "forward_outer",
                [flat(nx)] + kept_fields + [flat(h)] * 2,
                [forward, left, right, q, start, first, second, third],
                [pltpu.VMEM((2 * h, rows, LANES), f32)],
                aliases={4: 1, 5: 2, 6: 3, 7: 4},
            )
        prior = shift(ending, "seg", 1)
        if updated:
            sides = call(
                functools.partial(wide_kernel, nx),
                "wide",
                [flat(h)] * 2,
                [forward, left, right, *moved[1:], sums, first, second],
            )
        else:
            sides = [shift(sides[1], "space", 1), shift(sides[0], "space", -1)]
        mismatch, low, high, squares = call(
            functools.partial(mismatch_kernel, nx, updated),
            "mismatch",
            [flat(nx), flat(h), flat(h), ((1, LANES), f32)],
            [ending, after] + ([d_after, sums] if updated else []),
        )
        sides = [*sides, shift(high, "space", 1), shift(low, "space", -1)]
        fields = [start, first, second, third]
        planes = sum(nx - 2 * j for j in range(h))
        inner = call(
            functools.partial(adjoint_inner_kernel, nx),
            "adjoint_inner",
            [tiles(planes)] * 2,
            [backward, *fields, mismatch],
            [pltpu.VMEM((nx, rows, LANES), f32)] * 2,
        )
        lam = call(
            functools.partial(adjoint_outer_kernel, nx),
            "adjoint_outer",
            [tiles(nx)],
            [backward, *fields, *inner, *sides],
            [pltpu.VMEM((2 * h, rows, LANES), f32)] * 3,
        )[0]
        sent = iteration < ITERS - 1
        if not sent:
            kept = call(copy_kernel, "kept", [flat(nx)], [mismatch, inner[0]], specs=[VMEM, pl.BlockSpec(memory_space=pl.ANY)])[0]
        side = flat(WIDE + 2 * (WIDE - h))
        sums, descent, *edges = call(
            functools.partial(descent_kernel, nx, devices, sent),
            "descent",
            [((devices, LANES), f32)] + ([flat(nx), side, side] if sent else [tiles(nx)]),
            [lam, prior, start, squares]
            + ([states, forcing] if sent else [pltpu.with_memory_space_constraint(kept, pltpu.HBM)]),
            specs=[VMEM] * 4 + ([VMEM] * 2 if sent else [pl.BlockSpec(memory_space=pltpu.HBM)]),
        )
        sums = lax.all_to_all(sums, BOTH, 0, 0, tiled=True)
        if sent:
            moved = [descent, shift(edges[1], "space", 1), shift(edges[0], "space", -1)]
            d_after = shift(descent, "seg", -1)
    new = call(functools.partial(final_kernel, nx), "final", [flat(nx)], [start, descent, sums])[0]

    def placed(block):
        return jnp.transpose(block.reshape(points, nx, LANES), (1, 0, 2))[None]

    return (placed(new), placed(kept))


def solution(mesh):
    placed = (P("seg", "space", None, None), P("space", None, None), P())
    return jax.shard_map(
        per_device,
        mesh=mesh,
        in_specs=placed,
        out_specs=(P("seg", "space", None, None), P("seg", "space", None, None)),
        check_vma=False,
    )
```

```python
import functools

import jax
import jax.numpy as jnp
from jax import lax
from jax.experimental import pallas as pl
from jax.experimental.pallas import tpu as pltpu
from jax.sharding import PartitionSpec as P

STEPS = 4
ITERS = 2
ADVECT = 0.15
SPREAD = 0.2
PUSHED = 0.25
EPSILON = 1e-06
BOTH = ("seg", "space")
VMEM = pl.BlockSpec(memory_space=pltpu.VMEM)
LANES = 128
PARTS = 4


def padded(count, step):
    return -(-count // step) * step


def load(ref, i, planes):
    points = ref.shape[0] // planes
    plane = ref[pl.ds(i, points, stride=planes), :]
    return jnp.concatenate([plane, jnp.zeros((padded(points, 8) - points, LANES), jnp.float32)], 0)


def store(ref, i, planes, plane):
    points = ref.shape[0] // planes
    ref[pl.ds(i, points, stride=planes), :] = plane[:points]


WORK = {"forward_outer": 4e9, "inverse": 1e9}


def call(kernel, name, outs, operands, scratch=(), specs=None, fast=False, aliases=None):
    return pl.pallas_call(
        kernel,
        name=name,
        out_shape=[jax.ShapeDtypeStruct(shape, dtype) for shape, dtype in outs],
        in_specs=specs or [VMEM] * len(operands),
        out_specs=[VMEM] * len(outs),
        scratch_shapes=list(scratch),
        input_output_aliases=aliases or {},
        cost_estimate=pl.CostEstimate(flops=int(WORK[name]), transcendentals=0, bytes_accessed=1 << 20) if name in WORK and not fast else None,
        compiler_params=pltpu.CompilerParams(vmem_limit_bytes=32 * 1024 * 1024),
    )(*operands)


def inverse_kernel(points, rows, k_ref, forward_ref, backward_ref, square):
    row = lax.broadcasted_iota(jnp.int32, (LANES, LANES), 0)
    lane = lax.broadcasted_iota(jnp.int32, (LANES, LANES), 1)
    square[0:1, :] = jnp.zeros((1, LANES), jnp.float32)
    square[0:1, :points] = k_ref[...]
    k = jnp.sum(jnp.where(row == lane, square[0:1, :], 0.0), axis=1, keepdims=True)
    k = jnp.broadcast_to(k, (LANES, LANES))
    zero = jnp.zeros_like(k)
    a = jnp.where((row >= 1) & (row < points), -k, zero)
    c = jnp.where(row < points - 1, -k, zero)
    b = jnp.where(row < points, 1.0 + 2.0 * k, 1.0)
    d = jnp.where((row == lane) & (row < points), 1.0, 0.0)
    step = 1
    while step < points:
        up = lambda v: pltpu.roll(v, step, 0)
        down = lambda v: pltpu.roll(v, LANES - step, 0)
        alpha = -a / up(b)
        gamma = -c / down(b)
        b = b + alpha * up(c) + gamma * down(a)
        d = d + alpha * up(d) + gamma * down(d)
        a, c = alpha * up(a), gamma * down(c)
        step *= 2
    inverse = d / b
    square[...] = inverse
    stride = padded(points, 16)
    for ref, matrix in ((forward_ref, SPREAD * inverse), (backward_ref, square[...].T)):
        head = matrix.astype(jnp.bfloat16).astype(jnp.float32)
        tail = (matrix - head).astype(jnp.bfloat16).astype(jnp.float32)
        tail = pltpu.roll(tail, stride, 1)
        left = jnp.where(lane >= stride, tail, head)
        right = jnp.where(lane < stride + points - LANES, tail, pltpu.roll(head, 2 * stride - LANES, 1))
        ref[:, :LANES] = left[:rows].astype(jnp.bfloat16)
        ref[:, LANES:] = right[: rows, : 3 * stride - LANES].astype(jnp.bfloat16)


def product(matrix, planes):
    columns = []
    for plane in planes:
        rows = plane.shape[0]
        fill = jnp.zeros((padded(rows, 16) - rows, LANES), jnp.float32)
        plane = jnp.concatenate([plane, fill], 0) if fill.shape[0] else plane
        head = plane.astype(jnp.bfloat16)
        tail = (plane - head.astype(jnp.float32)).astype(jnp.bfloat16)
        columns.append(jnp.concatenate([head, head, tail], 0))
    right = jnp.concatenate(columns, 1) if len(columns) > 1 else columns[0]
    out = jnp.dot(matrix, right, preferred_element_type=jnp.float32)
    return [out[:, i * LANES : (i + 1) * LANES] for i in range(len(planes))]


def neighbours(plane):
    return pltpu.roll(plane, 1, 1) + pltpu.roll(plane, LANES - 1, 1)


def step_size(sums):
    total = jnp.sum(sums, axis=0, keepdims=True)
    lane = lax.broadcasted_iota(jnp.int32, total.shape, 1)
    squares = jnp.sum(jnp.where(lane < LANES // 2, 0.0, total), axis=1, keepdims=True)
    residual = jnp.sum(jnp.where(lane < LANES // 2, total, 0.0), axis=1, keepdims=True)
    return 0.5 * residual / (squares + EPSILON)


def parts(ref):
    size = padded(-(-ref.shape[0] // PARTS), 8)
    return [pl.ds(at, min(size, ref.shape[0] - at)) for at in range(0, ref.shape[0], size)]


def pack_kernel(nx, states_hbm, forcing_hbm, to_left, to_right, states, forcing, sems):
    h = STEPS
    copies = [
        [pltpu.make_async_copy(source.at[rows], target.at[rows], sems.at[k, j]) for j, rows in enumerate(parts(source))]
        for k, (source, target) in enumerate(((states_hbm, states), (forcing_hbm, forcing)))
    ]
    for copy in copies[0] + copies[1]:
        copy.start()
    for copy in copies[0]:
        copy.wait()
    for i in range(h):
        store(to_left, i, 2 * h - 1, load(states, i, nx))
        store(to_right, i, 2 * h - 1, load(states, nx - h + i, nx))
    for copy in copies[1]:
        copy.wait()
    for i in range(h - 1):
        store(to_left, h + i, 2 * h - 1, load(forcing, i, nx))
        store(to_right, h + i, 2 * h - 1, load(forcing, nx - h + 1 + i, nx))


def copy_kernel(given, order, out):
    out[...] = given[...]


def wall_profile(points, rows):
    row = lax.broadcasted_iota(jnp.int32, (rows, LANES), 0).astype(jnp.float32)
    return row * (2.0 / (points - 1)) - 1.0


def halve(total):
    row = jnp.sum(total, axis=0, keepdims=True)
    return row + pltpu.roll(row, LANES // 2, 1)


WIDTHS = (4, 3, 2, 1, 0)
WIDE = 7


def pushed_plane(base, before, here, ahead, force):
    return 3.0 * here + neighbours(here) + force - (base + here) * (ahead - before) * (0.5 * ADVECT / SPREAD)


def field_plane(nx, u0, start, fields, t, i):
    if t == 0:
        return u0[STEPS + i] if i < 0 else u0[STEPS + i - nx] if i >= nx else start[1 + i]
    return fields[t - 1][WIDTHS[t] + i]


def force_plane(nx, left, right, q_own, i):
    m = 2 * STEPS - 1
    if i < 0:
        return (PUSHED / SPREAD) * load(left, m + i, m)
    if i >= nx:
        return (PUSHED / SPREAD) * load(right, STEPS + i - nx, m)
    return q_own[i]


def forward_kernel(nx, matrix_ref, left, right, q_own, old, descent, d_left, d_right, sums, ending_ref, start, first, second, third, u0):
    h = STEPS
    m = 2 * h - 1
    parts = WIDE + 2 * (WIDE - h)
    points = left.shape[0] // m
    base = wall_profile(points, padded(points, 8))
    matrix = matrix_ref[...]
    tau = step_size(sums[...])
    for j in range(h):
        before = load(left, h - 1 - j, m) - tau * load(d_left, WIDE - 1 - j, parts)
        ahead = load(right, j, m) - tau * load(d_right, j, parts)
        if j == 0:
            start[0] = before
            start[nx + 1] = ahead
        u0[h - 1 - j] = before
        u0[h + j] = ahead
    for i in range(nx):
        start[1 + i] = old[1 + i] - tau * load(descent, i, nx)
    value = functools.partial(field_plane, nx, u0, start, (first, second, third))
    for t in range(h):
        planes = list(range(-WIDTHS[t + 1], nx + WIDTHS[t + 1]))
        for begin in range(0, len(planes), 2):
            group = planes[begin : begin + 2]
            pushed = [
                pushed_plane(base, value(t, i - 1), value(t, i), value(t, i + 1), force_plane(nx, left, right, q_own, i))
                for i in group
            ]
            for i, plane in zip(group, product(matrix, pushed)):
                if t == h - 1:
                    store(ending_ref, i, nx, plane)
                else:
                    (first, second, third)[t][WIDTHS[t + 1] + i] = plane


def forward_inner_kernel(nx, matrix_ref, states, forcing, start_ref, q_ref, first_ref, second_ref, third_ref):
    h = STEPS
    points = states.shape[0] // nx
    base = wall_profile(points, padded(points, 8))
    matrix = matrix_ref[...]
    for i in range(nx):
        start_ref[1 + i] = load(states, i, nx)
        q_ref[i] = (PUSHED / SPREAD) * load(forcing, i, nx)
    fields = ((start_ref, 1), (first_ref, WIDTHS[1]), (second_ref, WIDTHS[2]), (third_ref, WIDTHS[3]))
    for t in range(h - 1):
        (source, a), (target, b) = fields[t], fields[t + 1]
        planes = list(range(t + 1, nx - t - 1))
        for begin in range(0, len(planes), 2):
            group = planes[begin : begin + 2]
            pushed = [
                pushed_plane(base, source[a + i - 1], source[a + i], source[a + i + 1], q_ref[i]) for i in group
            ]
            for i, plane in zip(group, product(matrix, pushed)):
                target[b + i] = plane


def forward_outer_kernel(nx, matrix_ref, left, right, q_own, start_in, first_in, second_in, third_in, ending_ref, start, first, second, third, low_ref, high_ref, u0):
    h = STEPS
    m = 2 * h - 1
    points = left.shape[0] // m
    base = wall_profile(points, padded(points, 8))
    matrix = matrix_ref[...]
    for j in range(h):
        before, ahead = load(left, h - 1 - j, m), load(right, j, m)
        if j == 0:
            start[0] = before
            start[nx + 1] = ahead
        u0[h - 1 - j] = before
        u0[h + j] = ahead

    value = functools.partial(field_plane, nx, u0, start, (first, second, third))
    for t in range(h):
        planes = list(range(t + 1 - h, t + 1)) + list(range(nx - 1 - t, nx - 1 - t + h))
        for begin in range(0, 2 * h, 2):
            group = planes[begin : begin + 2]
            pushed = [
                pushed_plane(base, value(t, i - 1), value(t, i), value(t, i + 1), force_plane(nx, left, right, q_own, i))
                for i in group
            ]
            for i, plane in zip(group, product(matrix, pushed)):
                if t == h - 1:
                    store(ending_ref, i, nx, plane)
                else:
                    (first, second, third)[t][WIDTHS[t + 1] + i] = plane
    for i in range(h - 1):
        store(low_ref, i, h, third[WIDTHS[3] + 1 + i])
        store(high_ref, i, h, third[WIDTHS[3] + nx - h + i])
    store(low_ref, h - 1, h, second[WIDTHS[2] + 2])
    store(high_ref, h - 1, h, second[WIDTHS[2] + nx - 3])


def wide_kernel(nx, matrix_ref, left, right, d_left, d_right, sums, first, second, left_fields, right_fields):
    h = STEPS
    m = 2 * h - 1
    more = WIDE - h
    parts = WIDE + 2 * more
    points = left.shape[0] // m
    base = wall_profile(points, padded(points, 8))
    matrix = matrix_ref[...]
    tau = step_size(sums[...])
    scale = PUSHED / SPREAD

    def state(side, d):
        if side == 0:
            value = load(left, h - d, m) if d <= h else load(d_left, WIDE + WIDE - d, parts)
            return value - tau * load(d_left, WIDE - d, parts)
        value = load(right, d - 1, m) if d <= h else load(d_right, WIDE + d - 1 - h, parts)
        return value - tau * load(d_right, d - 1, parts)

    def push(side, d):
        if side == 0:
            return scale * (load(left, m - d, m) if d < h else load(d_left, parts - 1 - (d - h), parts))
        return scale * (load(right, h + d - 1, m) if d < h else load(d_right, WIDE + more + d - h, parts))

    u = [{d: state(side, d) for d in range(h - 1, WIDE + 1)} for side in range(2)]
    for t in range(3):
        reach = WIDE - t
        pushed, places = [], []
        for side in range(2):
            sign = 1.0 if side else -1.0
            for d in range(reach - 3, reach):
                here = u[side][d]
                slope = sign * (u[side][d + 1] - u[side][d - 1])
                pushed.append(
                    3.0 * here + neighbours(here) + push(side, d) - (base + here) * slope * (0.5 * ADVECT / SPREAD)
                )
                places.append((side, d))
        out = [{}, {}]
        for k in range(0, len(places), 2):
            for (side, d), plane in zip(places[k : k + 2], product(matrix, pushed[k : k + 2])):
                out[side][d] = plane
        for d in range(reach - 5, reach - 3):
            if t == 0:
                out[0][d], out[1][d] = first[WIDTHS[1] - d], first[WIDTHS[1] + nx - 1 + d]
            elif t == 1:
                out[0][d], out[1][d] = second[WIDTHS[2] - d], second[WIDTHS[2] + nx - 1 + d]
        u = out
        if t == 1:
            store(left_fields, h - 1, h, u[0][3])
            store(right_fields, h - 1, h, u[1][3])
    for d in range(2, h + 1):
        store(left_fields, h - d, h, u[0][d])
        store(right_fields, d - 2, h, u[1][d])


def mismatch_kernel(nx, updated, *refs):
    h = STEPS
    ending, after, *given = refs[:-4]
    mismatch_ref, low_ref, high_ref, squares_ref = refs[-4:]
    if updated:
        tau = step_size(given[1][...])
    total = None
    for i in range(nx):
        value = load(after, i, nx)
        if updated:
            value = value - tau * load(given[0], i, nx)
        value = load(ending, i, nx) - value
        store(mismatch_ref, i, nx, value)
        if i < h:
            store(low_ref, i, h, value)
        if i >= nx - h:
            store(high_ref, i - (nx - h), h, value)
        total = value * value if total is None else total + value * value
    squares_ref[...] = halve(total)


def adjoint_value(before, here, ahead):
    (u0, _, f0), (_, m1, _), (u2, _, f2) = before, here, ahead
    return SPREAD * (3.0 * m1 + neighbours(m1)) + (0.5 * ADVECT) * ((f2 - f0) - m1 * (u2 - u0))


def own_field(fields, t, i):
    return fields[t][i + (WIDTHS[t] if t else 1)]


def inner_range(nx, t):
    low = STEPS - 1 - t
    return low, nx - low, sum(nx - 2 * j for j in range(low))


def adjoint_inner_kernel(nx, matrix_ref, start, first, second, third, mismatch, mu_ref, flux_ref, a, b):
    h = STEPS
    points = mismatch.shape[0] // nx
    base = wall_profile(points, padded(points, 8))
    matrix = matrix_ref[...]
    for t in reversed(range(h)):
        source, target = (a, b) if t % 2 == 0 else (b, a)
        low, high, at = inner_range(nx, t)
        window = []
        for begin in range(low, high, 2):
            group = list(range(begin, min(begin + 2, high)))
            lams = [load(mismatch, i, nx) if t == h - 1 else source[i] for i in group]
            for i, mu in zip(group, product(matrix, lams)):
                u = own_field((start, first, second, third), t, i)
                flux = (base + u) * mu
                mu_ref[at + i - low] = mu
                flux_ref[at + i - low] = flux
                window = window[-2:] + [(u, mu, flux)]
                if len(window) == 3 and t > 0:
                    target[i - 1] = adjoint_value(*window)


def adjoint_outer_kernel(nx, matrix_ref, start, first, second, third, mu_ref, flux_ref, *refs):
    h = STEPS
    *sides, lam_ref, lams, mus, fluxes = refs
    points = sides[0].shape[0] // h
    left_fields, right_fields, left, right = sides
    base = wall_profile(points, padded(points, 8))
    matrix = matrix_ref[...]

    def field(t, i):
        if t == 2 and i == -3:
            return load(left_fields, h - 1, h)
        if t == 2 and i == nx + 2:
            return load(right_fields, h - 1, h)
        if t == 3 and i < -1:
            return load(left_fields, i + h, h)
        if t == 3 and i > nx:
            return load(right_fields, i - nx - 1, h)
        return own_field((start, first, second, third), t, i)

    for t in reversed(range(h)):
        low, high, at = inner_range(nx, t)
        planes = list(range(low - h, low)) + list(range(high, high + h))
        for begin in range(0, 2 * h, 2):
            group = planes[begin : begin + 2]
            if t < h - 1:
                given = [lams[begin + j] for j in range(2)]
            elif begin < h:
                given = [load(left, h + i, h) for i in group]
            else:
                given = [load(right, i - nx, h) for i in group]
            for j, mu in enumerate(product(matrix, given)):
                mus[begin + j] = mu
                fluxes[begin + j] = (base + field(t, group[j])) * mu

        def known(i, t=t, planes=planes, low=low, at=at):
            if i in planes:
                j = planes.index(i)
                return field(t, i), mus[j], fluxes[j]
            return field(t, i), mu_ref[at + i - low], flux_ref[at + i - low]

        for j, i in enumerate(list(range(low - h + 1, low + 1)) + list(range(high - 1, high + h - 1))):
            value = adjoint_value(known(i - 1), known(i), known(i + 1))
            if t == 0:
                lam_ref[i] = value
            else:
                lams[j] = value


def descent_kernel(nx, devices, sent, lam, prior, start, squares, *refs):
    h = STEPS
    states, forcing = refs[:2] if sent else (None, None)
    sums_ref, descent_ref, *edges = refs[2:] if sent else refs[1:]
    wide = WIDE
    more = wide - h
    parts = wide + 2 * more
    total = None
    for i in range(nx):
        value = lam[i] - (load(prior, i, nx) - start[i + 1])
        if sent:
            store(descent_ref, i, nx, value)
            if i < wide:
                store(edges[0], i, parts, value)
            if i >= nx - wide:
                store(edges[1], i - (nx - wide), parts, value)
        else:
            descent_ref[i] = value
        total = value * value if total is None else total + value * value
    for j in range(more if sent else 0):
        store(edges[0], wide + j, parts, load(states, h + j, nx))
        store(edges[1], wide + j, parts, load(states, nx - wide + j, nx))
        store(edges[0], wide + more + j, parts, load(forcing, h - 1 + j, nx))
        store(edges[1], wide + more + j, parts, load(forcing, nx - wide + 1 + j, nx))
    lane = lax.broadcasted_iota(jnp.int32, (1, LANES), 1)
    sums_ref[...] = jnp.broadcast_to(jnp.where(lane < LANES // 2, squares[...], halve(total)), (devices, LANES))


def final_kernel(nx, start, descent, sums, out_ref):
    tau = step_size(sums[...])
    for i in range(nx):
        store(out_ref, i, nx, start[i + 1] - tau * descent[i])


def shift(block, axis, distance):
    devices = lax.axis_size(axis)
    return lax.ppermute(block, axis, [((i - distance) % devices, i) for i in range(devices)])


def per_device(states, forcing, wall_viscosity):
    nx, points, _ = forcing.shape
    rows = padded(points, 8)
    depth = 3 * padded(points, 16)
    devices = lax.axis_size("seg") * lax.axis_size("space")
    h = STEPS
    f32, bf16 = jnp.float32, jnp.bfloat16

    def flat(planes):
        return ((planes * points, LANES), f32)

    def tiles(planes):
        return ((planes, rows, LANES), f32)

    states = jnp.transpose(states[0], (1, 0, 2)).reshape(nx * points, LANES)
    forcing = jnp.transpose(forcing, (1, 0, 2)).reshape(nx * points, LANES)
    to_left, to_right, states, forcing = call(
        functools.partial(pack_kernel, nx),
        "pack",
        [flat(2 * h - 1)] * 2 + [flat(nx)] * 2,
        [pltpu.with_memory_space_constraint(v, pltpu.HBM) for v in (states, forcing)],
        [pltpu.SemaphoreType.DMA((2, PARTS))],
        [pl.BlockSpec(memory_space=pltpu.HBM)] * 2,
    )
    left = shift(to_right, "space", 1)
    right = shift(to_left, "space", -1)
    after = shift(states, "seg", -1)
    forward, backward = call(
        functools.partial(inverse_kernel, points, rows),
        "inverse",
        [((rows, depth), bf16)] * 2,
        [wall_viscosity.reshape(1, points)],
        [pltpu.VMEM((LANES, LANES), f32)],
    )
    moved = d_after = sums = None
    for iteration in range(ITERS):
        updated = iteration > 0
        kept_fields = [tiles(nx + 2)] + [tiles(nx + 2 * width) for width in WIDTHS[1:-1]]
        if updated:
            ending, start, first, second, third = call(
                functools.partial(forward_kernel, nx),
                "forward",
                [flat(nx)] + kept_fields,
                [forward, left, right, q, start, *moved, sums],
                [pltpu.VMEM((2 * h, rows, LANES), f32)],
                fast=True,
            )
        else:
            start, q, first, second, third = call(
                functools.partial(forward_inner_kernel, nx),
                "forward_inner",
                [kept_fields[0], tiles(nx)] + kept_fields[1:],
                [forward, states, forcing],
            )
            ending, start, first, second, third, *sides = call(
                functools.partial(forward_outer_kernel, nx),
                "forward_outer",
                [flat(nx)] + kept_fields + [flat(h)] * 2,
                [forward, left, right, q, start, first, second, third],
                [pltpu.VMEM((2 * h, rows, LANES), f32)],
                aliases={4: 1, 5: 2, 6: 3, 7: 4},
            )
        prior = shift(ending, "seg", 1)
        if updated:
            sides = call(
                functools.partial(wide_kernel, nx),
                "wide",
                [flat(h)] * 2,
                [forward, left, right, *moved[1:], sums, first, second],
            )
        else:
            sides = [shift(sides[1], "space", 1), shift(sides[0], "space", -1)]
        mismatch, low, high, squares = call(
            functools.partial(mismatch_kernel, nx, updated),
            "mismatch",
            [flat(nx), flat(h), flat(h), ((1, LANES), f32)],
            [ending, after] + ([d_after, sums] if updated else []),
        )
        sides = [*sides, shift(high, "space", 1), shift(low, "space", -1)]
        fields = [start, first, second, third]
        planes = sum(nx - 2 * j for j in range(h))
        inner = call(
            functools.partial(adjoint_inner_kernel, nx),
            "adjoint_inner",
            [tiles(planes)] * 2,
            [backward, *fields, mismatch],
            [pltpu.VMEM((nx, rows, LANES), f32)] * 2,
        )
        lam = call(
            functools.partial(adjoint_outer_kernel, nx),
            "adjoint_outer",
            [tiles(nx)],
            [backward, *fields, *inner, *sides],
            [pltpu.VMEM((2 * h, rows, LANES), f32)] * 3,
        )[0]
        sent = iteration < ITERS - 1
        if not sent:
            kept = call(copy_kernel, "kept", [flat(nx)], [mismatch, sides[0]], specs=[VMEM, pl.BlockSpec(memory_space=pl.ANY)])[0]
        side = flat(WIDE + 2 * (WIDE - h))
        sums, descent, *edges = call(
            functools.partial(descent_kernel, nx, devices, sent),
            "descent",
            [((devices, LANES), f32)] + ([flat(nx), side, side] if sent else [tiles(nx)]),
            [lam, prior, start, squares]
            + ([states, forcing] if sent else [pltpu.with_memory_space_constraint(kept, pltpu.HBM)]),
            specs=[VMEM] * 4 + ([VMEM] * 2 if sent else [pl.BlockSpec(memory_space=pltpu.HBM)]),
        )
        sums = lax.all_to_all(sums, BOTH, 0, 0, tiled=True)
        if sent:
            moved = [descent, shift(edges[1], "space", 1), shift(edges[0], "space", -1)]
            d_after = shift(descent, "seg", -1)
    new = call(functools.partial(final_kernel, nx), "final", [flat(nx)], [start, descent, sums])[0]

    def placed(block):
        return jnp.transpose(block.reshape(points, nx, LANES), (1, 0, 2))[None]

    return (placed(new), placed(kept))


def solution(mesh):
    placed = (P("seg", "space", None, None), P("space", None, None), P())
    return jax.shard_map(
        per_device,
        mesh=mesh,
        in_specs=placed,
        out_specs=(P("seg", "space", None, None), P("seg", "space", None, None)),
        check_vma=False,
    )
```
